32 devices in a mesh: group: 1, blk: 32 (over z, y, x, core).
Axes of the slice: x: 2, y: 2, z: 4, core: 2. Of those that a mesh axis runs over, the one named last changes fastest.
Arguments:
- depth_logits: float32 [32, 112, 32, 128], P(('group', 'blk')), may hold values from -18 to 300
- context: bfloat16 [32, 80, 32, 128], P(('group', 'blk')), may hold values from -6 to 6
- lidar_bins: int32 [32, 32, 128], P(('group', 'blk')), may hold values from -1 to 111, as said below
- az_map: int32 [8, 128], replicated, may hold values from 0 to 255, as said below
- rng_map: int32 [8, 112], replicated, may hold values from 0 to 511, as said below
- conv1_weight: bfloat16 [3, 3, 80, 256], replicated, may hold values from -0.21875 to 0.21875
- conv2_weight: bfloat16 [3, 3, 256, 256], replicated, may hold values from -0.125 to 0.125
- out_grad: bfloat16 [256, 512, 256], P(('group', 'blk')), may hold values from -6 to 6
Outputs:
- logit_grad: float32 [32, 112, 32, 128], P(('group', 'blk'))
- context_grad: bfloat16 [32, 80, 32, 128], P(('group', 'blk'))
- conv1_grad: float32 [3, 3, 80, 256], P('group')
- conv2_grad: float32 [3, 3, 256, 256], P('group')
The draws below stay inside these ranges and needn't reach their ends.
Inputs may be any that keep to these rules, and one draw needn't show every extreme that they name: `lidar_bins`: -1 marks a pixel without a LiDAR return. `az_map`: with S = 32, the columns of camera c, in order and never going back, run through the azimuth cells (c * S - S // 4 + t) mod 256 for t = 0 to 3 * S // 2 - 1, each such cell taking two or three columns. `rng_map`: for each camera the range cell rises strictly with the depth bin.
All inputs are finite; a program needn't handle non-finite values.
Results may differ from the reference program's by a relative error of at most 0.024.
Values may be sent and summed in bfloat16 or wider, within the bound.
No kernel may reach another device: no remote copies, remote signals or barrier semaphores. Data moves between devices by JAX's collectives and lax.ppermute only.
A program may use at most 128 MiB of HBM per device.

```python
import jax
import jax.numpy as jnp
from jax import lax

BINS = 112
CH = 80
HID = 256
CAMS = 8
RG = 512
ROWS_DEV = 32
VIEWS = 32
AZ = 256
COLS = 128


def draw_depth_logits(key, part):
    shape = (VIEWS, BINS, ROWS_DEV, COLS)
    keys = jax.random.split(key, 1)
    return jnp.clip(3.0 * jax.random.normal(keys[0], shape, jnp.float32), -18.0, 18.0)


def draw_lidar_bins(key, part):
    keys = jax.random.split(key, 2)
    shape = (VIEWS, ROWS_DEV, COLS)
    has_return = jax.random.randint(keys[0], shape, 0, 3) == 0
    chosen = jax.random.randint(keys[1], shape, 0, BINS)
    return jnp.where(has_return, chosen, -1).astype(jnp.int32)


def draw_az_map(key, part):
    span = AZ // CAMS
    field_cells = 3 * span // 2
    keys = jax.random.split(key, CAMS)

    def one_camera(camera_key, camera):
        order = jax.random.permutation(camera_key, field_cells)
        counts = jnp.where(order < span // 2, 2, 3).astype(jnp.int32)
        ends = jnp.cumsum(counts)
        column_index = jnp.arange(COLS, dtype=jnp.int32)
        local = jnp.sum((ends[None, :] <= column_index[:, None]).astype(jnp.int32), axis=1)
        return (camera * span - span // 4 + local) % AZ
    return jax.vmap(one_camera)(keys, jnp.arange(CAMS, dtype=jnp.int32)).astype(jnp.int32)


def draw_rng_map(key, part):
    keys = jax.random.split(key, CAMS)

    def one_camera(camera_key):
        return jnp.sort(jax.random.permutation(camera_key, RG)[:BINS])
    return jax.vmap(one_camera)(keys).astype(jnp.int32)


def block_levels(rng, extent, cuts, low, top_value):
    def one(dim, parts):
        steps = jax.random.uniform(jax.random.fold_in(jax.random.fold_in(rng, 6), dim), (parts,), jnp.float32, low / len(cuts), top_value / len(cuts))
        return jnp.repeat(jnp.exp(steps), extent[dim] // parts).reshape((-1,) + (1,) * (len(extent) - dim - 1))

    loudness = one(*cuts[0])
    for cut in cuts[1:]:
        loudness = loudness * one(*cut)
    return loudness


def noise(stream_key, extent, scale, limit, cuts=(), kind=jnp.bfloat16):
    level = block_levels(stream_key, extent, cuts, -0.22, 0.18) if cuts else 1.0
    values = jax.random.normal(stream_key, extent, jnp.float32) * scale * level
    return jnp.minimum(jnp.maximum(values, -limit), limit).astype(kind)


def setup_inputs(seed: int = 0, part: int = 0) -> dict:
    arg_keys = jax.random.split(jax.random.key(seed), 9)
    part_keys = jax.random.split(jax.random.fold_in(arg_keys[8], part), 9)
    return {
        "depth_logits": draw_depth_logits(jax.random.fold_in(jax.random.fold_in(arg_keys[8], part), 71), part),
        "context": noise(part_keys[1], (VIEWS, CH, ROWS_DEV, COLS), 1.0, 6.0, ((0, 32),)),
        "lidar_bins": draw_lidar_bins(jax.random.fold_in(jax.random.fold_in(arg_keys[8], part), 71), part),
        "az_map": draw_az_map(jax.random.fold_in(arg_keys[8], 71), part),
        "rng_map": draw_rng_map(jax.random.fold_in(arg_keys[8], 71), part),
        "conv1_weight": noise(arg_keys[5], (3, 3, CH, HID), (9 * CH) ** -0.5, 0.21875),
        "conv2_weight": noise(arg_keys[6], (3, 3, HID, HID), (9 * HID) ** -0.5, 0.125),
        "out_grad": noise(part_keys[7], (AZ, RG, HID), 1.0, 6.0, ((0, 32),)),
    }


DEPTH_WEIGHT = 3.0
precise = lax.Precision.HIGHEST

def shifted(field, tap_row, tap_col):
    rolled = jnp.roll(field, 1 - tap_row, axis=0)
    padded = jnp.pad(rolled, ((0, 0), (1, 1), (0, 0)))
    return padded[:, tap_col:tap_col + field.shape[1]]

def convolve(field, weight):
    running = jnp.zeros(field.shape[:2] + (weight.shape[3],), jnp.float32)
    for tap_row in range(3):
        for tap_col in range(3):
            running = running + jnp.einsum('arc,co->aro', shifted(field, tap_row, tap_col).astype(jnp.float32), weight[tap_row, tap_col].astype(jnp.float32), precision=precise)
    return running

def input_grad(grad_field, weight):
    running = jnp.zeros(grad_field.shape[:2] + (weight.shape[2],), jnp.float32)
    for tap_row in range(3):
        for tap_col in range(3):
            running = running + jnp.einsum('aro,co->arc', shifted(grad_field, 2 - tap_row, 2 - tap_col).astype(jnp.float32), weight[tap_row, tap_col].astype(jnp.float32), precision=precise)
    return running

def weight_grad(field, grad_field):
    outer_rows = []
    for tap_row in range(3):
        outer_cols = []
        for tap_col in range(3):
            outer_cols.append(jnp.einsum('arc,aro->co', shifted(field, tap_row, tap_col).astype(jnp.float32), grad_field.astype(jnp.float32), precision=precise))
        outer_rows.append(jnp.stack(outer_cols))
    return jnp.stack(outer_rows)

def silu_slope(value):
    logistic = jax.nn.sigmoid(value)
    return logistic * (1.0 + value * (1.0 - logistic))

def reference(depth_logits, context, lidar_bins, az_map, rng_map, conv1_weight, conv2_weight, out_grad):
    view_count = depth_logits.shape[0]
    band_count = view_count // CAMS
    az_total = out_grad.shape[0]
    probs = jax.nn.softmax(depth_logits, axis=1)
    probs_low = probs.astype(jnp.bfloat16)
    wedge = jnp.einsum('vbrc,vhrc->vcbh', probs_low.astype(jnp.float32), context.astype(jnp.float32), precision=precise).astype(jnp.bfloat16)

    def place(running, view_index):
        camera = view_index // band_count
        sector_piece = jnp.zeros((az_total, BINS, CH), jnp.float32).at[az_map[camera]].add(wedge[view_index].astype(jnp.float32))
        sector_piece = lax.optimization_barrier(sector_piece.astype(jnp.bfloat16)).astype(jnp.float32)
        running = running.at[:, rng_map[camera], :].add(sector_piece)
        return (running, None)
    bev, _ = lax.scan(place, jnp.zeros((az_total, RG, CH), jnp.float32), jnp.arange(view_count, dtype=jnp.int32))
    bev_low = bev.astype(jnp.bfloat16)
    hidden_pre = convolve(bev_low, conv1_weight)
    activated = jax.nn.silu(hidden_pre).astype(jnp.bfloat16)
    conv2_grad = weight_grad(activated, out_grad)
    act_grad = input_grad(out_grad, conv2_weight)
    pre_grad = (act_grad * silu_slope(hidden_pre)).astype(jnp.bfloat16)
    conv1_grad = weight_grad(bev_low, pre_grad)
    bev_grad = input_grad(pre_grad, conv1_weight).astype(jnp.bfloat16)

    def view_grads(view_index):
        camera = view_index // band_count
        wedge_grad = bev_grad[az_map[camera]][:, rng_map[camera], :].astype(jnp.float32)
        prob_grad = jnp.einsum('cbh,hrc->brc', wedge_grad, context[view_index].astype(jnp.float32), precision=precise)
        ctx_grad = jnp.einsum('cbh,brc->hrc', wedge_grad, probs_low[view_index].astype(jnp.float32), precision=precise).astype(jnp.bfloat16)
        depth_prob = probs[view_index]
        expected = lax.optimization_barrier(jnp.sum(depth_prob * prob_grad, axis=0, keepdims=True))
        lidar_row = lidar_bins[view_index]
        onehot = (jnp.arange(BINS, dtype=jnp.int32)[:, None, None] == lidar_row[None]).astype(jnp.float32)
        has_return = (lidar_row >= 0).astype(jnp.float32)[None]
        grad_logit = depth_prob * (prob_grad - expected) + DEPTH_WEIGHT * (has_return * depth_prob - onehot)
        return (grad_logit, ctx_grad)
    logit_grad, context_grad = lax.map(view_grads, jnp.arange(view_count, dtype=jnp.int32))
    return (logit_grad, context_grad, conv1_grad, conv2_grad)
```

```python
import functools

import jax
import jax.numpy as jnp
from jax import lax
from jax.experimental import pallas as pl
from jax.experimental.pallas import tpu as pltpu
from jax.sharding import PartitionSpec as P

DEPTH_WEIGHT = 3.0
TAPS = 3
LANES = 128
LIMIT = 60 * 1024 * 1024
F32 = jnp.float32
BF16 = jnp.bfloat16


def product(left, right, left_dim, right_dim):
    return lax.dot_general(
        left, right, (((left_dim,), (right_dim,)), ((), ())), preferred_element_type=F32
    )


def padded_rows(value, rows):
    missing = rows - value.shape[0]
    if missing == 0:
        return value
    return jnp.concatenate([value, jnp.zeros((missing, value.shape[1]), value.dtype)], axis=0)


def pool_kernel(
    rows, table, logits, context, probs, probs_t, context_t, kept, sent, wide_p, wide_c, plain_c
):
    columns = logits.shape[1]
    bins = logits.shape[0] // rows
    channels = context.shape[0] // rows
    half = kept.shape[0]
    scores = logits[...].reshape(bins, rows, columns)
    powers = jnp.exp(scores - jnp.max(scores, axis=0, keepdims=True))
    shares = powers / jnp.sum(powers, axis=0, keepdims=True)
    probs[...] = shares.reshape(bins * rows, columns)
    plain_c[...] = context[...].astype(F32)

    def turn(row, _):
        block = padded_rows(probs[pl.ds(row, bins, stride=rows), :], LANES)
        wide_p[pl.ds(row, columns, stride=rows), :] = jnp.transpose(block)
        block = padded_rows(plain_c[pl.ds(row, channels, stride=rows), :], LANES)
        wide_c[pl.ds(row, columns, stride=rows), :] = jnp.transpose(block)
        return 0

    lax.fori_loop(0, rows, turn, 0, unroll=4)
    for wide, narrow in ((wide_p, probs_t), (wide_c, context_t)):
        narrow[0 : columns * rows, :] = wide[...].astype(BF16)
        narrow[columns * rows :, :] = jnp.zeros((rows, LANES), BF16)
    line = lax.broadcasted_iota(jnp.int32, (TAPS * rows, LANES), 0)

    def cell_sum(slot):
        span = pl.ds(pl.multiple_of(table[0, slot] * rows, rows), TAPS * rows)
        features = context_t[span, :]
        features = jnp.where(line < table[1, slot] * rows, features, jnp.zeros_like(features))
        return product(features, probs_t[span, :], 0, 0)[:channels].astype(BF16)

    def one_cell(slot, _):
        sent[slot] = cell_sum(half + slot)
        kept[slot] = cell_sum(slot)
        return 0

    lax.fori_loop(0, half, one_cell, 0, unroll=2)


def act_grad_kernel(first, *refs):
    *sources, weight, out, grid = refs
    base = 0
    for source, low, high in zip(sources, first[0], first[1]):
        grid[base : base + high - low] = source[low:high]
        base += high - low
    hidden = weight.shape[3]
    taps = jnp.concatenate(
        [weight[TAPS - 1 - i].reshape(TAPS * hidden, hidden) for i in range(TAPS)], axis=1
    )
    length = grid.shape[1]
    place = lax.broadcasted_iota(jnp.int32, (hidden, length), 1)

    def one_row(row, start):
        stacked = jnp.concatenate([grid[start + i] for i in range(TAPS)], axis=1)
        sums = product(taps, stacked, 1, 1)
        ahead = pltpu.roll(sums[:hidden], length - 1, 1)
        behind = pltpu.roll(sums[2 * hidden :], 1, 1)
        total = sums[hidden : 2 * hidden]
        total = total + jnp.where(place < length - 1, ahead, 0.0)
        total = total + jnp.where(place > 0, behind, 0.0)
        out[row] = total.astype(BF16)

    starts = first[2]
    if len(starts) > 4:

        def step(row, _):
            one_row(row, row)
            return 0

        lax.fori_loop(0, len(starts), step, 0)
    else:
        for row, start in enumerate(starts):
            one_row(row, start)


def grid_kernel(
    band,
    own,
    edge,
    low_halo,
    high_halo,
    ten,
    two,
    ranges,
    weight_t,
    weight,
    inner_grad,
    outer_grad,
    upstream,
    grads,
    own_reply,
    other_reply,
    cells,
    grid_low,
    grid_taps,
    act_taps,
    slope_rows,
    slope_lanes,
    grid_grad,
):
    sector, channels, lanes = own.shape
    hidden, length = inner_grad.shape[1:]
    bands = band[1]
    mine = band[0]
    wide = sector + 4
    cells[2 : 2 + sector, :, :lanes] = own[...]
    cells[0:2, :, :lanes] = jnp.where(mine == 0, edge[sector - 2 : sector], low_halo[...])
    cells[2 + sector :, :, :lanes] = jnp.where(mine == bands - 1, edge[0:2], high_halo[...])
    cells[:, :, lanes:] = jnp.zeros((wide, channels, lanes), BF16)

    @pl.when(mine == 0)
    def _():
        cells[0 : sector + 2, :, lanes:] = ten[...]

    @pl.when(mine == bands - 1)
    def _():
        cells[2:, :, lanes:] = ten[...]

    @pl.when(mine == 1)
    def _():
        cells[0:2, :, lanes:] = two[...]

    @pl.when(mine == bands - 2)
    def _():
        cells[2 + sector :, :, lanes:] = two[...]

    spots = lax.broadcasted_iota(jnp.int32, (2 * lanes, length), 1)
    range_hot = (spots == ranges[...]).astype(F32).astype(BF16)

    def behind(value):
        place = lax.broadcasted_iota(jnp.int32, value.shape, 1)
        return jnp.where(place > 0, pltpu.roll(value, 1, 1), 0.0)

    def ahead(value):
        place = lax.broadcasted_iota(jnp.int32, value.shape, 1)
        return jnp.where(place < length - 1, pltpu.roll(value, length - 1, 1), 0.0)

    for chunk in range(0, wide, 4):
        block = cells[chunk : chunk + 4].reshape(4 * channels, 2 * lanes)
        summed = product(block, range_hot, 1, 0)
        for row in range(chunk, chunk + 4):
            value = summed[(row - chunk) * channels : (row - chunk + 1) * channels]
            grid_low[row * channels : (row + 1) * channels, :] = value.astype(BF16)
            if 0 < row < wide - 1:
                spread = pl.ds((row - 1) * length, length)
                grid_taps[0:channels, spread] = behind(value).astype(BF16)
                grid_taps[channels : 2 * channels, spread] = value.astype(BF16)
                grid_taps[2 * channels :, spread] = ahead(value).astype(BF16)

    def one_row(row, act_grad):
        source = pl.ds(pl.multiple_of(row * channels, channels), TAPS * channels)
        sums = product(weight_t[...], grid_low[source, :], 1, 0)
        value = behind(sums[:hidden]) + sums[hidden : 2 * hidden] + ahead(sums[2 * hidden :])
        logistic = 1.0 / (1.0 + jnp.exp(-value))
        active = value * logistic
        spread = pl.ds(pl.multiple_of(row * length, length), length)
        act_taps[0:hidden, spread] = behind(active).astype(BF16)
        act_taps[hidden : 2 * hidden, spread] = active.astype(BF16)
        act_taps[2 * hidden :, spread] = ahead(active).astype(BF16)
        slope = logistic * (1.0 + value * (1.0 - logistic))
        result = (act_grad.astype(F32) * slope).astype(BF16)
        slope_rows[pl.ds(pl.multiple_of(row * hidden, hidden), hidden), :] = result
        slope_lanes[:, spread] = result

    for row, index in ((0, 0), (1, 1), (sector, 2), (sector + 1, 3)):
        one_row(row, outer_grad[index])

    def inner(index, _):
        one_row(index + 2, inner_grad[index])
        return 0

    lax.fori_loop(0, sector - 2, inner, 0)
    count = sector * length
    tall = TAPS * hidden
    short = TAPS * channels

    def second(tap, _):
        window = pl.ds(pl.multiple_of(tap * length, length), count)
        result = product(act_taps[:, window], upstream[...], 1, 0)
        grads[pl.ds(pl.multiple_of(tap * tall, tall), tall), :] = result.astype(BF16)
        return 0

    lax.fori_loop(0, TAPS, second, 0)
    for tap in range(TAPS):
        result = product(
            grid_taps[:, tap * length : tap * length + count],
            slope_lanes[:, length : length + count],
            1,
            1,
        )
        base = TAPS * tall + tap * short
        grads[base : base + short, :] = result.astype(BF16)
    base = TAPS * (tall + short)
    grads[base:, :] = jnp.zeros((grads.shape[0] - base, hidden), BF16)
    flipped = jnp.concatenate([weight[TAPS - 1 - i] for i in range(TAPS)], axis=1)

    def back(row, _):
        source = pl.ds(pl.multiple_of(row * hidden, hidden), TAPS * hidden)
        sums = product(flipped, slope_rows[source, :], 1, 0)
        value = ahead(sums[:channels]) + sums[channels : 2 * channels]
        value = value + behind(sums[2 * channels :])
        grid_grad[pl.ds(pl.multiple_of(row * channels, channels), channels), :] = value.astype(BF16)
        return 0

    lax.fori_loop(0, sector, back, 0)
    picked = product(grid_grad[...], range_hot, 1, 1).astype(BF16)
    own_reply[...] = picked[:, :lanes].reshape(sector, channels, lanes)
    other_reply[...] = picked[:, lanes:].reshape(sector, channels, lanes)


def pixel_kernel(
    rows,
    table,
    own,
    partner,
    edge,
    theirs,
    probs,
    probs_t,
    context_t,
    lidar,
    logit_grad,
    context_grad,
    wedges,
    wide_p,
    wide_c,
    plain_c,
):
    columns = probs.shape[1]
    bins = probs.shape[0] // rows
    channels = context_grad.shape[0] // rows
    sector = own.shape[0]
    wedges[0:sector] = own[...]
    wedges[sector : 2 * sector] = partner[...]
    wedges[2 * sector : 3 * sector] = edge[...]
    wedges[3 * sector :] = theirs[...]
    wide_c[...] = jnp.zeros_like(wide_c)

    def one_cell(cell, _):
        span = pl.ds(pl.multiple_of(table[0, cell] * rows, rows), TAPS * rows)
        slope = wedges[table[1, cell]]
        wide_p[span, :] = product(context_t[span, :][:, :channels], slope, 1, 0)
        wide_c[span, 0:channels] = product(probs_t[span, :], slope, 1, 1)
        return 0

    lax.fori_loop(0, wedges.shape[0], one_cell, 0, unroll=4)

    def turn(row, _):
        block = jnp.transpose(wide_p[pl.ds(row, columns, stride=rows), :])
        logit_grad[pl.ds(row, bins, stride=rows), :] = block[:bins]
        block = jnp.transpose(wide_c[pl.ds(row, columns, stride=rows), :])
        plain_c[pl.ds(row, channels, stride=rows), :] = block[:channels]
        return 0

    lax.fori_loop(0, rows, turn, 0, unroll=4)
    context_grad[...] = plain_c[...].astype(BF16)
    share = probs[...].reshape(bins, rows, columns)
    slope = logit_grad[...].reshape(bins, rows, columns)
    expected = jnp.sum(share * slope, axis=0, keepdims=True)
    target = lidar[...][None]
    seen = jnp.where(target >= 0, DEPTH_WEIGHT, 0.0)
    level = lax.broadcasted_iota(jnp.int32, share.shape, 0)
    hit = jnp.where(level == target, DEPTH_WEIGHT, 0.0)
    result = share * (slope - expected) + (seen * share - hit)
    logit_grad[...] = result.reshape(bins * rows, columns)


def vmem():
    return pl.BlockSpec(memory_space=pltpu.VMEM)


def smem():
    return pl.BlockSpec(memory_space=pltpu.SMEM)


def call(kernel, out_shape, scratch, spaces, flops, moved, name):
    many = isinstance(out_shape, (list, tuple))
    return pl.pallas_call(
        kernel,
        out_shape=out_shape,
        in_specs=spaces,
        out_specs=[vmem() for _ in out_shape] if many else vmem(),
        scratch_shapes=scratch,
        compiler_params=pltpu.CompilerParams(vmem_limit_bytes=LIMIT),
        cost_estimate=pl.CostEstimate(flops=flops, bytes_accessed=moved, transcendentals=0),
        name=name,
    )


def halves(part, upper):
    size = part.shape[0] // 2
    keep = lax.dynamic_slice_in_dim(part, upper * size, size, 0)
    send = lax.dynamic_slice_in_dim(part, (1 - upper) * size, size, 0)
    return keep, send


def rounded_sum(left, right):
    return (left.astype(F32) + right.astype(F32)).astype(BF16)


def swapped(value, blocks, mask):
    return lax.ppermute(value, "blk", [(i, i ^ mask) for i in range(blocks)])


def joined(value, other, upper):
    return jnp.where(
        upper == 1,
        jnp.concatenate([other, value], axis=0),
        jnp.concatenate([value, other], axis=0),
    )


def total_over_blocks(value, position, blocks):
    count = blocks.bit_length() - 1
    bit = [(position >> k) & 1 for k in range(count)]
    keep, send = halves(value, bit[0])
    value = rounded_sum(keep, swapped(send, blocks, 1))
    later = list(range(1, count))
    parts = jnp.split(value, TAPS, axis=0)
    orders = [later[k % len(later) :] + later[: k % len(later)] for k in range(TAPS)]
    for step in range(len(later)):
        for k in range(TAPS):
            axis = orders[k][step]
            keep, send = halves(parts[k], bit[axis])
            parts[k] = rounded_sum(keep, swapped(send, blocks, 1 << axis))
    for step in reversed(range(len(later))):
        for k in range(TAPS):
            axis = orders[k][step]
            parts[k] = joined(parts[k], swapped(parts[k], blocks, 1 << axis), bit[axis])
    value = jnp.concatenate(parts, axis=0)
    return joined(value, swapped(value, blocks, 1), bit[0])


def shards(
    depth_logits, context, lidar_bins, az_map, rng_map, conv1_weight, conv2_weight, out_grad
):
    blocks = lax.axis_size("blk")
    position = lax.axis_index("blk")
    cameras, columns = az_map.shape
    bands = blocks // cameras
    sector, length, hidden = out_grad.shape
    bins, rows = depth_logits.shape[1:3]
    channels = context.shape[1]
    if bands != 4 or blocks & (blocks - 1) or bins > LANES or channels > LANES or sector < 6:
        raise ValueError("unsupported sizes")
    camera = position // bands
    band = position % bands
    sight = bands * sector
    seen = sight + sight // 2

    forward = [(i, (i + 1) % blocks) for i in range(blocks)]
    backward = [((i + 1) % blocks, i) for i in range(blocks)]
    low_grad = lax.ppermute(out_grad[sector - 2 :], "blk", forward)
    high_grad = lax.ppermute(out_grad[:2], "blk", backward)

    az_row = lax.dynamic_slice_in_dim(az_map, camera, 1, 0)[0]
    local = (az_row - (camera * sight - sight // 4)) % (blocks * sector)
    marks = jnp.arange(seen + 1, dtype=jnp.int32)
    begins = jnp.sum((local[None, :] < marks[:, None]).astype(jnp.int32), axis=1)
    near = band ^ 1
    order = jnp.stack(
        [1 + band, 1 + (band ^ 2), 5 * (band % 2), 1 + near, 1 + (near ^ 2), 5 * (near % 2)]
    )
    sixth = jnp.arange(6, dtype=jnp.int32)
    inverse = jnp.sum(jnp.where(order[None, :] == sixth[:, None], sixth[None, :], 0), axis=1)
    steps = jnp.arange(sector, dtype=jnp.int32)
    cells = (order[:, None] * sector + steps[None, :]).reshape(-1)
    slots = (inverse[:, None] * sector + steps[None, :]).reshape(-1)
    hot = (cells[:, None] == marks[None, :seen]).astype(jnp.int32)
    widths = begins[1:] - begins[:-1]
    pool_table = jnp.stack(
        [jnp.sum(hot * begins[None, :seen], axis=1), jnp.sum(hot * widths[None, :], axis=1)]
    )
    pixel_table = jnp.stack([begins[:seen], slots])

    turned = (columns + 1) * rows
    half = 3 * sector
    probs, probs_t, context_t, kept, sent = call(
        functools.partial(pool_kernel, rows),
        [
            jax.ShapeDtypeStruct((bins * rows, columns), F32),
            jax.ShapeDtypeStruct((turned, LANES), BF16),
            jax.ShapeDtypeStruct((turned, LANES), BF16),
            jax.ShapeDtypeStruct((half, channels, LANES), BF16),
            jax.ShapeDtypeStruct((half, channels, LANES), BF16),
        ],
        [
            pltpu.VMEM((columns * rows, LANES), F32),
            pltpu.VMEM((columns * rows, LANES), F32),
            pltpu.VMEM((channels * rows, columns), F32),
        ],
        [smem(), vmem(), vmem()],
        2 * seen * 3 * rows * LANES * LANES,
        20 * bins * rows * columns,
        "pool",
    )(
        pool_table,
        depth_logits[0].reshape(bins * rows, columns),
        context[0].reshape(channels * rows, columns),
    )

    row_flops = 2 * TAPS * TAPS * hidden * hidden * length

    def act_grad(sources, lows, highs, starts):
        total = sum(h - l for l, h in zip(lows, highs))
        return call(
            functools.partial(act_grad_kernel, (lows, highs, starts)),
            jax.ShapeDtypeStruct((len(starts), hidden, length), BF16),
            [pltpu.VMEM((total, length, hidden), BF16)],
            [vmem() for _ in sources] + [vmem()],
            row_flops * len(starts),
            2 * (total + len(starts)) * length * hidden,
            "act_grad",
        )(*sources, conv2_weight)

    inner_grad = act_grad([out_grad], (0,), (sector,), tuple(range(sector - 2)))
    outer_grad = act_grad(
        [low_grad, out_grad, out_grad, high_grad],
        (0, 0, sector - 2, 0),
        (2, 2, sector, 2),
        (0, 1, 4, 5),
    )

    summed = rounded_sum(kept, swapped(sent, blocks, 1))
    own = rounded_sum(summed[:sector], swapped(summed[sector : 2 * sector], blocks, 2))
    inward = [(i, i ^ 2) for i in range(blocks) if i % bands in (1, 2)]
    outward = [(i ^ 2, i) for i in range(blocks) if i % bands in (1, 2)]
    edge = rounded_sum(
        summed[2 * sector :], lax.ppermute(summed[2 * sector :], "blk", inward)
    )
    first = band == 0
    firsts = [i for i in range(blocks) if i % bands == 0]
    lasts = [i for i in range(blocks) if i % bands == bands - 1]
    ten = jnp.where(
        first,
        jnp.concatenate([edge, own[:2]], axis=0),
        jnp.concatenate([own[sector - 2 :], edge], axis=0),
    )
    two = jnp.where(first, edge[:2], edge[sector - 2 :])

    def to_next(value, more):
        pairs = [(i, (i - 1 - more) % blocks) for i in firsts]
        pairs = pairs + [(i, (i + 1 + more) % blocks) for i in lasts]
        return lax.ppermute(value, "blk", pairs)

    ten = to_next(ten, 0)
    two = to_next(two, 1)
    low_halo = lax.ppermute(
        own[sector - 2 :], "blk", [(i, i + 1) for i in range(blocks) if i not in lasts]
    )
    high_halo = lax.ppermute(
        own[:2], "blk", [(i, i - 1) for i in range(blocks) if i not in firsts]
    )
    other = jnp.where(band < bands // 2, camera - 1, camera + 1) % cameras
    ranges = jnp.concatenate(
        [lax.dynamic_slice_in_dim(rng_map, k, 1, 0) for k in (camera, other)], axis=0
    )
    ranges = jnp.pad(ranges, ((0, 0), (0, LANES - bins)), constant_values=-1).reshape(-1, 1)
    weight_t = conv1_weight.transpose(1, 3, 0, 2).reshape(TAPS * hidden, TAPS * channels)
    weight = conv1_weight.reshape(TAPS, TAPS * channels, hidden)
    grad_rows = TAPS * TAPS * (hidden + channels)
    unit = TAPS * blocks * 16
    grad_rows = -(-grad_rows // unit) * unit
    wide = sector + 2
    grads, own_reply, other_reply = call(
        grid_kernel,
        [
            jax.ShapeDtypeStruct((grad_rows, hidden), BF16),
            jax.ShapeDtypeStruct((sector, channels, LANES), BF16),
            jax.ShapeDtypeStruct((sector, channels, LANES), BF16),
        ],
        [
            pltpu.VMEM((sector + 4, channels, 2 * LANES), BF16),
            pltpu.VMEM(((sector + 4) * channels, length), BF16),
            pltpu.VMEM((TAPS * channels, wide * length), BF16),
            pltpu.VMEM((TAPS * hidden, wide * length), BF16),
            pltpu.VMEM((wide * hidden, length), BF16),
            pltpu.VMEM((hidden, wide * length), BF16),
            pltpu.VMEM((sector * channels, length), BF16),
        ],
        [smem()] + [vmem()] * 12,
        row_flops * (sector + 3 * sector // 2),
        20 * sector * length * hidden,
        "grid",
    )(
        jnp.stack([band, jnp.full_like(band, bands)]),
        own,
        edge,
        low_halo,
        high_halo,
        ten,
        two,
        ranges,
        weight_t,
        weight,
        inner_grad,
        outer_grad,
        out_grad.reshape(sector * length, hidden),
    )

    partner = swapped(own_reply, blocks, 2)
    edge_reply = to_next(other_reply, 0)
    passed = lax.ppermute(edge_reply, "blk", outward)
    outer = jnp.logical_or(first, band == bands - 1)
    edge_reply = jnp.where(outer, edge_reply, passed)
    theirs = swapped(
        jnp.concatenate([own_reply, partner, edge_reply], axis=0), blocks, 1
    )
    total = total_over_blocks(grads, position, blocks)

    logit_grad, context_grad = call(
        functools.partial(pixel_kernel, rows),
        [
            jax.ShapeDtypeStruct((bins * rows, columns), F32),
            jax.ShapeDtypeStruct((channels * rows, columns), BF16),
        ],
        [
            pltpu.VMEM((seen, channels, LANES), BF16),
            pltpu.VMEM((turned, LANES), F32),
            pltpu.VMEM((turned, LANES), F32),
            pltpu.VMEM((channels * rows, columns), F32),
        ],
        [smem()] + [vmem()] * 8,
        4 * seen * 3 * rows * LANES * LANES,
        20 * bins * rows * columns,
        "pixel",
    )(pixel_table, own_reply, partner, edge_reply, theirs, probs, probs_t, context_t, lidar_bins[0])

    second = TAPS * TAPS * hidden
    both = second + TAPS * TAPS * channels
    return (
        logit_grad.reshape(1, bins, rows, columns),
        context_grad.reshape(1, channels, rows, columns),
        total[second:both].astype(F32).reshape(TAPS, TAPS, channels, hidden),
        total[:second].astype(F32).reshape(TAPS, TAPS, hidden, hidden),
    )


def solution(mesh):
    return jax.shard_map(
        shards,
        mesh=mesh,
        in_specs=(
            P(("group", "blk"), None, None, None),
            P(("group", "blk"), None, None, None),
            P(("group", "blk"), None, None),
            P(),
            P(),
            P(),
            P(),
            P(("group", "blk"), None, None),
        ),
        out_specs=(
            P(("group", "blk"), None, None, None),
            P(("group", "blk"), None, None, None),
            P("group", None, None, None),
            P("group", None, None, None),
        ),
        check_vma=False,
    )
```

```python
import functools

import jax
import jax.numpy as jnp
from jax import lax
from jax.experimental import pallas as pl
from jax.experimental.pallas import tpu as pltpu
from jax.sharding import PartitionSpec as P

DEPTH_WEIGHT = 3.0
TAPS = 3
LANES = 128
LIMIT = 60 * 1024 * 1024
F32 = jnp.float32
BF16 = jnp.bfloat16


def product(left, right, left_dim, right_dim):
    return lax.dot_general(
        left, right, (((left_dim,), (right_dim,)), ((), ())), preferred_element_type=F32
    )


def padded_rows(value, rows):
    missing = rows - value.shape[0]
    if missing == 0:
        return value
    return jnp.concatenate([value, jnp.zeros((missing, value.shape[1]), value.dtype)], axis=0)


def pool_kernel(
    rows,
    table,
    logits,
    context,
    probs_out,
    probs_t_out,
    context_t_out,
    kept,
    sent,
    probs,
    probs_t,
    context_t,
    wide_p,
    wide_c,
    plain_c,
    done,
):
    columns = logits.shape[1]
    bins = logits.shape[0] // rows
    channels = context.shape[0] // rows
    half = kept.shape[0]
    scores = logits[...].reshape(bins, rows, columns)
    powers = jnp.exp(scores - jnp.max(scores, axis=0, keepdims=True))
    shares = powers / jnp.sum(powers, axis=0, keepdims=True)
    probs[...] = shares.reshape(bins * rows, columns)
    copies = [pltpu.make_async_copy(probs, probs_out, done.at[0])]
    copies[0].start()
    plain_c[...] = context[...].astype(F32)

    def turn(row, _):
        block = padded_rows(probs[pl.ds(row, bins, stride=rows), :], LANES)
        wide_p[pl.ds(row, columns, stride=rows), :] = jnp.transpose(block)
        block = padded_rows(plain_c[pl.ds(row, channels, stride=rows), :], LANES)
        wide_c[pl.ds(row, columns, stride=rows), :] = jnp.transpose(block)
        return 0

    lax.fori_loop(0, rows, turn, 0, unroll=4)
    for wide, narrow, out in (
        (wide_p, probs_t, probs_t_out),
        (wide_c, context_t, context_t_out),
    ):
        narrow[0 : columns * rows, :] = wide[...].astype(BF16)
        narrow[columns * rows :, :] = jnp.zeros((rows, LANES), BF16)
        copies.append(pltpu.make_async_copy(narrow, out, done.at[len(copies)]))
        copies[-1].start()
    line = lax.broadcasted_iota(jnp.int32, (TAPS * rows, LANES), 0)

    def cell_sum(slot):
        span = pl.ds(pl.multiple_of(table[0, slot] * rows, rows), TAPS * rows)
        features = context_t[span, :]
        features = jnp.where(line < table[1, slot] * rows, features, jnp.zeros_like(features))
        return product(features, probs_t[span, :], 0, 0)[:channels].astype(BF16)

    def one_cell(slot, _):
        sent[slot] = cell_sum(half + slot)
        kept[slot] = cell_sum(slot)
        return 0

    lax.fori_loop(0, half, one_cell, 0, unroll=4)
    for copy in copies:
        copy.wait()


def act_grad_kernel(first, *refs):
    *sources, weight, out, grid = refs
    base = 0
    for source, low, high in zip(sources, first[0], first[1]):
        grid[base : base + high - low] = source[low:high]
        base += high - low
    hidden = weight.shape[3]
    taps = jnp.concatenate(
        [weight[TAPS - 1 - i].reshape(TAPS * hidden, hidden) for i in range(TAPS)], axis=1
    )
    length = grid.shape[1]
    place = lax.broadcasted_iota(jnp.int32, (hidden, length), 1)

    def one_row(row, start):
        stacked = jnp.concatenate([grid[start + i] for i in range(TAPS)], axis=1)
        sums = product(taps, stacked, 1, 1)
        ahead = pltpu.roll(sums[:hidden], length - 1, 1)
        behind = pltpu.roll(sums[2 * hidden :], 1, 1)
        total = sums[hidden : 2 * hidden]
        total = total + jnp.where(place < length - 1, ahead, 0.0)
        total = total + jnp.where(place > 0, behind, 0.0)
        out[row] = total.astype(BF16)

    starts = first[2]
    if len(starts) > 4 or tuple(starts) == tuple(range(len(starts))):

        def step(row, _):
            one_row(row, row)
            return 0

        lax.fori_loop(0, len(starts), step, 0)
    else:
        for row, start in enumerate(starts):
            one_row(row, start)


def grid_kernel(
    place,
    own,
    edge,
    near_halo,
    far_halo,
    two,
    ranges,
    weight_t,
    weight,
    inner_grad,
    outer_grad,
    upstream_in,
    keep,
    send,
    own_reply,
    other_reply,
    cells,
    grid_low,
    grid_taps,
    act_taps,
    slope_rows,
    slope_lanes,
    grid_grad,
    act_grads,
    upstream,
    grads,
    done,
):
    sector, channels, lanes = own.shape
    hidden, length = outer_grad.shape[1:]
    mine, bands, core = place[0], place[1], place[2]
    wide = sector + 4
    rows = sector + 2
    copies = [
        pltpu.make_async_copy(source, target, done.at[k])
        for k, (source, target) in enumerate(
            (
                (inner_grad, act_grads.at[2:sector]),
                (outer_grad.at[0:2], act_grads.at[0:2]),
                (outer_grad.at[2:4], act_grads.at[sector:]),
                (upstream_in, upstream),
            )
        )
    ]
    for copy in copies:
        copy.start()
    cells[2 : 2 + sector, :, :lanes] = own[...]
    cells[:, :, lanes:] = jnp.zeros((wide, channels, lanes), BF16)

    @pl.when(mine == 0)
    def _():
        cells[0:2, :, :lanes] = edge[sector - 2 : sector]
        cells[2 + sector :, :, :lanes] = near_halo[...]
        cells[0 : sector + 2, :, lanes:] = far_halo[...]

    @pl.when(mine == 1)
    def _():
        cells[0:2, :, :lanes] = near_halo[...]
        cells[2 + sector :, :, :lanes] = far_halo[0:2]
        cells[0:2, :, lanes:] = two[...]

    @pl.when(mine == bands - 2)
    def _():
        cells[0:2, :, :lanes] = far_halo[0:2]
        cells[2 + sector :, :, :lanes] = near_halo[...]
        cells[2 + sector :, :, lanes:] = two[...]

    @pl.when(mine == bands - 1)
    def _():
        cells[0:2, :, :lanes] = near_halo[...]
        cells[2 + sector :, :, :lanes] = edge[0:2]
        cells[2:, :, lanes:] = far_halo[...]

    spots = lax.broadcasted_iota(jnp.int32, (2 * lanes, length), 1)
    range_hot = (spots == ranges[...]).astype(F32).astype(BF16)

    def behind(value):
        turned = pltpu.roll(value, 1, 1)
        lane = lax.broadcasted_iota(jnp.int32, (value.shape[0], LANES), 1)
        first = jnp.where(lane > 0, turned[:, :LANES], 0.0)
        return jnp.concatenate([first, turned[:, LANES:]], axis=1)

    def ahead(value):
        turned = pltpu.roll(value, length - 1, 1)
        lane = lax.broadcasted_iota(jnp.int32, (value.shape[0], LANES), 1)
        last = jnp.where(lane < LANES - 1, turned[:, length - LANES :], 0.0)
        return jnp.concatenate([turned[:, : length - LANES], last], axis=1)

    for chunk in range(0, wide, 4):
        block = cells[chunk : chunk + 4].reshape(4 * channels, 2 * lanes)
        summed = product(block, range_hot, 1, 0)
        for row in range(chunk, chunk + 4):
            value = summed[(row - chunk) * channels : (row - chunk + 1) * channels]
            grid_low[row * channels : (row + 1) * channels, :] = value.astype(BF16)
            if 0 < row < wide - 1:
                spread = pl.ds((row - 1) * length, length)
                grid_taps[0:channels, spread] = behind(value).astype(BF16)
                grid_taps[channels : 2 * channels, spread] = value.astype(BF16)
                grid_taps[2 * channels :, spread] = ahead(value).astype(BF16)
    for copy in copies[:3]:
        copy.wait()

    def one_row(row, _):
        source = pl.ds(pl.multiple_of(row * channels, channels), TAPS * channels)
        sums = product(weight_t[...], grid_low[source, :], 1, 0)
        value = behind(sums[:hidden]) + sums[hidden : 2 * hidden] + ahead(sums[2 * hidden :])
        logistic = 0.5 + 0.5 * jnp.tanh(0.5 * value)
        active = value * logistic
        spread = pl.ds(pl.multiple_of(row * length, length), length)
        act_taps[0:hidden, spread] = behind(active).astype(BF16)
        act_taps[hidden : 2 * hidden, spread] = active.astype(BF16)
        act_taps[2 * hidden :, spread] = ahead(active).astype(BF16)
        slope = logistic * (1.0 + value * (1.0 - logistic))
        result = (act_grads[row].astype(F32) * slope).astype(BF16)
        slope_rows[pl.ds(pl.multiple_of(row * hidden, hidden), hidden), :] = result
        slope_lanes[:, spread] = result
        return 0

    lax.fori_loop(0, rows, one_row, 0, unroll=2)
    copies[3].wait()
    count = sector * length
    tall = TAPS * hidden
    short = TAPS * channels

    def second(tap, _):
        window = pl.ds(pl.multiple_of(tap * length, length), count)
        result = product(act_taps[:, window], upstream[...], 1, 0)
        grads[pl.ds(pl.multiple_of(tap * tall, tall), tall), :] = result.astype(BF16)
        return 0

    lax.fori_loop(0, TAPS, second, 0)
    for tap in range(TAPS):
        result = product(
            grid_taps[:, tap * length : tap * length + count],
            slope_lanes[:, length : length + count],
            1,
            1,
        )
        base = TAPS * tall + tap * short
        grads[base : base + short, :] = result.astype(BF16)
    base = TAPS * (tall + short)
    grads[base:, :] = jnp.zeros((grads.shape[0] - base, hidden), BF16)
    half = keep.shape[0]
    keep[...] = grads[pl.ds(pl.multiple_of(core * half, half), half), :]
    send[...] = grads[pl.ds(pl.multiple_of((1 - core) * half, half), half), :]
    flipped = jnp.concatenate([weight[TAPS - 1 - i] for i in range(TAPS)], axis=1)

    def back(row, _):
        source = pl.ds(pl.multiple_of(row * hidden, hidden), TAPS * hidden)
        sums = product(flipped, slope_rows[source, :], 1, 0)
        value = ahead(sums[:channels]) + sums[channels : 2 * channels]
        value = value + behind(sums[2 * channels :])
        grid_grad[pl.ds(pl.multiple_of(row * channels, channels), channels), :] = value.astype(BF16)
        return 0

    lax.fori_loop(0, sector, back, 0, unroll=2)
    picked = product(grid_grad[...], range_hot, 1, 1).astype(BF16)
    own_reply[...] = picked[:, :lanes].reshape(sector, channels, lanes)
    other_reply[...] = picked[:, lanes:].reshape(sector, channels, lanes)


def finish_kernel(place, value, other, second, first):
    half = value.shape[0]
    cut = second.shape[0] - half

    def write(low, high):
        second[0:half, :] = low[...].astype(F32)
        second[half:, :] = high[0:cut, :].astype(F32)
        first[...] = high[cut : cut + first.shape[0], :].astype(F32)

    @pl.when(place[2] == 0)
    def _():
        write(value, other)

    @pl.when(place[2] == 1)
    def _():
        write(other, value)


def logit_kernel(
    rows, table, own, partner, edge, theirs, probs, context_t, lidar, logit_grad, wedges, wide
):
    columns = probs.shape[1]
    bins = probs.shape[0] // rows
    sector, channels, _ = own.shape
    wedges[0:sector] = own[...]
    wedges[sector : 2 * sector] = partner[...]
    wedges[2 * sector : 3 * sector] = edge[...]
    wedges[3 * sector :] = theirs[...]

    def one_cell(cell, _):
        span = pl.ds(pl.multiple_of(table[0, cell] * rows, rows), TAPS * rows)
        slope = wedges[table[1, cell]]
        wide[span, :] = product(context_t[span, :][:, :channels], slope, 1, 0)
        return 0

    lax.fori_loop(0, wedges.shape[0], one_cell, 0, unroll=8)

    def turn(row, _):
        block = jnp.transpose(wide[pl.ds(row, columns, stride=rows), :])
        logit_grad[pl.ds(row, bins, stride=rows), :] = block[:bins]
        return 0

    lax.fori_loop(0, rows, turn, 0, unroll=4)
    share = probs[...].reshape(bins, rows, columns)
    slope = logit_grad[...].reshape(bins, rows, columns)
    expected = jnp.sum(share * slope, axis=0, keepdims=True)
    target = lidar[...][None]
    seen = jnp.where(target >= 0, DEPTH_WEIGHT, 0.0)
    level = lax.broadcasted_iota(jnp.int32, share.shape, 0)
    hit = jnp.where(level == target, DEPTH_WEIGHT, 0.0)
    result = share * (slope - expected) + (seen * share - hit)
    logit_grad[...] = result.reshape(bins * rows, columns)


def context_kernel(
    rows, table, own, partner, edge, theirs, probs_t, context_grad, wedges, wide, plain
):
    columns = context_grad.shape[1]
    sector, channels, _ = own.shape
    wedges[0:sector] = own[...]
    wedges[sector : 2 * sector] = partner[...]
    wedges[2 * sector : 3 * sector] = edge[...]
    wedges[3 * sector :] = theirs[...]
    wide[...] = jnp.zeros_like(wide)

    def one_cell(cell, _):
        span = pl.ds(pl.multiple_of(table[0, cell] * rows, rows), TAPS * rows)
        wide[span, 0:channels] = product(probs_t[span, :], wedges[table[1, cell]], 1, 1)
        return 0

    lax.fori_loop(0, wedges.shape[0], one_cell, 0, unroll=8)

    def turn(row, _):
        block = jnp.transpose(wide[pl.ds(row, columns, stride=rows), :])
        plain[pl.ds(row, channels, stride=rows), :] = block[:channels]
        return 0

    lax.fori_loop(0, rows, turn, 0, unroll=4)
    context_grad[...] = plain[...].astype(BF16)


def vmem():
    return pl.BlockSpec(memory_space=pltpu.VMEM)


def smem():
    return pl.BlockSpec(memory_space=pltpu.SMEM)


def anywhere():
    return pl.BlockSpec(memory_space=pl.ANY)


def call(kernel, out_shape, scratch, spaces, flops, moved, outs=None):
    many = isinstance(out_shape, (list, tuple))
    return pl.pallas_call(
        kernel,
        out_shape=out_shape,
        in_specs=spaces,
        out_specs=outs or ([vmem() for _ in out_shape] if many else vmem()),
        scratch_shapes=scratch,
        compiler_params=pltpu.CompilerParams(vmem_limit_bytes=LIMIT),
        cost_estimate=pl.CostEstimate(flops=flops, bytes_accessed=moved, transcendentals=0),
    )


def rounded_sum(left, right):
    return (left.astype(F32) + right.astype(F32)).astype(BF16)


def swapped(value, blocks, mask):
    return lax.ppermute(value, "blk", [(i, i ^ mask) for i in range(blocks)])


def piece(value, index, count):
    size = value.shape[0] // count
    return lax.dynamic_slice_in_dim(value, index * size, size, 0)


def total_over_blocks(keep, send, position, blocks):
    count = blocks.bit_length() - 1
    pairs = list(range(1, count, 2))
    orders = (pairs, pairs[1:] + pairs[:1])
    core = position & 1
    digits = [
        jnp.where(core == 0, position >> one, position >> two) & 3 for one, two in zip(*orders)
    ]

    def sent(part, step, mask):
        to = [(i, i ^ (mask << orders[i & 1][step])) for i in range(blocks)]
        return lax.ppermute(part, "blk", to)

    value = rounded_sum(keep, swapped(send, blocks, 1))
    for step, digit in enumerate(digits):
        arrived = [sent(piece(value, digit ^ mask, 4), step, mask) for mask in (3, 1, 2)]
        total = piece(value, digit, 4).astype(F32)
        for part in arrived:
            total = total + part.astype(F32)
        value = total.astype(BF16)
    for step, digit in reversed(list(enumerate(digits))):
        held = [value] + [sent(value, step, mask) for mask in (1, 2, 3)]
        high, low = digit >> 1 == 1, digit & 1 == 1

        def at(k):
            one = jnp.where(low, held[k ^ 1], held[k])
            two = jnp.where(low, held[k ^ 3], held[k ^ 2])
            return jnp.where(high, two, one)

        value = jnp.concatenate([at(k) for k in range(4)], axis=0)
    return value, swapped(value, blocks, 1)


def shards(
    depth_logits, context, lidar_bins, az_map, rng_map, conv1_weight, conv2_weight, out_grad
):
    blocks = lax.axis_size("blk")
    position = lax.axis_index("blk")
    cameras, columns = az_map.shape
    bands = blocks // cameras
    sector, length, hidden = out_grad.shape
    bins, rows = depth_logits.shape[1:3]
    channels = context.shape[1]
    if bands != 4 or blocks != 1 << (blocks.bit_length() - 1) or blocks.bit_length() % 2 or bins > LANES or channels > LANES or sector < 6:
        raise ValueError("unsupported sizes")
    camera = position // bands
    band = position % bands
    sight = bands * sector
    seen = sight + sight // 2

    core = position & 1
    place = jnp.stack([band, jnp.full_like(band, bands), core])
    on_chip = [(i, i ^ 1) for i in range(blocks)]
    off_chip = [(i, (i + 1 if i & 1 else i - 1) % blocks) for i in range(blocks)]

    def ends(value, near):
        count = value.shape[0]
        start = jnp.where((core == 0) == near, count - 2, 0)
        return lax.dynamic_slice_in_dim(value, start, 2, 0)

    near_grad = lax.ppermute(ends(out_grad, True), "blk", on_chip)
    far_grad = lax.ppermute(ends(out_grad, False), "blk", off_chip)
    low_grad = jnp.where(core == 0, far_grad, near_grad)
    high_grad = jnp.where(core == 0, near_grad, far_grad)

    az_row = lax.dynamic_slice_in_dim(az_map, camera, 1, 0)[0]
    local = (az_row - (camera * sight - sight // 4)) % (blocks * sector)
    marks = jnp.arange(seen + 1, dtype=jnp.int32)
    begins = jnp.sum((local[None, :] < marks[:, None]).astype(jnp.int32), axis=1)
    near = band ^ 1
    order = jnp.stack(
        [1 + band, 1 + (band ^ 2), 5 * (band % 2), 1 + near, 1 + (near ^ 2), 5 * (near % 2)]
    )
    sixth = jnp.arange(6, dtype=jnp.int32)
    inverse = jnp.sum(jnp.where(order[None, :] == sixth[:, None], sixth[None, :], 0), axis=1)
    steps = jnp.arange(sector, dtype=jnp.int32)
    cells = (order[:, None] * sector + steps[None, :]).reshape(-1)
    slots = (inverse[:, None] * sector + steps[None, :]).reshape(-1)
    hot = (cells[:, None] == marks[None, :seen]).astype(jnp.int32)
    widths = begins[1:] - begins[:-1]
    pool_table = jnp.stack(
        [jnp.sum(hot * begins[None, :seen], axis=1), jnp.sum(hot * widths[None, :], axis=1)]
    )
    pixel_table = jnp.stack([begins[:seen], slots])

    turned = (columns + 1) * rows
    half = 3 * sector
    probs, probs_t, context_t, kept, sent = call(
        functools.partial(pool_kernel, rows),
        [
            jax.ShapeDtypeStruct((bins * rows, columns), F32),
            jax.ShapeDtypeStruct((turned, LANES), BF16),
            jax.ShapeDtypeStruct((turned, LANES), BF16),
            jax.ShapeDtypeStruct((half, channels, LANES), BF16),
            jax.ShapeDtypeStruct((half, channels, LANES), BF16),
        ],
        [
            pltpu.VMEM((bins * rows, columns), F32),
            pltpu.VMEM((turned, LANES), BF16),
            pltpu.VMEM((turned, LANES), BF16),
            pltpu.VMEM((columns * rows, LANES), F32),
            pltpu.VMEM((columns * rows, LANES), F32),
            pltpu.VMEM((channels * rows, columns), F32),
            pltpu.SemaphoreType.DMA((3,)),
        ],
        [smem(), vmem(), vmem()],
        2 * seen * 3 * rows * LANES * LANES,
        20 * bins * rows * columns,
        [anywhere()] * 3 + [vmem()] * 2,
    )(
        pool_table,
        depth_logits[0].reshape(bins * rows, columns),
        context[0].reshape(channels * rows, columns),
    )

    row_flops = 2 * TAPS * TAPS * hidden * hidden * length

    def act_grad(sources, lows, highs, starts):
        total = sum(h - l for l, h in zip(lows, highs))
        return call(
            functools.partial(act_grad_kernel, (lows, highs, starts)),
            jax.ShapeDtypeStruct((len(starts), hidden, length), BF16),
            [pltpu.VMEM((total, length, hidden), BF16)],
            [vmem() for _ in sources] + [vmem()],
            row_flops * len(starts),
            2 * (total + len(starts)) * length * hidden,
        )(*sources, conv2_weight)

    inner_grad = act_grad([out_grad], (0,), (sector,), tuple(range(sector - 2)))
    outer_grad = act_grad(
        [low_grad, out_grad, out_grad, high_grad],
        (0, 0, sector - 2, 0),
        (2, 2, sector, 2),
        (0, 1, 4, 5),
    )

    summed = rounded_sum(kept, swapped(sent, blocks, 1))
    own = rounded_sum(summed[:sector], swapped(summed[sector : 2 * sector], blocks, 2))
    inward = [(i, i ^ 2) for i in range(blocks) if i % bands in (1, 2)]
    outward = [(i ^ 2, i) for i in range(blocks) if i % bands in (1, 2)]
    edge = rounded_sum(
        summed[2 * sector :], lax.ppermute(summed[2 * sector :], "blk", inward)
    )
    first = band == 0
    firsts = [i for i in range(blocks) if i % bands == 0]
    lasts = [i for i in range(blocks) if i % bands == bands - 1]
    last = band == bands - 1
    outer = jnp.logical_or(first, last)
    more = ((0, sector), (0, 0), (0, 0))
    far = jnp.where(
        first,
        jnp.concatenate([edge, own[:2]], axis=0),
        jnp.where(
            last,
            jnp.concatenate([own[sector - 2 :], edge], axis=0),
            jnp.pad(ends(own, False), more),
        ),
    )
    two = jnp.where(first, edge[:2], edge[sector - 2 :])

    def to_next(value, more):
        pairs = [(i, (i - 1 - more) % blocks) for i in firsts]
        pairs = pairs + [(i, (i + 1 + more) % blocks) for i in lasts]
        return lax.ppermute(value, "blk", pairs)

    far_halo = lax.ppermute(far, "blk", off_chip)
    two = to_next(two, 1)
    near_halo = lax.ppermute(ends(own, True), "blk", on_chip)
    other = jnp.where(band < bands // 2, camera - 1, camera + 1) % cameras
    ranges = jnp.concatenate(
        [lax.dynamic_slice_in_dim(rng_map, k, 1, 0) for k in (camera, other)], axis=0
    )
    ranges = jnp.pad(ranges, ((0, 0), (0, LANES - bins)), constant_values=-1).reshape(-1, 1)
    weight_t = conv1_weight.transpose(1, 3, 0, 2).reshape(TAPS * hidden, TAPS * channels)
    weight = conv1_weight.reshape(TAPS, TAPS * channels, hidden)
    grad_rows = TAPS * TAPS * (hidden + channels)
    unit = blocks * 16
    grad_rows = -(-grad_rows // unit) * unit
    wide = sector + 2
    keep, send, own_reply, other_reply = call(
        grid_kernel,
        [
            jax.ShapeDtypeStruct((grad_rows // 2, hidden), BF16),
            jax.ShapeDtypeStruct((grad_rows // 2, hidden), BF16),
            jax.ShapeDtypeStruct((sector, channels, LANES), BF16),
            jax.ShapeDtypeStruct((sector, channels, LANES), BF16),
        ],
        [
            pltpu.VMEM((sector + 4, channels, 2 * LANES), BF16),
            pltpu.VMEM(((sector + 4) * channels, length), BF16),
            pltpu.VMEM((TAPS * channels, wide * length), BF16),
            pltpu.VMEM((TAPS * hidden, wide * length), BF16),
            pltpu.VMEM((wide * hidden, length), BF16),
            pltpu.VMEM((hidden, wide * length), BF16),
            pltpu.VMEM((sector * channels, length), BF16),
            pltpu.VMEM((wide, hidden, length), BF16),
            pltpu.VMEM((sector * length, hidden), BF16),
            pltpu.VMEM((grad_rows, hidden), BF16),
            pltpu.SemaphoreType.DMA((4,)),
        ],
        [smem()] + [vmem()] * 8 + [anywhere()] * 3,
        row_flops * (sector + 3 * sector // 2),
        20 * sector * length * hidden,
    )(
        place,
        own,
        edge,
        near_halo,
        far_halo,
        two,
        ranges,
        weight_t,
        weight,
        inner_grad,
        outer_grad,
        out_grad.reshape(sector * length, hidden),
    )

    partner = swapped(own_reply, blocks, 2)
    edge_reply = to_next(other_reply, 0)
    passed = lax.ppermute(edge_reply, "blk", outward)
    edge_reply = jnp.where(outer, edge_reply, passed)
    theirs = swapped(
        jnp.concatenate([own_reply, partner, edge_reply], axis=0), blocks, 1
    )
    value, other_value = total_over_blocks(keep, send, position, blocks)

    replies = (own_reply, partner, edge_reply, theirs)
    scratch = [pltpu.VMEM((seen, channels, LANES), BF16), pltpu.VMEM((turned, LANES), F32)]
    cell_flops = 2 * seen * 3 * rows * LANES * LANES
    context_grad = call(
        functools.partial(context_kernel, rows),
        jax.ShapeDtypeStruct((channels * rows, columns), BF16),
        scratch + [pltpu.VMEM((channels * rows, columns), F32)],
        [smem()] + [vmem()] * 5,
        cell_flops,
        10 * bins * rows * columns,
    )(pixel_table, *replies, probs_t)
    logit_grad = call(
        functools.partial(logit_kernel, rows),
        jax.ShapeDtypeStruct((bins * rows, columns), F32),
        scratch,
        [smem()] + [vmem()] * 7,
        cell_flops,
        20 * bins * rows * columns,
    )(pixel_table, *replies, probs, context_t, lidar_bins[0])

    second = TAPS * TAPS * hidden
    first_rows = TAPS * TAPS * channels
    second_grad, first_grad = call(
        finish_kernel,
        [
            jax.ShapeDtypeStruct((second, hidden), F32),
            jax.ShapeDtypeStruct((first_rows, hidden), F32),
        ],
        [],
        [smem(), vmem(), vmem()],
        1,
        6 * grad_rows * hidden,
    )(place, value, other_value)
    return (
        logit_grad.reshape(1, bins, rows, columns),
        context_grad.reshape(1, channels, rows, columns),
        first_grad.reshape(TAPS, TAPS, channels, hidden),
        second_grad.reshape(TAPS, TAPS, hidden, hidden),
    )


def solution(mesh):
    return jax.shard_map(
        shards,
        mesh=mesh,
        in_specs=(
            P(("group", "blk"), None, None, None),
            P(("group", "blk"), None, None, None),
            P(("group", "blk"), None, None),
            P(),
            P(),
            P(),
            P(),
            P(("group", "blk"), None, None),
        ),
        out_specs=(
            P(("group", "blk"), None, None, None),
            P(("group", "blk"), None, None, None),
            P("group", None, None, None),
            P("group", None, None, None),
        ),
        check_vma=False,
    )
```

```python
import functools

import jax
import jax.numpy as jnp
from jax import lax
from jax.experimental import pallas as pl
from jax.experimental.pallas import tpu as pltpu
from jax.sharding import PartitionSpec as P

DEPTH_WEIGHT = 3.0
TAPS = 3
LANES = 128
F32 = jnp.float32
BF16 = jnp.bfloat16


def product(left, right, left_dim, right_dim):
    return lax.dot_general(
        left, right, (((left_dim,), (right_dim,)), ((), ())), preferred_element_type=F32
    )


def padded_rows(value, rows):
    missing = rows - value.shape[0]
    if missing == 0:
        return value
    return jnp.concatenate([value, jnp.zeros((missing, value.shape[1]), value.dtype)], axis=0)


def sectors_of(band, bands):
    partner = (band + 2) % bands
    return 1 + band, 1 + partner, (bands + 1) * (band % 2)


def pool_kernel(
    rows,
    sight,
    around,
    place,
    az_map,
    logits,
    context,
    probs_out,
    probs_t_out,
    context_t_out,
    kept,
    sent,
    begins,
    probs,
    probs_t,
    context_t,
    wide_p,
    wide_c,
    plain_c,
    done,
):
    columns = logits.shape[1]
    bins = logits.shape[0] // rows
    channels = context.shape[0] // rows
    half = kept.shape[0]
    sector = half // 3
    bands = 4
    position = place[0]
    band, camera = position % bands, position // bands
    seen = 2 * half
    begins[seen] = columns

    def mark(step, _):
        column = columns - 1 - step
        cell = az_map[camera, column] - camera * sight + sight // 4
        cell = jnp.where(cell < 0, cell + around, cell)
        begins[jnp.where(cell >= around, cell - around, cell)] = column
        return 0

    lax.fori_loop(0, columns, mark, 0, unroll=8)
    scores = logits[...].reshape(bins, rows, columns)
    powers = jnp.exp(scores - jnp.max(scores, axis=0, keepdims=True))
    shares = powers / jnp.sum(powers, axis=0, keepdims=True)
    probs[...] = shares.reshape(bins * rows, columns)
    copies = [pltpu.make_async_copy(probs, probs_out, done.at[0])]
    copies[0].start()
    plain_c[...] = context[...].astype(F32)

    def turn(row, _):
        block = padded_rows(probs[pl.ds(row, bins, stride=rows), :], LANES)
        wide_p[pl.ds(row, columns, stride=rows), :] = jnp.transpose(block)
        block = padded_rows(plain_c[pl.ds(row, channels, stride=rows), :], LANES)
        wide_c[pl.ds(row, columns, stride=rows), :] = jnp.transpose(block)
        return 0

    lax.fori_loop(0, rows, turn, 0, unroll=4)
    for wide, narrow, out in (
        (wide_p, probs_t, probs_t_out),
        (wide_c, context_t, context_t_out),
    ):
        narrow[0 : columns * rows, :] = wide[...].astype(BF16)
        narrow[columns * rows :, :] = jnp.zeros((rows, LANES), BF16)
        copies.append(pltpu.make_async_copy(narrow, out, done.at[len(copies)]))
        copies[-1].start()
    line = lax.broadcasted_iota(jnp.int32, (TAPS * rows, LANES), 0)

    def cell_sum(cell):
        start = begins[cell]
        span = pl.ds(pl.multiple_of(start * rows, rows), TAPS * rows)
        features = context_t[span, :]
        width = (begins[cell + 1] - start) * rows
        features = jnp.where(line < width, features, jnp.zeros_like(features))
        return product(features, probs_t[span, :], 0, 0)[:channels].astype(BF16)

    near = band + 1 - 2 * (band % 2)
    for group, (mine, theirs) in enumerate(
        zip(sectors_of(band, bands), sectors_of(near, bands))
    ):

        def one_cell(step, _, group=group, mine=mine, theirs=theirs):
            sent[group * sector + step] = cell_sum(theirs * sector + step)
            kept[group * sector + step] = cell_sum(mine * sector + step)
            return 0

        lax.fori_loop(0, sector, one_cell, 0, unroll=4)
    for copy in copies:
        copy.wait()


def act_row(taps, source, start, out, row):
    hidden, length = out.shape[1:]
    stacked = jnp.concatenate([source[start + i] for i in range(TAPS)], axis=1)
    sums = product(taps, stacked, 1, 1)
    place = lax.broadcasted_iota(jnp.int32, (hidden, length), 1)
    ahead = pltpu.roll(sums[:hidden], length - 1, 1)
    behind = pltpu.roll(sums[2 * hidden :], 1, 1)
    total = sums[hidden : 2 * hidden]
    total = total + jnp.where(place < length - 1, ahead, 0.0)
    total = total + jnp.where(place > 0, behind, 0.0)
    out[row] = total.astype(BF16)


def act_taps_of(weight):
    hidden = weight.shape[3]
    return jnp.concatenate(
        [weight[TAPS - 1 - i].reshape(TAPS * hidden, hidden) for i in range(TAPS)], axis=1
    )


def inner_acts_kernel(upstream, weight, out):
    def step(row, _):
        act_row(act_taps_of(weight), upstream, row, out, row)
        return 0

    lax.fori_loop(0, out.shape[0], step, 0)


def outer_acts_kernel(place, near, far, upstream, weight, out, low, high):
    sector = upstream.shape[0]
    low[2:4] = upstream[0:2]
    high[0:2] = upstream[sector - 2 :]

    @pl.when(place[0] % 2 == 0)
    def _():
        low[0:2] = far[...]
        high[2:4] = near[...]

    @pl.when(place[0] % 2 == 1)
    def _():
        low[0:2] = near[...]
        high[2:4] = far[...]

    def step(row, _):
        act_row(act_taps_of(weight), low, row, out, row)
        act_row(act_taps_of(weight), high, row, out, row + 2)
        return 0

    lax.fori_loop(0, 2, step, 0)


def grid_kernel(
    place,
    own,
    edge,
    near_halo,
    far_halo,
    two,
    ranges,
    weight,
    inner_grad,
    outer_grad,
    upstream,
    keep,
    send,
    own_reply,
    other_reply,
    cells,
    grid_low,
    grid_taps,
    act_taps,
    slope_rows,
    slope_lanes,
    grid_grad,
    weight_t,
    range_hot,
    picks,
    grads,
):
    sector, channels, lanes = own.shape
    hidden, length = outer_grad.shape[1:]
    bands = 4
    cameras, bins = ranges.shape
    position = place[0]
    mine, core = position % bands, position % 2
    camera = position // bands
    other = jnp.where(mine < bands // 2, camera + cameras - 1, camera + 1) % cameras
    wide = sector + 4
    cells[2 : 2 + sector, :, :lanes] = own[...]
    cells[:, :, lanes:] = jnp.zeros((wide, channels, lanes), BF16)

    @pl.when(mine == 0)
    def _():
        cells[0:2, :, :lanes] = edge[sector - 2 : sector]
        cells[2 + sector :, :, :lanes] = near_halo[...]
        cells[0 : sector + 2, :, lanes:] = far_halo[...]

    @pl.when(mine == 1)
    def _():
        cells[0:2, :, :lanes] = near_halo[...]
        cells[2 + sector :, :, :lanes] = far_halo[0:2]
        cells[0:2, :, lanes:] = two[...]

    @pl.when(mine == bands - 2)
    def _():
        cells[0:2, :, :lanes] = far_halo[0:2]
        cells[2 + sector :, :, :lanes] = near_halo[...]
        cells[2 + sector :, :, lanes:] = two[...]

    @pl.when(mine == bands - 1)
    def _():
        cells[0:2, :, :lanes] = near_halo[...]
        cells[2 + sector :, :, :lanes] = edge[0:2]
        cells[2:, :, lanes:] = far_halo[...]

    picks[...] = jnp.full(picks.shape, -1, jnp.int32)
    picks[0:1, 0:bins] = ranges[pl.ds(camera, 1), :]
    picks[0:1, lanes : lanes + bins] = ranges[pl.ds(other, 1), :]
    spots = lax.broadcasted_iota(jnp.int32, (length, 2 * lanes), 0)
    range_hot[...] = (spots == picks[0:1, :]).astype(F32).astype(BF16)
    for column in range(TAPS):
        for row in range(TAPS):
            weight_t[column * hidden : (column + 1) * hidden, row * channels : (row + 1) * channels] = (
                jnp.transpose(
                    weight[row, column * channels : (column + 1) * channels, :].astype(F32)
                ).astype(BF16)
            )

    def behind(value):
        turned = pltpu.roll(value, 1, 1)
        lane = lax.broadcasted_iota(jnp.int32, (value.shape[0], LANES), 1)
        first = jnp.where(lane > 0, turned[:, :LANES], 0.0)
        return jnp.concatenate([first, turned[:, LANES:]], axis=1)

    def ahead(value):
        turned = pltpu.roll(value, length - 1, 1)
        lane = lax.broadcasted_iota(jnp.int32, (value.shape[0], LANES), 1)
        last = jnp.where(lane < LANES - 1, turned[:, length - LANES :], 0.0)
        return jnp.concatenate([turned[:, : length - LANES], last], axis=1)

    for chunk in range(0, wide, 4):
        block = cells[chunk : chunk + 4].reshape(4 * channels, 2 * lanes)
        summed = product(block, range_hot[...], 1, 1)
        for row in range(chunk, chunk + 4):
            value = summed[(row - chunk) * channels : (row - chunk + 1) * channels]
            grid_low[row * channels : (row + 1) * channels, :] = value.astype(BF16)
            if 0 < row < wide - 1:
                spread = pl.ds((row - 1) * length, length)
                grid_taps[0:channels, spread] = behind(value).astype(BF16)
                grid_taps[channels : 2 * channels, spread] = value.astype(BF16)
                grid_taps[2 * channels :, spread] = ahead(value).astype(BF16)

    def one_row(row, act_grad):
        source = pl.ds(pl.multiple_of(row * channels, channels), TAPS * channels)
        sums = product(weight_t[...], grid_low[source, :], 1, 0)
        value = behind(sums[:hidden]) + sums[hidden : 2 * hidden] + ahead(sums[2 * hidden :])
        logistic = 0.5 + 0.5 * jnp.tanh(0.5 * value)
        active = value * logistic
        spread = pl.ds(pl.multiple_of(row * length, length), length)
        act_taps[0:hidden, spread] = behind(active).astype(BF16)
        act_taps[hidden : 2 * hidden, spread] = active.astype(BF16)
        act_taps[2 * hidden :, spread] = ahead(active).astype(BF16)
        slope = logistic * (1.0 + value * (1.0 - logistic))
        result = (act_grad.astype(F32) * slope).astype(BF16)
        slope_rows[pl.ds(pl.multiple_of(row * hidden, hidden), hidden), :] = result
        slope_lanes[:, spread] = result

    def outside(pair, _):
        one_row(pair, outer_grad[pair])
        one_row(pair + sector, outer_grad[pair + 2])
        return 0

    def inside(row, _):
        one_row(row + 2, inner_grad[row])
        return 0

    lax.fori_loop(0, 2, outside, 0)
    lax.fori_loop(0, sector - 2, inside, 0, unroll=2)
    count = sector * length
    tall = TAPS * hidden
    short = TAPS * channels

    def second(tap, _):
        window = pl.ds(pl.multiple_of(tap * length, length), count)
        result = product(act_taps[:, window], upstream[...], 1, 0)
        grads[pl.ds(pl.multiple_of(tap * tall, tall), tall), :] = result.astype(BF16)
        return 0

    lax.fori_loop(0, TAPS, second, 0)
    for tap in range(TAPS):
        result = product(
            grid_taps[:, tap * length : tap * length + count],
            slope_lanes[:, length : length + count],
            1,
            1,
        )
        base = TAPS * tall + tap * short
        grads[base : base + short, :] = result.astype(BF16)
    base = TAPS * (tall + short)
    grads[base:, :] = jnp.zeros((grads.shape[0] - base, hidden), BF16)
    half = keep.shape[0]
    keep[...] = grads[pl.ds(pl.multiple_of(core * half, half), half), :]
    send[...] = grads[pl.ds(pl.multiple_of((1 - core) * half, half), half), :]
    flipped = jnp.concatenate([weight[TAPS - 1 - i] for i in range(TAPS)], axis=1)

    def back(row, _):
        source = pl.ds(pl.multiple_of(row * hidden, hidden), TAPS * hidden)
        sums = product(flipped, slope_rows[source, :], 1, 0)
        value = ahead(sums[:channels]) + sums[channels : 2 * channels]
        value = value + behind(sums[2 * channels :])
        grid_grad[pl.ds(pl.multiple_of(row * channels, channels), channels), :] = value.astype(BF16)
        return 0

    lax.fori_loop(0, sector, back, 0, unroll=2)
    picked = product(grid_grad[...], range_hot[...], 1, 0).astype(BF16)
    own_reply[...] = picked[:, :lanes].reshape(sector, channels, lanes)
    other_reply[...] = picked[:, lanes:].reshape(sector, channels, lanes)


def finish_kernel(shifts, place, value, other, second, first, total):
    half = value.shape[0]
    size = half // 4
    position = place[0]
    core = position % 2
    for source, side in ((value, core), (other, 1 - core)):
        digit = jnp.where(side == 0, position >> shifts[0], position >> shifts[1]) & 3
        for mask in range(4):
            spot = side * half + (digit ^ mask) * size
            total[pl.ds(pl.multiple_of(spot, size), size), :] = source[
                mask * size : (mask + 1) * size, :
            ]
    count = second.shape[0]
    second[...] = total[0:count, :].astype(F32)
    first[...] = total[count : count + first.shape[0], :].astype(F32)


def lay_out(place, sector, mine, theirs, wedges):
    bands = 4
    band = place[0] % bands
    near = band + 1 - 2 * (band % 2)
    for group, spot in enumerate(sectors_of(band, bands)):
        wedges[pl.ds(spot * sector, sector)] = mine[group][...]
    for group, spot in enumerate(sectors_of(near, bands)):
        wedges[pl.ds(spot * sector, sector)] = theirs[group * sector : (group + 1) * sector]


def logit_kernel(
    rows,
    place,
    begins,
    own,
    partner,
    edge,
    theirs,
    probs,
    context_t,
    lidar,
    logit_grad,
    wedges,
    wide,
):
    columns = probs.shape[1]
    bins = probs.shape[0] // rows
    sector, channels, _ = own.shape
    lay_out(place, sector, (own, partner, edge), theirs, wedges)

    def one_cell(cell, _):
        span = pl.ds(pl.multiple_of(begins[cell] * rows, rows), TAPS * rows)
        wide[span, :] = product(context_t[span, :][:, :channels], wedges[cell], 1, 0)
        return 0

    lax.fori_loop(0, wedges.shape[0], one_cell, 0, unroll=8)

    def turn(row, _):
        block = jnp.transpose(wide[pl.ds(row, columns, stride=rows), :])
        logit_grad[pl.ds(row, bins, stride=rows), :] = block[:bins]
        return 0

    lax.fori_loop(0, rows, turn, 0, unroll=4)
    share = probs[...].reshape(bins, rows, columns)
    slope = logit_grad[...].reshape(bins, rows, columns)
    expected = jnp.sum(share * slope, axis=0, keepdims=True)
    target = lidar[...][None]
    seen = jnp.where(target >= 0, DEPTH_WEIGHT, 0.0)
    level = lax.broadcasted_iota(jnp.int32, share.shape, 0)
    hit = jnp.where(level == target, DEPTH_WEIGHT, 0.0)
    result = share * (slope - expected) + (seen * share - hit)
    logit_grad[...] = result.reshape(bins * rows, columns)


def context_kernel(
    rows,
    place,
    begins,
    own,
    partner,
    edge,
    theirs,
    probs_t,
    context_grad,
    wedges,
    wide,
    plain,
):
    columns = context_grad.shape[1]
    sector, channels, _ = own.shape
    lay_out(place, sector, (own, partner, edge), theirs, wedges)
    wide[...] = jnp.zeros_like(wide)

    def one_cell(cell, _):
        span = pl.ds(pl.multiple_of(begins[cell] * rows, rows), TAPS * rows)
        wide[span, 0:channels] = product(probs_t[span, :], wedges[cell], 1, 1)
        return 0

    lax.fori_loop(0, wedges.shape[0], one_cell, 0, unroll=8)

    def turn(row, _):
        block = jnp.transpose(wide[pl.ds(row, columns, stride=rows), :])
        plain[pl.ds(row, channels, stride=rows), :] = block[:channels]
        return 0

    lax.fori_loop(0, rows, turn, 0, unroll=4)
    context_grad[...] = plain[...].astype(BF16)


def vmem():
    return pl.BlockSpec(memory_space=pltpu.VMEM)


def smem():
    return pl.BlockSpec(memory_space=pltpu.SMEM)


def anywhere():
    return pl.BlockSpec(memory_space=pltpu.HBM)


def call(kernel, out_shape, scratch, spaces, flops, moved, outs=None, limit=16):
    many = isinstance(out_shape, (list, tuple))
    return pl.pallas_call(
        kernel,
        out_shape=out_shape,
        in_specs=spaces,
        out_specs=outs or ([vmem() for _ in out_shape] if many else vmem()),
        scratch_shapes=scratch,
        compiler_params=pltpu.CompilerParams(vmem_limit_bytes=limit * 1024 * 1024),
        cost_estimate=pl.CostEstimate(flops=flops, bytes_accessed=moved, transcendentals=0),
    )


def rounded_sum(left, right):
    return (left.astype(F32) + right.astype(F32)).astype(BF16)


def swapped(value, blocks, mask):
    return lax.ppermute(value, "blk", [(i, i ^ mask) for i in range(blocks)])


def piece(value, index, count):
    size = value.shape[0] // count
    return lax.dynamic_slice_in_dim(value, index * size, size, 0)


def axis_orders(count):
    pairs = list(range(1, count, 2))
    return pairs, pairs[1:] + pairs[:1]


def total_over_blocks(keep, send, position, blocks):
    count = blocks.bit_length() - 1
    orders = axis_orders(count)
    core = position & 1
    digits = [
        jnp.where(core == 0, position >> one, position >> two) & 3 for one, two in zip(*orders)
    ]

    def sent(part, step, mask):
        to = [(i, i ^ (mask << orders[i & 1][step])) for i in range(blocks)]
        return lax.ppermute(part, "blk", to)

    value = rounded_sum(keep, swapped(send, blocks, 1))
    for step, digit in enumerate(digits):
        leaving = [piece(value, digit ^ mask, 4) for mask in (3, 1, 2)]
        arrived = [sent(part, step, mask) for part, mask in zip(leaving, (3, 1, 2))]
        total = piece(value, digit, 4).astype(F32)
        for part in arrived:
            total = total + part.astype(F32)
        value = total.astype(BF16)
    for step, digit in reversed(list(enumerate(digits))):
        held = [value] + [sent(value, step, mask) for mask in (1, 2, 3)]
        if step == 0:
            value = jnp.concatenate(held, axis=0)
            break
        high, low = digit >> 1 == 1, digit & 1 == 1

        def at(k):
            one = jnp.where(low, held[k ^ 1], held[k])
            two = jnp.where(low, held[k ^ 3], held[k ^ 2])
            return jnp.where(high, two, one)

        value = jnp.concatenate([at(k) for k in range(4)], axis=0)
    return value, swapped(value, blocks, 1)


def shards(
    depth_logits, context, lidar_bins, az_map, rng_map, conv1_weight, conv2_weight, out_grad
):
    blocks = lax.axis_size("blk")
    position = lax.axis_index("blk")
    cameras, columns = az_map.shape
    bands = blocks // cameras
    sector, length, hidden = out_grad.shape
    bins, rows = depth_logits.shape[1:3]
    channels = context.shape[1]
    if bands != 4 or blocks != 1 << (blocks.bit_length() - 1) or blocks.bit_length() % 2 or bins > LANES or channels > LANES or sector < 6:
        raise ValueError("unsupported sizes")
    band = position % bands
    sight = bands * sector
    seen = sight + sight // 2

    core = position & 1
    place = position.reshape(1)
    on_chip = [(i, i ^ 1) for i in range(blocks)]
    off_chip = [(i, (i + 1 if i & 1 else i - 1) % blocks) for i in range(blocks)]

    def ends(value, near):
        count = value.shape[0]
        start = jnp.where((core == 0) == near, count - 2, 0)
        return lax.dynamic_slice_in_dim(value, start, 2, 0)

    far_grad = lax.ppermute(ends(out_grad, False), "blk", off_chip)
    near_grad = lax.ppermute(ends(out_grad, True), "blk", on_chip)

    turned = (columns + 1) * rows
    half = 3 * sector
    probs, probs_t, context_t, kept, sent, begins = call(
        functools.partial(pool_kernel, rows, sight, blocks * sector),
        [
            jax.ShapeDtypeStruct((bins * rows, columns), F32),
            jax.ShapeDtypeStruct((turned, LANES), BF16),
            jax.ShapeDtypeStruct((turned, LANES), BF16),
            jax.ShapeDtypeStruct((half, channels, LANES), BF16),
            jax.ShapeDtypeStruct((half, channels, LANES), BF16),
            jax.ShapeDtypeStruct((seen + 1,), jnp.int32),
        ],
        [
            pltpu.VMEM((bins * rows, columns), F32),
            pltpu.VMEM((turned, LANES), BF16),
            pltpu.VMEM((turned, LANES), BF16),
            pltpu.VMEM((columns * rows, LANES), F32),
            pltpu.VMEM((columns * rows, LANES), F32),
            pltpu.VMEM((channels * rows, columns), F32),
            pltpu.SemaphoreType.DMA((3,)),
        ],
        [smem(), smem(), vmem(), vmem()],
        2 * seen * 3 * rows * LANES * LANES,
        20 * bins * rows * columns,
        [anywhere()] * 3 + [vmem()] * 2 + [smem()],
        limit=56,
    )(
        place,
        az_map,
        depth_logits[0].reshape(bins * rows, columns),
        context[0].reshape(channels * rows, columns),
    )

    row_flops = 2 * TAPS * TAPS * hidden * hidden * length

    inner_grad = call(
        inner_acts_kernel,
        jax.ShapeDtypeStruct((sector - 2, hidden, length), BF16),
        [],
        [vmem()] * 2,
        row_flops * (sector - 2),
        4 * sector * length * hidden,
    )(out_grad, conv2_weight)
    outer_grad = call(
        outer_acts_kernel,
        jax.ShapeDtypeStruct((4, hidden, length), BF16),
        [pltpu.VMEM((4, length, hidden), BF16)] * 2,
        [smem()] + [vmem()] * 4,
        row_flops * 4,
        16 * length * hidden,
    )(place, near_grad, far_grad, out_grad, conv2_weight)

    summed = rounded_sum(kept, swapped(sent, blocks, 1))
    own = rounded_sum(summed[:sector], swapped(summed[sector : 2 * sector], blocks, 2))
    inward = [(i, i ^ 2) for i in range(blocks) if i % bands in (1, 2)]
    outward = [(i ^ 2, i) for i in range(blocks) if i % bands in (1, 2)]
    edge = rounded_sum(
        summed[2 * sector :], lax.ppermute(summed[2 * sector :], "blk", inward)
    )
    first = band == 0
    firsts = [i for i in range(blocks) if i % bands == 0]
    lasts = [i for i in range(blocks) if i % bands == bands - 1]
    last = band == bands - 1
    outer = jnp.logical_or(first, last)
    more = ((0, sector), (0, 0), (0, 0))
    far = jnp.where(
        first,
        jnp.concatenate([edge, own[:2]], axis=0),
        jnp.where(
            last,
            jnp.concatenate([own[sector - 2 :], edge], axis=0),
            jnp.pad(ends(own, False), more),
        ),
    )
    two = jnp.where(first, edge[:2], edge[sector - 2 :])

    def to_next(value, more):
        pairs = [(i, (i - 1 - more) % blocks) for i in firsts]
        pairs = pairs + [(i, (i + 1 + more) % blocks) for i in lasts]
        return lax.ppermute(value, "blk", pairs)

    far_halo = lax.ppermute(far, "blk", off_chip)
    two = to_next(two, 1)
    near_halo = lax.ppermute(ends(own, True), "blk", on_chip)
    weight = conv1_weight.reshape(TAPS, TAPS * channels, hidden)
    grad_rows = TAPS * TAPS * (hidden + channels)
    unit = blocks * 16
    grad_rows = -(-grad_rows // unit) * unit
    wide = sector + 2
    keep, send, own_reply, other_reply = call(
        grid_kernel,
        [
            jax.ShapeDtypeStruct((grad_rows // 2, hidden), BF16),
            jax.ShapeDtypeStruct((grad_rows // 2, hidden), BF16),
            jax.ShapeDtypeStruct((sector, channels, LANES), BF16),
            jax.ShapeDtypeStruct((sector, channels, LANES), BF16),
        ],
        [
            pltpu.VMEM((sector + 4, channels, 2 * LANES), BF16),
            pltpu.VMEM(((sector + 4) * channels, length), BF16),
            pltpu.VMEM((TAPS * channels, wide * length), BF16),
            pltpu.VMEM((TAPS * hidden, wide * length), BF16),
            pltpu.VMEM((wide * hidden, length), BF16),
            pltpu.VMEM((hidden, wide * length), BF16),
            pltpu.VMEM((sector * channels, length), BF16),
            pltpu.VMEM((TAPS * hidden, TAPS * channels), BF16),
            pltpu.VMEM((length, 2 * LANES), BF16),
            pltpu.VMEM((8, 2 * LANES), jnp.int32),
            pltpu.VMEM((grad_rows, hidden), BF16),
        ],
        [smem()] + [vmem()] * 10,
        row_flops * (sector + 3 * sector // 2),
        20 * sector * length * hidden,
        limit=32,
    )(
        place,
        own,
        edge,
        near_halo,
        far_halo,
        two,
        rng_map,
        weight,
        inner_grad,
        outer_grad,
        out_grad.reshape(sector * length, hidden),
    )

    partner = swapped(own_reply, blocks, 2)
    edge_reply = to_next(other_reply, 0)
    passed = lax.ppermute(edge_reply, "blk", outward)
    edge_reply = jnp.where(outer, edge_reply, passed)
    theirs = swapped(
        jnp.concatenate([own_reply, partner, edge_reply], axis=0), blocks, 1
    )
    value, other_value = total_over_blocks(keep, send, position, blocks)

    replies = (own_reply, partner, edge_reply, theirs)
    scratch = [pltpu.VMEM((seen, channels, LANES), BF16), pltpu.VMEM((turned, LANES), F32)]
    cell_flops = 2 * seen * 3 * rows * LANES * LANES
    context_grad = call(
        functools.partial(context_kernel, rows),
        jax.ShapeDtypeStruct((channels * rows, columns), BF16),
        scratch + [pltpu.VMEM((channels * rows, columns), F32)],
        [smem()] * 2 + [vmem()] * 5,
        cell_flops,
        10 * bins * rows * columns,
    )(place, begins, *replies, probs_t)
    logit_grad = call(
        functools.partial(logit_kernel, rows),
        jax.ShapeDtypeStruct((bins * rows, columns), F32),
        scratch,
        [smem()] * 2 + [vmem()] * 7,
        cell_flops,
        20 * bins * rows * columns,
    )(place, begins, *replies, probs, context_t, lidar_bins[0])

    second = TAPS * TAPS * hidden
    first_rows = TAPS * TAPS * channels
    second_grad, first_grad = call(
        functools.partial(
            finish_kernel, [order[0] for order in axis_orders(blocks.bit_length() - 1)]
        ),
        [
            jax.ShapeDtypeStruct((second, hidden), F32),
            jax.ShapeDtypeStruct((first_rows, hidden), F32),
        ],
        [pltpu.VMEM((grad_rows, hidden), BF16)],
        [smem(), vmem(), vmem()],
        1,
        6 * grad_rows * hidden,
    )(place, value, other_value)
    return (
        logit_grad.reshape(1, bins, rows, columns),
        context_grad.reshape(1, channels, rows, columns),
        first_grad.reshape(TAPS, TAPS, channels, hidden),
        second_grad.reshape(TAPS, TAPS, hidden, hidden),
    )


def solution(mesh):
    return jax.shard_map(
        shards,
        mesh=mesh,
        in_specs=(
            P(("group", "blk"), None, None, None),
            P(("group", "blk"), None, None, None),
            P(("group", "blk"), None, None),
            P(),
            P(),
            P(),
            P(),
            P(("group", "blk"), None, None),
        ),
        out_specs=(
            P(("group", "blk"), None, None, None),
            P(("group", "blk"), None, None, None),
            P("group", None, None, None),
            P("group", None, None, None),
        ),
        check_vma=False,
    )
```

```python
import functools

import jax
import jax.numpy as jnp
from jax import lax
from jax.experimental import pallas as pl
from jax.experimental.pallas import tpu as pltpu
from jax.sharding import PartitionSpec as P

DEPTH_WEIGHT = 3.0
TAPS = 3
LANES = 128
F32 = jnp.float32
BF16 = jnp.bfloat16


def product(left, right, left_dim, right_dim):
    return lax.dot_general(
        left, right, (((left_dim,), (right_dim,)), ((), ())), preferred_element_type=F32
    )


def padded_rows(value, rows):
    missing = rows - value.shape[0]
    if missing == 0:
        return value
    return jnp.concatenate([value, jnp.zeros((missing, value.shape[1]), value.dtype)], axis=0)


def sectors_of(band, bands):
    partner = (band + 2) % bands
    return 1 + band, 1 + partner, (bands + 1) * (band % 2)


def pool_kernel(
    rows,
    sight,
    around,
    place,
    az_map,
    logits,
    context,
    probs_out,
    probs_t_out,
    context_t_out,
    kept,
    sent,
    begins,
    probs,
    wide_p,
    wide_c,
    plain_c,
    done,
):
    columns = logits.shape[1]
    bins = logits.shape[0] // rows
    channels = context.shape[0] // rows
    half = kept.shape[0]
    sector = half // 3
    bands = 4
    position = place[0]
    band, camera = position % bands, position // bands
    seen = 2 * half
    begins[seen] = columns
    scores = logits[...].reshape(bins, rows, columns)
    powers = jnp.exp(scores - jnp.max(scores, axis=0, keepdims=True))
    shares = powers / jnp.sum(powers, axis=0, keepdims=True)
    probs[...] = shares.reshape(bins * rows, columns)
    copies = [pltpu.make_async_copy(probs, probs_out, done.at[0])]
    copies[0].start()
    plain_c[...] = context[...].astype(F32)
    one = lax.broadcasted_iota(jnp.int32, (columns, columns), 0)
    same = (one == lax.broadcasted_iota(jnp.int32, (columns, columns), 1)).astype(F32)
    same = same.astype(BF16)

    def turn(row, _):
        for k in range(columns // rows):
            column = columns - 1 - row * (columns // rows) - k
            cell = az_map[camera, column] - camera * sight + sight // 4
            cell = jnp.where(cell < 0, cell + around, cell)
            begins[jnp.where(cell >= around, cell - around, cell)] = column
        block = padded_rows(probs[pl.ds(row, bins, stride=rows), :], LANES)
        wide_p[pl.ds(row, columns, stride=rows), :] = jnp.transpose(block)
        block = padded_rows(plain_c[pl.ds(row, channels, stride=rows), :].astype(BF16), LANES)
        wide_c[pl.ds(row, columns, stride=rows), :] = product(same, block, 1, 1)
        return 0

    lax.fori_loop(0, rows, turn, 0, unroll=8)
    for wide, out in ((wide_p, probs_t_out), (wide_c, context_t_out)):
        wide[columns * rows :, :] = jnp.zeros((rows, LANES), F32)
        copies.append(pltpu.make_async_copy(wide, out, done.at[len(copies)]))
        copies[-1].start()
    line = lax.broadcasted_iota(jnp.int32, (TAPS * rows, LANES), 0)

    def cell_sum(cell):
        start = begins[cell]
        span = pl.ds(pl.multiple_of(start * rows, rows), TAPS * rows)
        width = (begins[cell + 1] - start) * rows
        features = jnp.where(line < width, wide_c[span, :], 0.0).astype(BF16)
        return product(features, wide_p[span, :].astype(BF16), 0, 0)[:channels].astype(BF16)

    near = band + 1 - 2 * (band % 2)
    for group, (mine, theirs) in enumerate(
        zip(sectors_of(band, bands), sectors_of(near, bands))
    ):

        def one_cell(step, _, group=group, mine=mine, theirs=theirs):
            sent[group * sector + step] = cell_sum(theirs * sector + step)
            kept[group * sector + step] = cell_sum(mine * sector + step)
            return 0

        lax.fori_loop(0, sector, one_cell, 0, unroll=4)
    for copy in copies:
        copy.wait()


def act_row(taps, source, start, out, row):
    hidden, length = out.shape[1:]
    stacked = jnp.concatenate([source[start + i] for i in range(TAPS)], axis=1)
    sums = product(taps, stacked, 1, 1)
    place = lax.broadcasted_iota(jnp.int32, (hidden, length), 1)
    ahead = pltpu.roll(sums[:hidden], length - 1, 1)
    behind = pltpu.roll(sums[2 * hidden :], 1, 1)
    total = sums[hidden : 2 * hidden]
    total = total + jnp.where(place < length - 1, ahead, 0.0)
    total = total + jnp.where(place > 0, behind, 0.0)
    out[row] = total.astype(BF16)


def act_taps_of(weight):
    hidden = weight.shape[3]
    return jnp.concatenate(
        [weight[TAPS - 1 - i].reshape(TAPS * hidden, hidden) for i in range(TAPS)], axis=1
    )


def inner_acts_kernel(upstream, weight, out):
    def step(row, _):
        act_row(act_taps_of(weight), upstream, row, out, row)
        return 0

    lax.fori_loop(0, out.shape[0], step, 0)


def outer_acts_kernel(place, near, far, upstream, weight, out, low, high):
    sector = upstream.shape[0]
    low[2:4] = upstream[0:2]
    high[0:2] = upstream[sector - 2 :]

    @pl.when(place[0] % 2 == 0)
    def _():
        low[0:2] = far[...]
        high[2:4] = near[...]

    @pl.when(place[0] % 2 == 1)
    def _():
        low[0:2] = near[...]
        high[2:4] = far[...]

    def step(row, _):
        act_row(act_taps_of(weight), low, row, out, row)
        act_row(act_taps_of(weight), high, row, out, row + 2)
        return 0

    lax.fori_loop(0, 2, step, 0)


def grid_kernel(
    place,
    own,
    edge,
    near_halo,
    far_halo,
    ranges,
    weight,
    inner_grad,
    outer_grad,
    upstream,
    keep,
    send,
    own_reply,
    other_reply,
    cells,
    grid_low,
    grid_taps,
    act_taps,
    slope_rows,
    slope_lanes,
    grid_grad,
    weight_t,
    range_hot,
    picks,
    grads,
    act_grads,
    sums_a,
    sums_b,
):
    sector, channels, lanes = own.shape
    hidden, length = outer_grad.shape[1:]
    bands = 4
    cameras, bins = ranges.shape
    position = place[0]
    mine, core = position % bands, position % 2
    camera = position // bands
    other = jnp.where(mine < bands // 2, camera + cameras - 1, camera + 1) % cameras
    wide = sector + 4
    cells[2 : 2 + sector, :, :lanes] = own[...]
    cells[:, :, lanes:] = jnp.zeros((wide, channels, lanes), BF16)

    @pl.when(mine == 0)
    def _():
        cells[0:2, :, :lanes] = edge[sector - 2 : sector]
        cells[2 + sector :, :, :lanes] = near_halo[0:2]
        cells[0 : sector + 2, :, lanes:] = far_halo[...]

    @pl.when(mine == 1)
    def _():
        cells[0:2, :, :lanes] = near_halo[0:2]
        cells[2 + sector :, :, :lanes] = far_halo[0:2]
        cells[0:2, :, lanes:] = near_halo[2:4]

    @pl.when(mine == bands - 2)
    def _():
        cells[0:2, :, :lanes] = far_halo[0:2]
        cells[2 + sector :, :, :lanes] = near_halo[0:2]
        cells[2 + sector :, :, lanes:] = near_halo[2:4]

    @pl.when(mine == bands - 1)
    def _():
        cells[0:2, :, :lanes] = near_halo[0:2]
        cells[2 + sector :, :, :lanes] = edge[0:2]
        cells[2:, :, lanes:] = far_halo[...]

    picks[...] = jnp.full(picks.shape, -1, jnp.int32)
    picks[0:1, 0:bins] = ranges[pl.ds(camera, 1), :]
    picks[0:1, lanes : lanes + bins] = ranges[pl.ds(other, 1), :]
    spots = lax.broadcasted_iota(jnp.int32, (length, 2 * lanes), 0)
    range_hot[...] = (spots == picks[0:1, :]).astype(F32).astype(BF16)
    for column in range(TAPS):
        for row in range(TAPS):
            weight_t[column * hidden : (column + 1) * hidden, row * channels : (row + 1) * channels] = (
                jnp.transpose(
                    weight[row, column * channels : (column + 1) * channels, :].astype(F32)
                ).astype(BF16)
            )

    def behind(value):
        turned = pltpu.roll(value, 1, 1)
        lane = lax.broadcasted_iota(jnp.int32, (value.shape[0], LANES), 1)
        first = jnp.where(lane > 0, turned[:, :LANES], 0.0)
        return jnp.concatenate([first, turned[:, LANES:]], axis=1)

    def ahead(value):
        turned = pltpu.roll(value, length - 1, 1)
        lane = lax.broadcasted_iota(jnp.int32, (value.shape[0], LANES), 1)
        last = jnp.where(lane < LANES - 1, turned[:, length - LANES :], 0.0)
        return jnp.concatenate([turned[:, : length - LANES], last], axis=1)

    for chunk in range(0, wide, 4):
        block = cells[chunk : chunk + 4].reshape(4 * channels, 2 * lanes)
        summed = product(block, range_hot[...], 1, 1)
        for row in range(chunk, chunk + 4):
            value = summed[(row - chunk) * channels : (row - chunk + 1) * channels]
            grid_low[row * channels : (row + 1) * channels, :] = value.astype(BF16)
            if 0 < row < wide - 1:
                spread = pl.ds((row - 1) * length, length)
                grid_taps[0:channels, spread] = behind(value).astype(BF16)
                grid_taps[channels : 2 * channels, spread] = value.astype(BF16)
                grid_taps[2 * channels :, spread] = ahead(value).astype(BF16)

    flipped = jnp.concatenate([weight[TAPS - 1 - i] for i in range(TAPS)], axis=1)

    def convolved(row, into):
        source = pl.ds(pl.multiple_of(row * channels, channels), TAPS * channels)
        into[...] = product(weight_t[...], grid_low[source, :], 1, 0)

    def back(row):
        source = pl.ds(pl.multiple_of(row * hidden, hidden), TAPS * hidden)
        sums = product(flipped, slope_rows[source, :], 1, 0)
        value = ahead(sums[:channels]) + sums[channels : 2 * channels]
        value = value + behind(sums[2 * channels :])
        grid_grad[pl.ds(pl.multiple_of(row * channels, channels), channels), :] = value.astype(BF16)

    def activated(row, sums):
        value = behind(sums[:hidden, :]) + sums[hidden : 2 * hidden, :]
        value = value + ahead(sums[2 * hidden :, :])
        logistic = 0.5 + 0.5 * jnp.tanh(0.5 * value)
        active = value * logistic
        start = pl.multiple_of(row * length, length)
        spread = pl.ds(start, length)
        low = active.astype(BF16)
        act_taps[0:hidden, spread] = pltpu.roll(low, 1, 1)
        act_taps[hidden : 2 * hidden, spread] = low
        act_taps[2 * hidden :, spread] = pltpu.roll(low, length - 1, 1)
        nothing = jnp.zeros((hidden, LANES), BF16)
        lane = lax.broadcasted_iota(jnp.int32, (hidden, LANES), 1)
        first = pl.ds(start, LANES)
        act_taps[0:hidden, first] = jnp.where(lane > 0, act_taps[0:hidden, first], nothing)
        last = pl.ds(pl.multiple_of(start + length - LANES, LANES), LANES)
        act_taps[2 * hidden :, last] = jnp.where(
            lane < LANES - 1, act_taps[2 * hidden :, last], nothing
        )
        slope = logistic * (1.0 + value * (1.0 - logistic))
        result = (act_grads[row].astype(F32) * slope).astype(BF16)
        slope_rows[pl.ds(pl.multiple_of(row * hidden, hidden), hidden), :] = result
        slope_lanes[:, spread] = result

    act_grads[0:2] = outer_grad[0:2]
    act_grads[2:sector] = inner_grad[...]
    act_grads[sector:] = outer_grad[2:4]
    rows = sector + 2
    slope_rows[0 : 3 * hidden, :] = jnp.zeros((3 * hidden, length), BF16)

    def two_rows(pair, _):
        row = 2 * pair
        back(jnp.maximum(row - 3, 0))
        convolved(row + 1, sums_b)
        activated(row, sums_a)
        back(jnp.maximum(row - 2, 0))
        convolved(jnp.minimum(row + 2, rows - 1), sums_a)
        activated(row + 1, sums_b)
        return 0

    convolved(0, sums_a)
    lax.fori_loop(0, rows // 2, two_rows, 0)
    back(sector - 1)
    count = sector * length
    tall = TAPS * hidden
    short = TAPS * channels

    def second(tap, _):
        window = pl.ds(pl.multiple_of(tap * length, length), count)
        result = product(act_taps[:, window], upstream[...], 1, 0)
        grads[pl.ds(pl.multiple_of(tap * tall, tall), tall), :] = result.astype(BF16)
        return 0

    lax.fori_loop(0, TAPS, second, 0)
    windows = [grid_taps[:, tap * length : tap * length + count] for tap in range(TAPS)]
    result = product(
        jnp.concatenate(windows, axis=0), slope_lanes[:, length : length + count], 1, 1
    )
    grads[TAPS * tall : TAPS * (tall + short), :] = result.astype(BF16)
    base = TAPS * (tall + short)
    grads[base:, :] = jnp.zeros((grads.shape[0] - base, hidden), BF16)
    half = keep.shape[0]
    keep[...] = grads[pl.ds(pl.multiple_of(core * half, half), half), :]
    send[...] = grads[pl.ds(pl.multiple_of((1 - core) * half, half), half), :]
    picked = product(grid_grad[...], range_hot[...], 1, 0).astype(BF16)
    own_reply[...] = picked[:, :lanes].reshape(sector, channels, lanes)
    other_reply[...] = picked[:, lanes:].reshape(sector, channels, lanes)


def finish_kernel(shifts, place, value, other, second, first, total):
    half = value.shape[0]
    size = half // 4
    position = place[0]
    core = position % 2
    for source, side in ((value, core), (other, 1 - core)):
        digit = jnp.where(side == 0, position >> shifts[0], position >> shifts[1]) & 3
        for mask in range(4):
            spot = side * half + (digit ^ mask) * size
            total[pl.ds(pl.multiple_of(spot, size), size), :] = source[
                mask * size : (mask + 1) * size, :
            ]
    count = second.shape[0]
    second[...] = total[0:count, :].astype(F32)
    first[...] = total[count : count + first.shape[0], :].astype(F32)


def lay_out(place, sector, mine, theirs, wedges):
    bands = 4
    band = place[0] % bands
    near = band + 1 - 2 * (band % 2)
    for group, spot in enumerate(sectors_of(band, bands)):
        wedges[pl.ds(spot * sector, sector)] = mine[group][...]
    for group, spot in enumerate(sectors_of(near, bands)):
        wedges[pl.ds(spot * sector, sector)] = theirs[group * sector : (group + 1) * sector]


def logit_kernel(
    rows,
    place,
    begins,
    own,
    partner,
    edge,
    theirs,
    probs,
    context_t,
    lidar,
    logit_grad,
    wedges,
    wide,
):
    columns = probs.shape[1]
    bins = probs.shape[0] // rows
    sector, channels, _ = own.shape
    lay_out(place, sector, (own, partner, edge), theirs, wedges)

    def one_cell(cell, _):
        span = pl.ds(pl.multiple_of(begins[cell] * rows, rows), TAPS * rows)
        features = context_t[span, :][:, :channels].astype(BF16)
        wide[span, :] = product(features, wedges[cell], 1, 0)
        return 0

    lax.fori_loop(0, wedges.shape[0], one_cell, 0, unroll=8)

    def turn(row, _):
        block = jnp.transpose(wide[pl.ds(row, columns, stride=rows), :])
        logit_grad[pl.ds(row, bins, stride=rows), :] = block[:bins]
        return 0

    lax.fori_loop(0, rows, turn, 0, unroll=4)
    share = probs[...].reshape(bins, rows, columns)
    slope = logit_grad[...].reshape(bins, rows, columns)
    expected = jnp.sum(share * slope, axis=0, keepdims=True)
    target = lidar[...][None]
    seen = jnp.where(target >= 0, DEPTH_WEIGHT, 0.0)
    level = lax.broadcasted_iota(jnp.int32, share.shape, 0)
    hit = jnp.where(level == target, DEPTH_WEIGHT, 0.0)
    result = share * (slope - expected) + (seen * share - hit)
    logit_grad[...] = result.reshape(bins * rows, columns)


def context_kernel(
    rows,
    place,
    begins,
    own,
    partner,
    edge,
    theirs,
    probs_t,
    context_grad,
    wedges,
    wide,
    plain,
):
    columns = context_grad.shape[1]
    sector, channels, _ = own.shape
    lay_out(place, sector, (own, partner, edge), theirs, wedges)
    wide[...] = jnp.zeros_like(wide)

    def one_cell(cell, _):
        span = pl.ds(pl.multiple_of(begins[cell] * rows, rows), TAPS * rows)
        shares = probs_t[span, :].astype(BF16)
        wide[span, 0:channels] = product(shares, wedges[cell], 1, 1)
        return 0

    lax.fori_loop(0, wedges.shape[0], one_cell, 0, unroll=8)

    def turn(row, _):
        block = jnp.transpose(wide[pl.ds(row, columns, stride=rows), :])
        plain[pl.ds(row, channels, stride=rows), :] = block[:channels]
        return 0

    lax.fori_loop(0, rows, turn, 0, unroll=4)
    context_grad[...] = plain[...].astype(BF16)


def vmem():
    return pl.BlockSpec(memory_space=pltpu.VMEM)


def smem():
    return pl.BlockSpec(memory_space=pltpu.SMEM)


def anywhere():
    return pl.BlockSpec(memory_space=pltpu.HBM)


def call(kernel, out_shape, scratch, spaces, flops, moved, outs=None, limit=16):
    many = isinstance(out_shape, (list, tuple))
    return pl.pallas_call(
        kernel,
        out_shape=out_shape,
        in_specs=spaces,
        out_specs=outs or ([vmem() for _ in out_shape] if many else vmem()),
        scratch_shapes=scratch,
        compiler_params=pltpu.CompilerParams(vmem_limit_bytes=limit * 1024 * 1024),
        cost_estimate=pl.CostEstimate(flops=flops, bytes_accessed=moved, transcendentals=0),
    )


def rounded_sum(left, right):
    return (left.astype(F32) + right.astype(F32)).astype(BF16)


def swapped(value, blocks, mask):
    return lax.ppermute(value, "blk", [(i, i ^ mask) for i in range(blocks)])


def piece(value, index, count):
    size = value.shape[0] // count
    return lax.dynamic_slice_in_dim(value, index * size, size, 0)


def axis_orders(count):
    pairs = list(range(1, count, 2))
    return pairs, pairs[1:] + pairs[:1]


def total_over_blocks(keep, send, position, blocks):
    count = blocks.bit_length() - 1
    orders = axis_orders(count)
    core = position & 1
    digits = [
        jnp.where(core == 0, position >> one, position >> two) & 3 for one, two in zip(*orders)
    ]

    def sent(part, step, mask):
        to = [(i, i ^ (mask << orders[i & 1][step])) for i in range(blocks)]
        return lax.ppermute(part, "blk", to)

    value = rounded_sum(keep, swapped(send, blocks, 1))
    for step, digit in enumerate(digits):
        leaving = [piece(value, digit ^ mask, 4) for mask in (3, 1, 2)]
        arrived = [sent(part, step, mask) for part, mask in zip(leaving, (3, 1, 2))]
        total = piece(value, digit, 4).astype(F32)
        for part in arrived:
            total = total + part.astype(F32)
        value = total.astype(BF16)
    for step, digit in reversed(list(enumerate(digits))):
        held = [value] + [sent(value, step, mask) for mask in (1, 2, 3)]
        if step == 0:
            value = jnp.concatenate(held, axis=0)
            break
        high, low = digit >> 1 == 1, digit & 1 == 1

        def at(k):
            one = jnp.where(low, held[k ^ 1], held[k])
            two = jnp.where(low, held[k ^ 3], held[k ^ 2])
            return jnp.where(high, two, one)

        value = jnp.concatenate([at(k) for k in range(4)], axis=0)
    return value, swapped(value, blocks, 1)


def shards(
    depth_logits, context, lidar_bins, az_map, rng_map, conv1_weight, conv2_weight, out_grad
):
    blocks = lax.axis_size("blk")
    position = lax.axis_index("blk")
    cameras, columns = az_map.shape
    bands = blocks // cameras
    sector, length, hidden = out_grad.shape
    bins, rows = depth_logits.shape[1:3]
    channels = context.shape[1]
    if bands != 4 or blocks != 1 << (blocks.bit_length() - 1) or blocks.bit_length() % 2 or bins > LANES or channels > LANES or sector < 6 or sector % 2:
        raise ValueError("unsupported sizes")
    band = position % bands
    sight = bands * sector
    seen = sight + sight // 2

    core = position & 1
    place = position.reshape(1)
    on_chip = [(i, i ^ 1) for i in range(blocks)]
    off_chip = [(i, (i + 1 if i & 1 else i - 1) % blocks) for i in range(blocks)]

    def ends(value, near):
        return jnp.where((core == 0) == near, value[-2:], value[:2])

    far_grad = lax.ppermute(ends(out_grad, False), "blk", off_chip)
    near_grad = lax.ppermute(ends(out_grad, True), "blk", on_chip)

    turned = (columns + 1) * rows
    half = 3 * sector
    probs, probs_t, context_t, kept, sent, begins = call(
        functools.partial(pool_kernel, rows, sight, blocks * sector),
        [
            jax.ShapeDtypeStruct((bins * rows, columns), F32),
            jax.ShapeDtypeStruct((turned, LANES), F32),
            jax.ShapeDtypeStruct((turned, LANES), F32),
            jax.ShapeDtypeStruct((half, channels, LANES), BF16),
            jax.ShapeDtypeStruct((half, channels, LANES), BF16),
            jax.ShapeDtypeStruct((seen + 1,), jnp.int32),
        ],
        [
            pltpu.VMEM((bins * rows, columns), F32),
            pltpu.VMEM((turned, LANES), F32),
            pltpu.VMEM((turned, LANES), F32),
            pltpu.VMEM((channels * rows, columns), F32),
            pltpu.SemaphoreType.DMA((3,)),
        ],
        [smem(), smem(), vmem(), vmem()],
        2 * seen * 3 * rows * LANES * LANES,
        20 * bins * rows * columns,
        [anywhere()] * 3 + [vmem()] * 2 + [smem()],
        limit=56,
    )(
        place,
        az_map,
        depth_logits[0].reshape(bins * rows, columns),
        context[0].reshape(channels * rows, columns),
    )

    row_flops = 2 * TAPS * TAPS * hidden * hidden * length

    inner_grad = call(
        inner_acts_kernel,
        jax.ShapeDtypeStruct((sector - 2, hidden, length), BF16),
        [],
        [vmem()] * 2,
        row_flops * (sector - 2),
        4 * sector * length * hidden,
    )(out_grad, conv2_weight)
    outer_grad = call(
        outer_acts_kernel,
        jax.ShapeDtypeStruct((4, hidden, length), BF16),
        [pltpu.VMEM((4, length, hidden), BF16)] * 2,
        [smem()] + [vmem()] * 4,
        row_flops * 4,
        16 * length * hidden,
    )(place, near_grad, far_grad, out_grad, conv2_weight)

    summed = rounded_sum(kept, swapped(sent, blocks, 1))
    own = rounded_sum(summed[:sector], swapped(summed[sector : 2 * sector], blocks, 2))
    inward = [(i, i ^ 2) for i in range(blocks) if i % bands in (1, 2)]
    outward = [(i ^ 2, i) for i in range(blocks) if i % bands in (1, 2)]
    edge = rounded_sum(
        summed[2 * sector :], lax.ppermute(summed[2 * sector :], "blk", inward)
    )
    first = band == 0
    firsts = [i for i in range(blocks) if i % bands == 0]
    lasts = [i for i in range(blocks) if i % bands == bands - 1]
    last = band == bands - 1
    outer = jnp.logical_or(first, last)
    more = ((0, sector), (0, 0), (0, 0))
    far = jnp.where(
        first,
        jnp.concatenate([edge, own[:2]], axis=0),
        jnp.where(
            last,
            jnp.concatenate([own[sector - 2 :], edge], axis=0),
            jnp.pad(ends(own, False), more),
        ),
    )

    def to_next(value):
        pairs = [(i, (i - 1) % blocks) for i in firsts]
        pairs = pairs + [(i, (i + 1) % blocks) for i in lasts]
        return lax.ppermute(value, "blk", pairs)

    far_halo = lax.ppermute(far, "blk", off_chip)
    passed = jnp.where(first, far_halo[sector:], far_halo[:2])
    near_halo = lax.ppermute(
        jnp.concatenate([ends(own, True), passed], axis=0), "blk", on_chip
    )
    weight = conv1_weight.reshape(TAPS, TAPS * channels, hidden)
    grad_rows = TAPS * TAPS * (hidden + channels)
    unit = blocks * 16
    grad_rows = -(-grad_rows // unit) * unit
    wide = sector + 2
    keep, send, own_reply, other_reply = call(
        grid_kernel,
        [
            jax.ShapeDtypeStruct((grad_rows // 2, hidden), BF16),
            jax.ShapeDtypeStruct((grad_rows // 2, hidden), BF16),
            jax.ShapeDtypeStruct((sector, channels, LANES), BF16),
            jax.ShapeDtypeStruct((sector, channels, LANES), BF16),
        ],
        [
            pltpu.VMEM((sector + 4, channels, 2 * LANES), BF16),
            pltpu.VMEM(((sector + 4) * channels, length), BF16),
            pltpu.VMEM((TAPS * channels, wide * length), BF16),
            pltpu.VMEM((TAPS * hidden, wide * length), BF16),
            pltpu.VMEM((wide * hidden, length), BF16),
            pltpu.VMEM((hidden, wide * length), BF16),
            pltpu.VMEM((sector * channels, length), BF16),
            pltpu.VMEM((TAPS * hidden, TAPS * channels), BF16),
            pltpu.VMEM((length, 2 * LANES), BF16),
            pltpu.VMEM((8, 2 * LANES), jnp.int32),
            pltpu.VMEM((grad_rows, hidden), BF16),
            pltpu.VMEM((wide, hidden, length), BF16),
            pltpu.VMEM((TAPS * hidden, length), F32),
            pltpu.VMEM((TAPS * hidden, length), F32),
        ],
        [smem()] + [vmem()] * 9,
        row_flops * (sector + 3 * sector // 2),
        20 * sector * length * hidden,
        limit=34,
    )(
        place,
        own,
        edge,
        near_halo,
        far_halo,
        rng_map,
        weight,
        inner_grad,
        outer_grad,
        out_grad.reshape(sector * length, hidden),
    )

    partner = swapped(own_reply, blocks, 2)
    edge_reply = to_next(other_reply)
    passed = lax.ppermute(edge_reply, "blk", outward)
    edge_reply = jnp.where(outer, edge_reply, passed)
    theirs = swapped(
        jnp.concatenate([own_reply, partner, edge_reply], axis=0), blocks, 1
    )
    value, other_value = total_over_blocks(keep, send, position, blocks)

    replies = (own_reply, partner, edge_reply, theirs)
    scratch = [pltpu.VMEM((seen, channels, LANES), BF16), pltpu.VMEM((turned, LANES), F32)]
    cell_flops = 2 * seen * 3 * rows * LANES * LANES
    context_grad = call(
        functools.partial(context_kernel, rows),
        jax.ShapeDtypeStruct((channels * rows, columns), BF16),
        scratch + [pltpu.VMEM((channels * rows, columns), F32)],
        [smem()] * 2 + [vmem()] * 5,
        cell_flops,
        10 * bins * rows * columns,
    )(place, begins, *replies, probs_t)
    logit_grad = call(
        functools.partial(logit_kernel, rows),
        jax.ShapeDtypeStruct((bins * rows, columns), F32),
        scratch,
        [smem()] * 2 + [vmem()] * 7,
        cell_flops,
        20 * bins * rows * columns,
    )(place, begins, *replies, probs, context_t, lidar_bins[0])

    second = TAPS * TAPS * hidden
    first_rows = TAPS * TAPS * channels
    second_grad, first_grad = call(
        functools.partial(
            finish_kernel, [order[0] for order in axis_orders(blocks.bit_length() - 1)]
        ),
        [
            jax.ShapeDtypeStruct((second, hidden), F32),
            jax.ShapeDtypeStruct((first_rows, hidden), F32),
        ],
        [pltpu.VMEM((grad_rows, hidden), BF16)],
        [smem(), vmem(), vmem()],
        1,
        6 * grad_rows * hidden,
    )(place, value, other_value)
    return (
        logit_grad.reshape(1, bins, rows, columns),
        context_grad.reshape(1, channels, rows, columns),
        first_grad.reshape(TAPS, TAPS, channels, hidden),
        second_grad.reshape(TAPS, TAPS, hidden, hidden),
    )


def solution(mesh):
    return jax.shard_map(
        shards,
        mesh=mesh,
        in_specs=(
            P(("group", "blk"), None, None, None),
            P(("group", "blk"), None, None, None),
            P(("group", "blk"), None, None),
            P(),
            P(),
            P(),
            P(),
            P(("group", "blk"), None, None),
        ),
        out_specs=(
            P(("group", "blk"), None, None, None),
            P(("group", "blk"), None, None, None),
            P("group", None, None, None),
            P("group", None, None, None),
        ),
        check_vma=False,
    )
```

```python
import functools

import jax
import jax.numpy as jnp
from jax import lax
from jax.experimental import pallas as pl
from jax.experimental.pallas import tpu as pltpu
from jax.sharding import PartitionSpec as P

DEPTH_WEIGHT = 3.0
TAPS = 3
LANES = 128
SLACK = 8
F32 = jnp.float32
BF16 = jnp.bfloat16


def product(left, right, left_dim, right_dim):
    return lax.dot_general(
        left, right, (((left_dim,), (right_dim,)), ((), ())), preferred_element_type=F32
    )


def padded_rows(value, rows):
    missing = rows - value.shape[0]
    if missing == 0:
        return value
    return jnp.concatenate([value, jnp.zeros((missing, value.shape[1]), value.dtype)], axis=0)


def sectors_of(band, bands):
    partner = (band + 2) % bands
    return 1 + band, 1 + partner, (bands + 1) * (band % 2)


def pool_kernel(
    rows,
    sight,
    around,
    place,
    az_map,
    logits,
    context,
    probs_out,
    probs_t_out,
    context_t_out,
    kept,
    sent,
    begins,
    probs,
    apart_p,
    apart_c,
    wide_p,
    wide_c,
    done,
):
    columns = logits.shape[1]
    bins = logits.shape[0] // rows
    channels = context.shape[0] // rows
    half = kept.shape[0]
    sector = half // 3
    bands = 4
    position = place[0]
    band, camera = position % bands, position // bands
    seen = 2 * half
    begins[seen] = columns
    scores = logits[...].reshape(bins, rows, columns)
    powers = jnp.exp(scores - jnp.max(scores, axis=0, keepdims=True))
    shares = powers / jnp.sum(powers, axis=0, keepdims=True)
    probs[...] = shares.reshape(bins * rows, columns)
    copies = [pltpu.make_async_copy(probs, probs_out, done.at[0])]
    copies[0].start()
    pitch = rows + SLACK
    for level in range(bins):
        apart_p[level * pitch : level * pitch + rows, :] = shares[level]
    for level in range(channels):
        features = context[level * rows : (level + 1) * rows, :]
        apart_c[level * pitch : level * pitch + rows, :] = features.astype(F32)
    one = lax.broadcasted_iota(jnp.int32, (columns, columns), 0)
    same = (one == lax.broadcasted_iota(jnp.int32, (columns, columns), 1)).astype(F32)
    same = same.astype(BF16)

    def turn(row, _):
        for k in range(columns // rows):
            column = columns - 1 - row * (columns // rows) - k
            cell = az_map[camera, column] - camera * sight + sight // 4
            cell = jnp.where(cell < 0, cell + around, cell)
            begins[jnp.where(cell >= around, cell - around, cell)] = column
        block = padded_rows(apart_p[pl.ds(row, bins, stride=pitch), :], LANES)
        wide_p[pl.ds(row, columns, stride=pitch), :] = jnp.transpose(block)
        block = padded_rows(apart_c[pl.ds(row, channels, stride=pitch), :].astype(BF16), LANES)
        wide_c[pl.ds(row, columns, stride=pitch), :] = product(same, block, 1, 1)
        return 0

    lax.fori_loop(0, rows, turn, 0, unroll=8)
    for wide, out in ((wide_p, probs_t_out), (wide_c, context_t_out)):
        wide[columns * pitch :, :] = jnp.zeros((pitch, LANES), F32)
        source = wide.reshape(columns + 1, pitch, LANES).at[:, 0:rows, :]
        copies.append(pltpu.make_async_copy(source, out, done.at[len(copies)]))
        copies[-1].start()
    line = lax.broadcasted_iota(jnp.int32, (TAPS * rows, LANES), 0)

    def cell_sum(cell):
        start = begins[cell]
        spans = [pl.ds(pl.multiple_of((start + k) * pitch, 8), rows) for k in range(TAPS)]
        features = jnp.concatenate([wide_c[span, :] for span in spans], axis=0)
        shares = jnp.concatenate([wide_p[span, :] for span in spans], axis=0)
        width = (begins[cell + 1] - start) * rows
        features = jnp.where(line < width, features, 0.0).astype(BF16)
        return product(features, shares.astype(BF16), 0, 0)[:channels].astype(BF16)

    near = band + 1 - 2 * (band % 2)
    for group, (mine, theirs) in enumerate(
        zip(sectors_of(band, bands), sectors_of(near, bands))
    ):

        def one_cell(step, _, group=group, mine=mine, theirs=theirs):
            sent[group * sector + step] = cell_sum(theirs * sector + step)
            kept[group * sector + step] = cell_sum(mine * sector + step)
            return 0

        lax.fori_loop(0, sector, one_cell, 0, unroll=4)
    for copy in copies:
        copy.wait()


def act_row(taps, source, start, out, row):
    hidden, length = out.shape[1:]
    stacked = jnp.concatenate([source[start + i] for i in range(TAPS)], axis=1)
    sums = product(taps, stacked, 1, 1)
    place = lax.broadcasted_iota(jnp.int32, (hidden, length), 1)
    ahead = pltpu.roll(sums[:hidden], length - 1, 1)
    behind = pltpu.roll(sums[2 * hidden :], 1, 1)
    total = sums[hidden : 2 * hidden]
    total = total + jnp.where(place < length - 1, ahead, 0.0)
    total = total + jnp.where(place > 0, behind, 0.0)
    out[row] = total.astype(BF16)


def act_taps_of(weight):
    hidden = weight.shape[3]
    return jnp.concatenate(
        [weight[TAPS - 1 - i].reshape(TAPS * hidden, hidden) for i in range(TAPS)], axis=1
    )


def inner_acts_kernel(upstream, weight, out):
    def step(row, _):
        act_row(act_taps_of(weight), upstream, row, out, row)
        return 0

    lax.fori_loop(0, out.shape[0], step, 0)


def outer_acts_kernel(
    place,
    near,
    far,
    upstream,
    weight,
    inner,
    first_weight,
    ranges,
    out,
    weight_t,
    range_hot,
    low,
    high,
    picks,
):
    sector, length, hidden = upstream.shape
    bands = 4
    cameras, bins = ranges.shape
    channels = first_weight.shape[1] // TAPS
    lanes = range_hot.shape[1] // 2
    mine, camera = place[0] % bands, place[0] // bands
    other = jnp.where(mine < bands // 2, camera + cameras - 1, camera + 1) % cameras
    picks[...] = jnp.full(picks.shape, -1, jnp.int32)
    picks[0:1, 0:bins] = ranges[pl.ds(camera, 1), :]
    picks[0:1, lanes : lanes + bins] = ranges[pl.ds(other, 1), :]
    spots = lax.broadcasted_iota(jnp.int32, (length, 2 * lanes), 0)
    range_hot[...] = (spots == picks[0:1, :]).astype(F32).astype(BF16)
    for column in range(TAPS):
        for row in range(TAPS):
            weight_t[column * hidden : (column + 1) * hidden, row * channels : (row + 1) * channels] = (
                jnp.transpose(
                    first_weight[row, column * channels : (column + 1) * channels, :].astype(F32)
                ).astype(BF16)
            )
    out[2:sector] = inner[...]
    low[2:4] = upstream[0:2]
    high[0:2] = upstream[sector - 2 :]

    @pl.when(place[0] % 2 == 0)
    def _():
        low[0:2] = far[...]
        high[2:4] = near[...]

    @pl.when(place[0] % 2 == 1)
    def _():
        low[0:2] = near[...]
        high[2:4] = far[...]

    def step(row, _):
        act_row(act_taps_of(weight), low, row, out, row)
        act_row(act_taps_of(weight), high, row, out, row + sector)
        return 0

    lax.fori_loop(0, 2, step, 0)


def grid_kernel(
    place,
    own,
    edge,
    near_halo,
    far_halo,
    weight,
    weight_t,
    range_hot,
    act_grads,
    upstream,
    keep,
    send,
    own_reply,
    other_reply,
    cells,
    grid_low,
    grid_taps,
    act_taps,
    slope_rows,
    slope_lanes,
    grid_grad,
    grads,
    sums_a,
    sums_b,
):
    sector, channels, lanes = own.shape
    hidden, length = act_grads.shape[1:]
    bands = 4
    position = place[0]
    mine, core = position % bands, position % 2
    wide = sector + 4
    cells[2 : 2 + sector, :, :lanes] = own[...]
    cells[:, :, lanes:] = jnp.zeros((wide, channels, lanes), BF16)

    @pl.when(mine == 0)
    def _():
        cells[0:2, :, :lanes] = edge[sector - 2 : sector]
        cells[2 + sector :, :, :lanes] = near_halo[0:2]
        cells[0 : sector + 2, :, lanes:] = far_halo[...]

    @pl.when(mine == 1)
    def _():
        cells[0:2, :, :lanes] = near_halo[0:2]
        cells[2 + sector :, :, :lanes] = far_halo[0:2]
        cells[0:2, :, lanes:] = near_halo[2:4]

    @pl.when(mine == bands - 2)
    def _():
        cells[0:2, :, :lanes] = far_halo[0:2]
        cells[2 + sector :, :, :lanes] = near_halo[0:2]
        cells[2 + sector :, :, lanes:] = near_halo[2:4]

    @pl.when(mine == bands - 1)
    def _():
        cells[0:2, :, :lanes] = near_halo[0:2]
        cells[2 + sector :, :, :lanes] = edge[0:2]
        cells[2:, :, lanes:] = far_halo[...]

    def behind(value):
        turned = pltpu.roll(value, 1, 1)
        lane = lax.broadcasted_iota(jnp.int32, (value.shape[0], LANES), 1)
        first = jnp.where(lane > 0, turned[:, :LANES], 0.0)
        return jnp.concatenate([first, turned[:, LANES:]], axis=1)

    def ahead(value):
        turned = pltpu.roll(value, length - 1, 1)
        lane = lax.broadcasted_iota(jnp.int32, (value.shape[0], LANES), 1)
        last = jnp.where(lane < LANES - 1, turned[:, length - LANES :], 0.0)
        return jnp.concatenate([turned[:, : length - LANES], last], axis=1)

    for chunk in range(0, wide, 4):
        block = cells[chunk : chunk + 4].reshape(4 * channels, 2 * lanes)
        summed = product(block, range_hot[...], 1, 1)
        for row in range(chunk, chunk + 4):
            value = summed[(row - chunk) * channels : (row - chunk + 1) * channels]
            grid_low[row * channels : (row + 1) * channels, :] = value.astype(BF16)
            if 0 < row < wide - 1:
                spread = pl.ds((row - 1) * length, length)
                grid_taps[0:channels, spread] = behind(value).astype(BF16)
                grid_taps[channels : 2 * channels, spread] = value.astype(BF16)
                grid_taps[2 * channels :, spread] = ahead(value).astype(BF16)

    flipped = jnp.concatenate([weight[TAPS - 1 - i] for i in range(TAPS)], axis=1)

    def convolved(row, into):
        source = pl.ds(pl.multiple_of(row * channels, channels), TAPS * channels)
        into[...] = product(weight_t[...], grid_low[source, :], 1, 0)

    def back(row):
        source = pl.ds(pl.multiple_of(row * hidden, hidden), TAPS * hidden)
        sums = product(flipped, slope_rows[source, :], 1, 0)
        value = ahead(sums[:channels]) + sums[channels : 2 * channels]
        value = value + behind(sums[2 * channels :])
        grid_grad[pl.ds(pl.multiple_of(row * channels, channels), channels), :] = value.astype(BF16)

    def activated(row, sums):
        value = behind(sums[:hidden, :]) + sums[hidden : 2 * hidden, :]
        value = value + ahead(sums[2 * hidden :, :])
        logistic = 0.5 + 0.5 * jnp.tanh(0.5 * value)
        active = value * logistic
        start = pl.multiple_of(row * length, length)
        spread = pl.ds(start, length)
        low = active.astype(BF16)
        act_taps[0:hidden, spread] = pltpu.roll(low, 1, 1)
        act_taps[hidden : 2 * hidden, spread] = low
        act_taps[2 * hidden :, spread] = pltpu.roll(low, length - 1, 1)
        nothing = jnp.zeros((hidden, LANES), BF16)
        lane = lax.broadcasted_iota(jnp.int32, (hidden, LANES), 1)
        first = pl.ds(start, LANES)
        act_taps[0:hidden, first] = jnp.where(lane > 0, act_taps[0:hidden, first], nothing)
        last = pl.ds(pl.multiple_of(start + length - LANES, LANES), LANES)
        act_taps[2 * hidden :, last] = jnp.where(
            lane < LANES - 1, act_taps[2 * hidden :, last], nothing
        )
        slope = logistic * (1.0 + value * (1.0 - logistic))
        result = (act_grads[row].astype(F32) * slope).astype(BF16)
        slope_rows[pl.ds(pl.multiple_of(row * hidden, hidden), hidden), :] = result
        slope_lanes[:, spread] = result

    rows = sector + 2
    slope_rows[0 : 3 * hidden, :] = jnp.zeros((3 * hidden, length), BF16)

    def two_rows(pair, _):
        row = 2 * pair
        back(jnp.maximum(row - 3, 0))
        convolved(row + 1, sums_b)
        activated(row, sums_a)
        back(jnp.maximum(row - 2, 0))
        convolved(jnp.minimum(row + 2, rows - 1), sums_a)
        activated(row + 1, sums_b)
        return 0

    convolved(0, sums_a)
    lax.fori_loop(0, rows // 2, two_rows, 0)
    back(sector - 1)
    count = sector * length
    tall = TAPS * hidden
    short = TAPS * channels

    def second(tap, _):
        window = pl.ds(pl.multiple_of(tap * length, length), count)
        result = product(act_taps[:, window], upstream[...], 1, 0)
        grads[pl.ds(pl.multiple_of(tap * tall, tall), tall), :] = result.astype(BF16)
        return 0

    lax.fori_loop(0, TAPS, second, 0)
    windows = [grid_taps[:, tap * length : tap * length + count] for tap in range(TAPS)]
    result = product(
        jnp.concatenate(windows, axis=0), slope_lanes[:, length : length + count], 1, 1
    )
    grads[TAPS * tall : TAPS * (tall + short), :] = result.astype(BF16)
    base = TAPS * (tall + short)
    grads[base:, :] = jnp.zeros((grads.shape[0] - base, hidden), BF16)
    half = keep.shape[0]
    keep[...] = grads[pl.ds(pl.multiple_of(core * half, half), half), :]
    send[...] = grads[pl.ds(pl.multiple_of((1 - core) * half, half), half), :]
    picked = product(grid_grad[...], range_hot[...], 1, 0).astype(BF16)
    own_reply[...] = picked[:, :lanes].reshape(sector, channels, lanes)
    other_reply[...] = picked[:, lanes:].reshape(sector, channels, lanes)


def finish_kernel(shifts, place, value, other, second, first, total):
    half = value.shape[0]
    size = half // 4
    position = place[0]
    core = position % 2
    for source, side in ((value, core), (other, 1 - core)):
        digit = jnp.where(side == 0, position >> shifts[0], position >> shifts[1]) & 3
        for mask in range(4):
            spot = side * half + (digit ^ mask) * size
            total[pl.ds(pl.multiple_of(spot, size), size), :] = source[
                mask * size : (mask + 1) * size, :
            ]
    count = second.shape[0]
    second[...] = total[0:count, :].astype(F32)
    first[...] = total[count : count + first.shape[0], :].astype(F32)


def lay_out(place, sector, mine, theirs, wedges):
    bands = 4
    band = place[0] % bands
    near = band + 1 - 2 * (band % 2)
    for group, spot in enumerate(sectors_of(band, bands)):
        wedges[pl.ds(spot * sector, sector)] = mine[group][...]
    for group, spot in enumerate(sectors_of(near, bands)):
        wedges[pl.ds(spot * sector, sector)] = theirs[group * sector : (group + 1) * sector]


def logit_kernel(
    rows,
    place,
    begins,
    own,
    partner,
    edge,
    theirs,
    probs,
    context_t,
    lidar,
    logit_grad,
    wedges,
    wide,
    apart,
):
    columns = probs.shape[1]
    bins = probs.shape[0] // rows
    sector, channels, _ = own.shape
    lay_out(place, sector, (own, partner, edge), theirs, wedges)

    pitch = rows + SLACK

    def one_cell(cell, _):
        start = begins[cell]
        features = context_t[pl.ds(start, TAPS)].reshape(TAPS * rows, LANES)
        result = product(features[:, :channels].astype(BF16), wedges[cell], 1, 0)
        for k in range(TAPS):
            span = pl.ds(pl.multiple_of((start + k) * pitch, 8), rows)
            wide[span, :] = result[k * rows : (k + 1) * rows]
        return 0

    lax.fori_loop(0, wedges.shape[0], one_cell, 0, unroll=8)

    def turn(row, _):
        block = jnp.transpose(wide[pl.ds(row, columns, stride=pitch), :])
        apart[pl.ds(row, bins, stride=pitch), :] = block[:bins]
        return 0

    lax.fori_loop(0, rows, turn, 0, unroll=8)
    sums = [jnp.zeros((rows, columns), F32) for _ in range(4)]
    for level in range(bins):
        share = probs[level * rows : (level + 1) * rows, :]
        sums[level % 4] += share * apart[level * pitch : level * pitch + rows, :]
    expected = (sums[0] + sums[1]) + (sums[2] + sums[3])
    target = lidar[...]
    seen = jnp.where(target >= 0, DEPTH_WEIGHT, 0.0)
    for level in range(bins):
        share = probs[level * rows : (level + 1) * rows, :]
        slope = apart[level * pitch : level * pitch + rows, :]
        hit = jnp.where(target == level, DEPTH_WEIGHT, 0.0)
        result = share * (slope - expected) + (seen * share - hit)
        logit_grad[level * rows : (level + 1) * rows, :] = result


def context_kernel(
    rows,
    place,
    begins,
    own,
    partner,
    edge,
    theirs,
    probs_t,
    context_grad,
    wedges,
    wide,
    apart,
):
    columns = context_grad.shape[1]
    sector, channels, _ = own.shape
    lay_out(place, sector, (own, partner, edge), theirs, wedges)

    pitch = rows + SLACK

    def one_cell(cell, _):
        start = begins[cell]
        shares = probs_t[pl.ds(start, TAPS)].reshape(TAPS * rows, LANES)
        result = product(shares.astype(BF16), wedges[cell], 1, 1)
        for k in range(TAPS):
            span = pl.ds(pl.multiple_of((start + k) * pitch, 8), rows)
            wide[span, 0:channels] = result[k * rows : (k + 1) * rows]
        return 0

    lax.fori_loop(0, wedges.shape[0], one_cell, 0, unroll=8)
    one = lax.broadcasted_iota(jnp.int32, (channels, channels), 0)
    same = (one == lax.broadcasted_iota(jnp.int32, (channels, channels), 1)).astype(F32)
    same = same.astype(BF16)

    def turn(row, _):
        block = wide[pl.ds(row, columns, stride=pitch), :][:, :channels].astype(BF16)
        apart[pl.ds(row, channels, stride=pitch), :] = product(same, block, 1, 1)
        return 0

    lax.fori_loop(0, rows, turn, 0, unroll=8)
    for level in range(channels):
        block = apart[level * pitch : level * pitch + rows, :]
        context_grad[level * rows : (level + 1) * rows, :] = block.astype(BF16)


def vmem():
    return pl.BlockSpec(memory_space=pltpu.VMEM)


def smem():
    return pl.BlockSpec(memory_space=pltpu.SMEM)


def anywhere():
    return pl.BlockSpec(memory_space=pltpu.HBM)


def call(kernel, out_shape, scratch, spaces, flops, moved, outs=None, limit=16):
    many = isinstance(out_shape, (list, tuple))
    return pl.pallas_call(
        kernel,
        out_shape=out_shape,
        in_specs=spaces,
        out_specs=outs or ([vmem() for _ in out_shape] if many else vmem()),
        scratch_shapes=scratch,
        compiler_params=pltpu.CompilerParams(vmem_limit_bytes=limit * 1024 * 1024),
        cost_estimate=pl.CostEstimate(flops=flops, bytes_accessed=moved, transcendentals=0),
    )


def rounded_sum(left, right):
    return (left.astype(F32) + right.astype(F32)).astype(BF16)


def swapped(value, blocks, mask):
    return lax.ppermute(value, "blk", [(i, i ^ mask) for i in range(blocks)])


def piece(value, index, count):
    size = value.shape[0] // count
    return lax.dynamic_slice_in_dim(value, index * size, size, 0)


def axis_orders(count):
    pairs = list(range(1, count, 2))
    return pairs, pairs[1:] + pairs[:1]


def total_over_blocks(keep, send, position, blocks):
    count = blocks.bit_length() - 1
    orders = axis_orders(count)
    core = position & 1
    digits = [
        jnp.where(core == 0, position >> one, position >> two) & 3 for one, two in zip(*orders)
    ]

    def sent(part, step, mask):
        to = [(i, i ^ (mask << orders[i & 1][step])) for i in range(blocks)]
        return lax.ppermute(part, "blk", to)

    value = rounded_sum(keep, swapped(send, blocks, 1))
    for step, digit in enumerate(digits):
        leaving = [piece(value, digit ^ mask, 4) for mask in (3, 1, 2)]
        arrived = [sent(part, step, mask) for part, mask in zip(leaving, (3, 1, 2))]
        total = piece(value, digit, 4).astype(F32)
        for part in arrived:
            total = total + part.astype(F32)
        value = total.astype(BF16)
    for step, digit in reversed(list(enumerate(digits))):
        held = [value] + [sent(value, step, mask) for mask in (1, 2, 3)]
        if step == 0:
            value = jnp.concatenate(held, axis=0)
            break
        high, low = digit >> 1 == 1, digit & 1 == 1

        def at(k):
            one = jnp.where(low, held[k ^ 1], held[k])
            two = jnp.where(low, held[k ^ 3], held[k ^ 2])
            return jnp.where(high, two, one)

        value = jnp.concatenate([at(k) for k in range(4)], axis=0)
    return value, swapped(value, blocks, 1)


def shards(
    depth_logits, context, lidar_bins, az_map, rng_map, conv1_weight, conv2_weight, out_grad
):
    blocks = lax.axis_size("blk")
    position = lax.axis_index("blk")
    cameras, columns = az_map.shape
    bands = blocks // cameras
    sector, length, hidden = out_grad.shape
    bins, rows = depth_logits.shape[1:3]
    channels = context.shape[1]
    if bands != 4 or blocks != 1 << (blocks.bit_length() - 1) or blocks.bit_length() % 2 or bins > LANES or channels > LANES or sector < 6 or sector % 2:
        raise ValueError("unsupported sizes")
    band = position % bands
    sight = bands * sector
    seen = sight + sight // 2

    core = position & 1
    place = position.reshape(1)
    on_chip = [(i, i ^ 1) for i in range(blocks)]
    off_chip = [(i, (i + 1 if i & 1 else i - 1) % blocks) for i in range(blocks)]

    def ends(value, near):
        return jnp.where((core == 0) == near, value[-2:], value[:2])

    far_grad = lax.ppermute(ends(out_grad, False), "blk", off_chip)
    near_grad = lax.ppermute(ends(out_grad, True), "blk", on_chip)

    turned = (columns + 1) * (rows + SLACK)
    half = 3 * sector
    probs, probs_t, context_t, kept, sent, begins = call(
        functools.partial(pool_kernel, rows, sight, blocks * sector),
        [
            jax.ShapeDtypeStruct((bins * rows, columns), F32),
            jax.ShapeDtypeStruct((columns + 1, rows, LANES), F32),
            jax.ShapeDtypeStruct((columns + 1, rows, LANES), F32),
            jax.ShapeDtypeStruct((half, channels, LANES), BF16),
            jax.ShapeDtypeStruct((half, channels, LANES), BF16),
            jax.ShapeDtypeStruct((seen + 1,), jnp.int32),
        ],
        [
            pltpu.VMEM((bins * rows, columns), F32),
            pltpu.VMEM((bins * (rows + SLACK), columns), F32),
            pltpu.VMEM((channels * (rows + SLACK), columns), F32),
            pltpu.VMEM((turned, LANES), F32),
            pltpu.VMEM((turned, LANES), F32),
            pltpu.SemaphoreType.DMA((3,)),
        ],
        [smem(), smem(), vmem(), vmem()],
        2 * seen * 3 * rows * LANES * LANES,
        20 * bins * rows * columns,
        [anywhere()] * 3 + [vmem()] * 2 + [smem()],
        limit=56,
    )(
        place,
        az_map,
        depth_logits[0].reshape(bins * rows, columns),
        context[0].reshape(channels * rows, columns),
    )

    row_flops = 2 * TAPS * TAPS * hidden * hidden * length

    inner_grad = call(
        inner_acts_kernel,
        jax.ShapeDtypeStruct((sector - 2, hidden, length), BF16),
        [],
        [vmem()] * 2,
        row_flops * (sector - 2),
        4 * sector * length * hidden,
    )(out_grad, conv2_weight)
    weight = conv1_weight.reshape(TAPS, TAPS * channels, hidden)
    act_grads, weight_t, range_hot = call(
        outer_acts_kernel,
        [
            jax.ShapeDtypeStruct((sector + 2, hidden, length), BF16),
            jax.ShapeDtypeStruct((TAPS * hidden, TAPS * channels), BF16),
            jax.ShapeDtypeStruct((length, 2 * LANES), BF16),
        ],
        [pltpu.VMEM((4, length, hidden), BF16)] * 2 + [pltpu.VMEM((8, 2 * LANES), jnp.int32)],
        [smem()] + [vmem()] * 7,
        row_flops * 4,
        16 * length * hidden,
    )(place, near_grad, far_grad, out_grad, conv2_weight, inner_grad, weight, rng_map)

    summed = rounded_sum(kept, swapped(sent, blocks, 1))
    own = rounded_sum(summed[:sector], swapped(summed[sector : 2 * sector], blocks, 2))
    inward = [(i, i ^ 2) for i in range(blocks) if i % bands in (1, 2)]
    outward = [(i ^ 2, i) for i in range(blocks) if i % bands in (1, 2)]
    edge = rounded_sum(
        summed[2 * sector :], lax.ppermute(summed[2 * sector :], "blk", inward)
    )
    first = band == 0
    firsts = [i for i in range(blocks) if i % bands == 0]
    lasts = [i for i in range(blocks) if i % bands == bands - 1]
    last = band == bands - 1
    outer = jnp.logical_or(first, last)
    more = ((0, sector), (0, 0), (0, 0))
    far = jnp.where(
        first,
        jnp.concatenate([edge, own[:2]], axis=0),
        jnp.where(
            last,
            jnp.concatenate([own[sector - 2 :], edge], axis=0),
            jnp.pad(ends(own, False), more),
        ),
    )

    def to_next(value):
        pairs = [(i, (i - 1) % blocks) for i in firsts]
        pairs = pairs + [(i, (i + 1) % blocks) for i in lasts]
        return lax.ppermute(value, "blk", pairs)

    far_halo = lax.ppermute(far, "blk", off_chip)
    passed = jnp.where(first, far_halo[sector:], far_halo[:2])
    near_halo = lax.ppermute(
        jnp.concatenate([ends(own, True), passed], axis=0), "blk", on_chip
    )
    grad_rows = TAPS * TAPS * (hidden + channels)
    unit = blocks * 16
    grad_rows = -(-grad_rows // unit) * unit
    wide = sector + 2
    keep, send, own_reply, other_reply = call(
        grid_kernel,
        [
            jax.ShapeDtypeStruct((grad_rows // 2, hidden), BF16),
            jax.ShapeDtypeStruct((grad_rows // 2, hidden), BF16),
            jax.ShapeDtypeStruct((sector, channels, LANES), BF16),
            jax.ShapeDtypeStruct((sector, channels, LANES), BF16),
        ],
        [
            pltpu.VMEM((sector + 4, channels, 2 * LANES), BF16),
            pltpu.VMEM(((sector + 4) * channels, length), BF16),
            pltpu.VMEM((TAPS * channels, wide * length), BF16),
            pltpu.VMEM((TAPS * hidden, wide * length), BF16),
            pltpu.VMEM((wide * hidden, length), BF16),
            pltpu.VMEM((hidden, wide * length), BF16),
            pltpu.VMEM((sector * channels, length), BF16),
            pltpu.VMEM((grad_rows, hidden), BF16),
            pltpu.VMEM((TAPS * hidden, length), F32),
            pltpu.VMEM((TAPS * hidden, length), F32),
        ],
        [smem()] + [vmem()] * 9,
        row_flops * (sector + 3 * sector // 2),
        20 * sector * length * hidden,
        limit=32,
    )(
        place,
        own,
        edge,
        near_halo,
        far_halo,
        weight,
        weight_t,
        range_hot,
        act_grads,
        out_grad.reshape(sector * length, hidden),
    )

    partner = swapped(own_reply, blocks, 2)
    edge_reply = to_next(other_reply)
    passed = lax.ppermute(edge_reply, "blk", outward)
    edge_reply = jnp.where(outer, edge_reply, passed)
    theirs = swapped(
        jnp.concatenate([own_reply, partner, edge_reply], axis=0), blocks, 1
    )
    value, other_value = total_over_blocks(keep, send, position, blocks)

    replies = (own_reply, partner, edge_reply, theirs)
    scratch = [pltpu.VMEM((seen, channels, LANES), BF16), pltpu.VMEM((turned, LANES), F32)]
    cell_flops = 2 * seen * 3 * rows * LANES * LANES
    context_grad = call(
        functools.partial(context_kernel, rows),
        jax.ShapeDtypeStruct((channels * rows, columns), BF16),
        scratch + [pltpu.VMEM((channels * (rows + SLACK), columns), F32)],
        [smem()] * 2 + [vmem()] * 5,
        cell_flops,
        10 * bins * rows * columns,
    )(place, begins, *replies, probs_t)
    logit_grad = call(
        functools.partial(logit_kernel, rows),
        jax.ShapeDtypeStruct((bins * rows, columns), F32),
        scratch + [pltpu.VMEM((bins * (rows + SLACK), columns), F32)],
        [smem()] * 2 + [vmem()] * 7,
        cell_flops,
        20 * bins * rows * columns,
    )(place, begins, *replies, probs, context_t, lidar_bins[0])

    second = TAPS * TAPS * hidden
    first_rows = TAPS * TAPS * channels
    second_grad, first_grad = call(
        functools.partial(
            finish_kernel, [order[0] for order in axis_orders(blocks.bit_length() - 1)]
        ),
        [
            jax.ShapeDtypeStruct((second, hidden), F32),
            jax.ShapeDtypeStruct((first_rows, hidden), F32),
        ],
        [pltpu.VMEM((grad_rows, hidden), BF16)],
        [smem(), vmem(), vmem()],
        1,
        6 * grad_rows * hidden,
    )(place, value, other_value)
    return (
        logit_grad.reshape(1, bins, rows, columns),
        context_grad.reshape(1, channels, rows, columns),
        first_grad.reshape(TAPS, TAPS, channels, hidden),
        second_grad.reshape(TAPS, TAPS, hidden, hidden),
    )


def solution(mesh):
    return jax.shard_map(
        shards,
        mesh=mesh,
        in_specs=(
            P(("group", "blk"), None, None, None),
            P(("group", "blk"), None, None, None),
            P(("group", "blk"), None, None),
            P(),
            P(),
            P(),
            P(),
            P(("group", "blk"), None, None),
        ),
        out_specs=(
            P(("group", "blk"), None, None, None),
            P(("group", "blk"), None, None, None),
            P("group", None, None, None),
            P("group", None, None, None),
        ),
        check_vma=False,
    )
```

```python
import functools

import jax
import jax.numpy as jnp
from jax import lax
from jax.experimental import pallas as pl
from jax.experimental.pallas import tpu as pltpu
from jax.sharding import PartitionSpec as P

DEPTH_WEIGHT = 3.0
TAPS = 3
LANES = 128
SLACK = 8
F32 = jnp.float32
BF16 = jnp.bfloat16


def product(left, right, left_dim, right_dim):
    return lax.dot_general(
        left, right, (((left_dim,), (right_dim,)), ((), ())), preferred_element_type=F32
    )


def padded_rows(value, rows):
    missing = rows - value.shape[0]
    if missing == 0:
        return value
    return jnp.concatenate([value, jnp.zeros((missing, value.shape[1]), value.dtype)], axis=0)


def sectors_of(band, bands):
    partner = (band + 2) % bands
    return 1 + band, 1 + partner, (bands + 1) * (band % 2)


def pool_kernel(
    rows,
    sight,
    around,
    place,
    az_map,
    logits,
    context,
    probs_out,
    probs_t_out,
    context_t_out,
    kept,
    sent,
    begins,
    probs,
    apart_p,
    apart_c,
    wide_p,
    wide_c,
    done,
):
    columns = logits.shape[1]
    bins = logits.shape[0] // rows
    channels = context.shape[0] // rows
    half = kept.shape[0]
    sector = half // 3
    bands = 4
    position = place[0]
    band, camera = position % bands, position // bands
    seen = 2 * half
    begins[seen] = columns
    scores = logits[...].reshape(bins, rows, columns)
    powers = jnp.exp(scores - jnp.max(scores, axis=0, keepdims=True))
    shares = powers / jnp.sum(powers, axis=0, keepdims=True)
    probs[...] = shares.reshape(bins * rows, columns)
    copies = [pltpu.make_async_copy(probs, probs_out, done.at[0])]
    copies[0].start()
    pitch = rows + SLACK
    for level in range(bins):
        apart_p[level * pitch : level * pitch + rows, :] = shares[level]
    for level in range(channels):
        features = context[level * rows : (level + 1) * rows, :]
        apart_c[level * pitch : level * pitch + rows, :] = features.astype(F32)
    one = lax.broadcasted_iota(jnp.int32, (columns, columns), 0)
    same = (one == lax.broadcasted_iota(jnp.int32, (columns, columns), 1)).astype(F32)
    same = same.astype(BF16)

    def turn(row, _):
        for k in range(columns // rows):
            column = columns - 1 - row * (columns // rows) - k
            cell = az_map[camera, column] - camera * sight + sight // 4
            cell = jnp.where(cell < 0, cell + around, cell)
            begins[jnp.where(cell >= around, cell - around, cell)] = column
        block = padded_rows(apart_p[pl.ds(row, bins, stride=pitch), :], LANES)
        wide_p[pl.ds(row, columns, stride=pitch), :] = jnp.transpose(block)
        block = padded_rows(apart_c[pl.ds(row, channels, stride=pitch), :].astype(BF16), LANES)
        wide_c[pl.ds(row, columns, stride=pitch), :] = product(same, block, 1, 1)
        return 0

    lax.fori_loop(0, rows, turn, 0, unroll=8)
    for wide, out in ((wide_p, probs_t_out), (wide_c, context_t_out)):
        wide[columns * pitch :, :] = jnp.zeros((pitch, LANES), F32)
        source = wide.reshape(columns + 1, pitch, LANES).at[:, 0:rows, :]
        copies.append(pltpu.make_async_copy(source, out, done.at[len(copies)]))
        copies[-1].start()
    line = lax.broadcasted_iota(jnp.int32, (TAPS * rows, LANES), 0)

    def cell_sum(cell):
        start = begins[cell]
        spans = [pl.ds(pl.multiple_of((start + k) * pitch, 8), rows) for k in range(TAPS)]
        features = jnp.concatenate([wide_c[span, :] for span in spans], axis=0)
        shares = jnp.concatenate([wide_p[span, :] for span in spans], axis=0)
        width = (begins[cell + 1] - start) * rows
        features = jnp.where(line < width, features, 0.0).astype(BF16)
        return product(features, shares.astype(BF16), 0, 0)[:channels].astype(BF16)

    near = band + 1 - 2 * (band % 2)
    for group, (mine, theirs) in enumerate(
        zip(sectors_of(band, bands), sectors_of(near, bands))
    ):

        def one_cell(step, _, group=group, mine=mine, theirs=theirs):
            sent[group * sector + step] = cell_sum(theirs * sector + step)
            kept[group * sector + step] = cell_sum(mine * sector + step)
            return 0

        lax.fori_loop(0, sector, one_cell, 0, unroll=4)
    for copy in copies:
        copy.wait()


def act_row(taps, source, start, out, row):
    hidden, length = out.shape[1:]
    stacked = jnp.concatenate([source[start + i] for i in range(TAPS)], axis=1)
    sums = product(taps, stacked, 1, 1)
    place = lax.broadcasted_iota(jnp.int32, (hidden, length), 1)
    ahead = pltpu.roll(sums[:hidden], length - 1, 1)
    behind = pltpu.roll(sums[2 * hidden :], 1, 1)
    total = sums[hidden : 2 * hidden]
    total = total + jnp.where(place < length - 1, ahead, 0.0)
    total = total + jnp.where(place > 0, behind, 0.0)
    out[row] = total.astype(BF16)


def act_taps_of(weight):
    hidden = weight.shape[3]
    return jnp.concatenate(
        [weight[TAPS - 1 - i].reshape(TAPS * hidden, hidden) for i in range(TAPS)], axis=1
    )


def inner_acts_kernel(upstream, weight, out):
    def step(row, _):
        act_row(act_taps_of(weight), upstream, row, out, row)
        return 0

    lax.fori_loop(0, out.shape[0], step, 0)


def outer_acts_kernel(
    place,
    near,
    far,
    upstream,
    weight,
    inner,
    first_weight,
    ranges,
    out,
    weight_t,
    range_hot,
    low,
    high,
    picks,
):
    sector, length, hidden = upstream.shape
    bands = 4
    cameras, bins = ranges.shape
    channels = first_weight.shape[1] // TAPS
    lanes = range_hot.shape[1] // 2
    mine, camera = place[0] % bands, place[0] // bands
    other = jnp.where(mine < bands // 2, camera + cameras - 1, camera + 1) % cameras
    picks[...] = jnp.full(picks.shape, -1, jnp.int32)
    picks[0:1, 0:bins] = ranges[pl.ds(camera, 1), :]
    picks[0:1, lanes : lanes + bins] = ranges[pl.ds(other, 1), :]
    spots = lax.broadcasted_iota(jnp.int32, (length, 2 * lanes), 0)
    range_hot[...] = (spots == picks[0:1, :]).astype(F32).astype(BF16)
    for column in range(TAPS):
        for row in range(TAPS):
            weight_t[column * hidden : (column + 1) * hidden, row * channels : (row + 1) * channels] = (
                jnp.transpose(
                    first_weight[row, column * channels : (column + 1) * channels, :].astype(F32)
                ).astype(BF16)
            )
    ready = inner.shape[0]
    out[2 : 2 + ready] = inner[...]
    low[2:4] = upstream[0:2]
    high[0:2] = upstream[sector - 2 :]

    @pl.when(place[0] % 2 == 0)
    def _():
        low[0:2] = far[...]
        high[2:4] = near[...]

    @pl.when(place[0] % 2 == 1)
    def _():
        low[0:2] = near[...]
        high[2:4] = far[...]

    def step(row, _):
        act_row(act_taps_of(weight), low, row, out, row)
        act_row(act_taps_of(weight), high, row, out, row + sector)
        return 0

    def more(row, _):
        act_row(act_taps_of(weight), upstream, row, out, row + 2)
        return 0

    lax.fori_loop(0, 2, step, 0)
    lax.fori_loop(ready, sector - 2, more, 0)


def grid_kernel(
    place,
    own,
    edge,
    near_halo,
    far_halo,
    weight,
    weight_t,
    range_hot,
    act_grads,
    upstream,
    keep,
    send,
    own_reply,
    other_reply,
    cells,
    grid_low,
    grid_taps,
    act_taps,
    slope_rows,
    slope_lanes,
    grid_grad,
    grads,
    sums_a,
    sums_b,
):
    sector, channels, lanes = own.shape
    hidden, length = act_grads.shape[1:]
    bands = 4
    position = place[0]
    mine, core = position % bands, position % 2
    wide = sector + 4
    cells[2 : 2 + sector, :, :lanes] = own[...]
    cells[:, :, lanes:] = jnp.zeros((wide, channels, lanes), BF16)

    @pl.when(mine == 0)
    def _():
        cells[0:2, :, :lanes] = edge[sector - 2 : sector]
        cells[2 + sector :, :, :lanes] = near_halo[0:2]
        cells[0 : sector + 2, :, lanes:] = far_halo[...]

    @pl.when(mine == 1)
    def _():
        cells[0:2, :, :lanes] = near_halo[0:2]
        cells[2 + sector :, :, :lanes] = far_halo[0:2]
        cells[0:2, :, lanes:] = near_halo[2:4]

    @pl.when(mine == bands - 2)
    def _():
        cells[0:2, :, :lanes] = far_halo[0:2]
        cells[2 + sector :, :, :lanes] = near_halo[0:2]
        cells[2 + sector :, :, lanes:] = near_halo[2:4]

    @pl.when(mine == bands - 1)
    def _():
        cells[0:2, :, :lanes] = near_halo[0:2]
        cells[2 + sector :, :, :lanes] = edge[0:2]
        cells[2:, :, lanes:] = far_halo[...]

    def behind(value):
        turned = pltpu.roll(value, 1, 1)
        lane = lax.broadcasted_iota(jnp.int32, (value.shape[0], LANES), 1)
        first = jnp.where(lane > 0, turned[:, :LANES], 0.0)
        return jnp.concatenate([first, turned[:, LANES:]], axis=1)

    def ahead(value):
        turned = pltpu.roll(value, length - 1, 1)
        lane = lax.broadcasted_iota(jnp.int32, (value.shape[0], LANES), 1)
        last = jnp.where(lane < LANES - 1, turned[:, length - LANES :], 0.0)
        return jnp.concatenate([turned[:, : length - LANES], last], axis=1)

    for chunk in range(0, wide, 4):
        block = cells[chunk : chunk + 4].reshape(4 * channels, 2 * lanes)
        summed = product(block, range_hot[...], 1, 1)
        for row in range(chunk, chunk + 4):
            value = summed[(row - chunk) * channels : (row - chunk + 1) * channels]
            grid_low[row * channels : (row + 1) * channels, :] = value.astype(BF16)
            if 0 < row < wide - 1:
                spread = pl.ds((row - 1) * length, length)
                grid_taps[0:channels, spread] = behind(value).astype(BF16)
                grid_taps[channels : 2 * channels, spread] = value.astype(BF16)
                grid_taps[2 * channels :, spread] = ahead(value).astype(BF16)

    flipped = jnp.concatenate([weight[TAPS - 1 - i] for i in range(TAPS)], axis=1)

    def convolved(row, into):
        source = pl.ds(pl.multiple_of(row * channels, channels), TAPS * channels)
        into[...] = product(weight_t[...], grid_low[source, :], 1, 0)

    def back(row):
        source = pl.ds(pl.multiple_of(row * hidden, hidden), TAPS * hidden)
        sums = product(flipped, slope_rows[source, :], 1, 0)
        value = ahead(sums[:channels]) + sums[channels : 2 * channels]
        value = value + behind(sums[2 * channels :])
        grid_grad[pl.ds(pl.multiple_of(row * channels, channels), channels), :] = value.astype(BF16)

    def activated(row, sums):
        value = behind(sums[:hidden, :]) + sums[hidden : 2 * hidden, :]
        value = value + ahead(sums[2 * hidden :, :])
        logistic = 0.5 + 0.5 * jnp.tanh(0.5 * value)
        active = value * logistic
        start = pl.multiple_of(row * length, length)
        spread = pl.ds(start, length)
        low = active.astype(BF16)
        act_taps[0:hidden, spread] = pltpu.roll(low, 1, 1)
        act_taps[hidden : 2 * hidden, spread] = low
        act_taps[2 * hidden :, spread] = pltpu.roll(low, length - 1, 1)
        nothing = jnp.zeros((hidden, LANES), BF16)
        lane = lax.broadcasted_iota(jnp.int32, (hidden, LANES), 1)
        first = pl.ds(start, LANES)
        act_taps[0:hidden, first] = jnp.where(lane > 0, act_taps[0:hidden, first], nothing)
        last = pl.ds(pl.multiple_of(start + length - LANES, LANES), LANES)
        act_taps[2 * hidden :, last] = jnp.where(
            lane < LANES - 1, act_taps[2 * hidden :, last], nothing
        )
        slope = logistic * (1.0 + value * (1.0 - logistic))
        result = (act_grads[row].astype(F32) * slope).astype(BF16)
        slope_rows[pl.ds(pl.multiple_of(row * hidden, hidden), hidden), :] = result
        slope_lanes[:, spread] = result

    rows = sector + 2
    slope_rows[0 : 3 * hidden, :] = jnp.zeros((3 * hidden, length), BF16)

    def two_rows(pair, _):
        row = 2 * pair
        back(jnp.maximum(row - 3, 0))
        convolved(row + 1, sums_b)
        activated(row, sums_a)
        back(jnp.maximum(row - 2, 0))
        convolved(jnp.minimum(row + 2, rows - 1), sums_a)
        activated(row + 1, sums_b)
        return 0

    convolved(0, sums_a)
    lax.fori_loop(0, rows // 2, two_rows, 0)
    back(sector - 1)
    count = sector * length
    tall = TAPS * hidden
    short = TAPS * channels

    def second(tap, _):
        window = pl.ds(pl.multiple_of(tap * length, length), count)
        result = product(act_taps[:, window], upstream[...], 1, 0)
        grads[pl.ds(pl.multiple_of(tap * tall, tall), tall), :] = result.astype(BF16)
        return 0

    lax.fori_loop(0, TAPS, second, 0)
    windows = [grid_taps[:, tap * length : tap * length + count] for tap in range(TAPS)]
    result = product(
        jnp.concatenate(windows, axis=0), slope_lanes[:, length : length + count], 1, 1
    )
    grads[TAPS * tall : TAPS * (tall + short), :] = result.astype(BF16)
    base = TAPS * (tall + short)
    grads[base:, :] = jnp.zeros((grads.shape[0] - base, hidden), BF16)
    half = keep.shape[0]
    keep[...] = grads[pl.ds(pl.multiple_of(core * half, half), half), :]
    send[...] = grads[pl.ds(pl.multiple_of((1 - core) * half, half), half), :]
    picked = product(grid_grad[...], range_hot[...], 1, 0).astype(BF16)
    own_reply[...] = picked[:, :lanes].reshape(sector, channels, lanes)
    other_reply[...] = picked[:, lanes:].reshape(sector, channels, lanes)


def finish_kernel(shifts, place, value, other, second, first, total):
    half = value.shape[0]
    size = half // 4
    position = place[0]
    core = position % 2
    for source, side in ((value, core), (other, 1 - core)):
        digit = jnp.where(side == 0, position >> shifts[0], position >> shifts[1]) & 3
        for mask in range(4):
            spot = side * half + (digit ^ mask) * size
            total[pl.ds(pl.multiple_of(spot, size), size), :] = source[
                mask * size : (mask + 1) * size, :
            ]
    count = second.shape[0]
    second[...] = total[0:count, :].astype(F32)
    first[...] = total[count : count + first.shape[0], :].astype(F32)


def lay_out(place, sector, mine, theirs, wedges):
    bands = 4
    band = place[0] % bands
    near = band + 1 - 2 * (band % 2)
    for group, spot in enumerate(sectors_of(band, bands)):
        wedges[pl.ds(spot * sector, sector)] = mine[group][...]
    for group, spot in enumerate(sectors_of(near, bands)):
        wedges[pl.ds(spot * sector, sector)] = theirs[group * sector : (group + 1) * sector]


def logit_kernel(
    rows,
    place,
    begins,
    own,
    partner,
    edge,
    theirs,
    probs,
    context_t,
    lidar,
    logit_grad,
    wedges,
    wide,
    apart,
):
    columns = probs.shape[1]
    bins = probs.shape[0] // rows
    sector, channels, _ = own.shape
    lay_out(place, sector, (own, partner, edge), theirs, wedges)

    pitch = rows + SLACK

    def one_cell(cell, _):
        start = begins[cell]
        features = context_t[pl.ds(start, TAPS)].reshape(TAPS * rows, LANES)
        result = product(features[:, :channels].astype(BF16), wedges[cell], 1, 0)
        for k in range(TAPS):
            span = pl.ds(pl.multiple_of((start + k) * pitch, 8), rows)
            wide[span, :] = result[k * rows : (k + 1) * rows]
        return 0

    lax.fori_loop(0, wedges.shape[0], one_cell, 0, unroll=8)

    def turn(row, _):
        block = jnp.transpose(wide[pl.ds(row, columns, stride=pitch), :])
        apart[pl.ds(row, bins, stride=pitch), :] = block[:bins]
        return 0

    lax.fori_loop(0, rows, turn, 0, unroll=8)
    sums = [jnp.zeros((rows, columns), F32) for _ in range(4)]
    for level in range(bins):
        share = probs[level * rows : (level + 1) * rows, :]
        sums[level % 4] += share * apart[level * pitch : level * pitch + rows, :]
    expected = (sums[0] + sums[1]) + (sums[2] + sums[3])
    target = lidar[...]
    seen = jnp.where(target >= 0, DEPTH_WEIGHT, 0.0)
    for level in range(bins):
        share = probs[level * rows : (level + 1) * rows, :]
        slope = apart[level * pitch : level * pitch + rows, :]
        hit = jnp.where(target == level, DEPTH_WEIGHT, 0.0)
        result = share * (slope - expected) + (seen * share - hit)
        logit_grad[level * rows : (level + 1) * rows, :] = result


def context_kernel(
    rows,
    place,
    begins,
    own,
    partner,
    edge,
    theirs,
    probs_t,
    context_grad,
    wedges,
    wide,
    apart,
):
    columns = context_grad.shape[1]
    sector, channels, _ = own.shape
    lay_out(place, sector, (own, partner, edge), theirs, wedges)

    pitch = rows + SLACK

    def one_cell(cell, _):
        start = begins[cell]
        shares = probs_t[pl.ds(start, TAPS)].reshape(TAPS * rows, LANES)
        result = product(shares.astype(BF16), wedges[cell], 1, 1)
        for k in range(TAPS):
            span = pl.ds(pl.multiple_of((start + k) * pitch, 8), rows)
            wide[span, 0:channels] = result[k * rows : (k + 1) * rows]
        return 0

    lax.fori_loop(0, wedges.shape[0], one_cell, 0, unroll=8)
    one = lax.broadcasted_iota(jnp.int32, (channels, channels), 0)
    same = (one == lax.broadcasted_iota(jnp.int32, (channels, channels), 1)).astype(F32)
    same = same.astype(BF16)

    def turn(row, _):
        block = wide[pl.ds(row, columns, stride=pitch), :][:, :channels].astype(BF16)
        apart[pl.ds(row, channels, stride=pitch), :] = product(same, block, 1, 1)
        return 0

    lax.fori_loop(0, rows, turn, 0, unroll=8)
    for level in range(channels):
        block = apart[level * pitch : level * pitch + rows, :]
        context_grad[level * rows : (level + 1) * rows, :] = block.astype(BF16)


def vmem():
    return pl.BlockSpec(memory_space=pltpu.VMEM)


def smem():
    return pl.BlockSpec(memory_space=pltpu.SMEM)


def anywhere():
    return pl.BlockSpec(memory_space=pltpu.HBM)


def call(kernel, out_shape, scratch, spaces, flops, moved, outs=None, limit=16):
    many = isinstance(out_shape, (list, tuple))
    return pl.pallas_call(
        kernel,
        out_shape=out_shape,
        in_specs=spaces,
        out_specs=outs or ([vmem() for _ in out_shape] if many else vmem()),
        scratch_shapes=scratch,
        compiler_params=pltpu.CompilerParams(vmem_limit_bytes=limit * 1024 * 1024),
        cost_estimate=pl.CostEstimate(flops=flops, bytes_accessed=moved, transcendentals=0),
    )


def rounded_sum(left, right):
    return (left.astype(F32) + right.astype(F32)).astype(BF16)


def swapped(value, blocks, mask):
    return lax.ppermute(value, "blk", [(i, i ^ mask) for i in range(blocks)])


def piece(value, index, count):
    size = value.shape[0] // count
    return lax.dynamic_slice_in_dim(value, index * size, size, 0)


def axis_orders(count):
    pairs = list(range(1, count, 2))
    return pairs, pairs[1:] + pairs[:1]


def total_over_blocks(keep, send, position, blocks):
    count = blocks.bit_length() - 1
    orders = axis_orders(count)
    core = position & 1
    digits = [
        jnp.where(core == 0, position >> one, position >> two) & 3 for one, two in zip(*orders)
    ]

    def sent(part, step, mask):
        to = [(i, i ^ (mask << orders[i & 1][step])) for i in range(blocks)]
        return lax.ppermute(part, "blk", to)

    value = rounded_sum(keep, swapped(send, blocks, 1))
    for step, digit in enumerate(digits):
        leaving = [piece(value, digit ^ mask, 4) for mask in (3, 1, 2)]
        arrived = [sent(part, step, mask) for part, mask in zip(leaving, (3, 1, 2))]
        total = piece(value, digit, 4).astype(F32)
        for part in arrived:
            total = total + part.astype(F32)
        value = total.astype(BF16)
    for step, digit in reversed(list(enumerate(digits))):
        held = [value] + [sent(value, step, mask) for mask in (1, 2, 3)]
        if step == 0:
            value = jnp.concatenate(held, axis=0)
            break
        high, low = digit >> 1 == 1, digit & 1 == 1

        def at(k):
            one = jnp.where(low, held[k ^ 1], held[k])
            two = jnp.where(low, held[k ^ 3], held[k ^ 2])
            return jnp.where(high, two, one)

        value = jnp.concatenate([at(k) for k in range(4)], axis=0)
    return value, swapped(value, blocks, 1)


def shards(
    depth_logits, context, lidar_bins, az_map, rng_map, conv1_weight, conv2_weight, out_grad
):
    blocks = lax.axis_size("blk")
    position = lax.axis_index("blk")
    cameras, columns = az_map.shape
    bands = blocks // cameras
    sector, length, hidden = out_grad.shape
    bins, rows = depth_logits.shape[1:3]
    channels = context.shape[1]
    if bands != 4 or blocks != 1 << (blocks.bit_length() - 1) or blocks.bit_length() % 2 or bins > LANES or channels > LANES or sector < 6 or sector % 2:
        raise ValueError("unsupported sizes")
    band = position % bands
    sight = bands * sector
    seen = sight + sight // 2

    core = position & 1
    place = position.reshape(1)
    on_chip = [(i, i ^ 1) for i in range(blocks)]
    off_chip = [(i, (i + 1 if i & 1 else i - 1) % blocks) for i in range(blocks)]

    def ends(value, near):
        return jnp.where((core == 0) == near, value[-2:], value[:2])

    far_grad = lax.ppermute(ends(out_grad, False), "blk", off_chip)
    near_grad = lax.ppermute(ends(out_grad, True), "blk", on_chip)

    turned = (columns + 1) * (rows + SLACK)
    half = 3 * sector
    probs, probs_t, context_t, kept, sent, begins = call(
        functools.partial(pool_kernel, rows, sight, blocks * sector),
        [
            jax.ShapeDtypeStruct((bins * rows, columns), F32),
            jax.ShapeDtypeStruct((columns + 1, rows, LANES), F32),
            jax.ShapeDtypeStruct((columns + 1, rows, LANES), F32),
            jax.ShapeDtypeStruct((half, channels, LANES), BF16),
            jax.ShapeDtypeStruct((half, channels, LANES), BF16),
            jax.ShapeDtypeStruct((seen + 1,), jnp.int32),
        ],
        [
            pltpu.VMEM((bins * rows, columns), F32),
            pltpu.VMEM((bins * (rows + SLACK), columns), F32),
            pltpu.VMEM((channels * (rows + SLACK), columns), F32),
            pltpu.VMEM((turned, LANES), F32),
            pltpu.VMEM((turned, LANES), F32),
            pltpu.SemaphoreType.DMA((3,)),
        ],
        [smem(), smem(), vmem(), vmem()],
        2 * seen * 3 * rows * LANES * LANES,
        20 * bins * rows * columns,
        [anywhere()] * 3 + [vmem()] * 2 + [smem()],
        limit=56,
    )(
        place,
        az_map,
        depth_logits[0].reshape(bins * rows, columns),
        context[0].reshape(channels * rows, columns),
    )

    row_flops = 2 * TAPS * TAPS * hidden * hidden * length

    inner_grad = call(
        inner_acts_kernel,
        jax.ShapeDtypeStruct((sector - 3, hidden, length), BF16),
        [],
        [vmem()] * 2,
        row_flops * (sector - 3),
        4 * sector * length * hidden,
    )(out_grad, conv2_weight)
    weight = conv1_weight.reshape(TAPS, TAPS * channels, hidden)
    act_grads, weight_t, range_hot = call(
        outer_acts_kernel,
        [
            jax.ShapeDtypeStruct((sector + 2, hidden, length), BF16),
            jax.ShapeDtypeStruct((TAPS * hidden, TAPS * channels), BF16),
            jax.ShapeDtypeStruct((length, 2 * LANES), BF16),
        ],
        [pltpu.VMEM((4, length, hidden), BF16)] * 2 + [pltpu.VMEM((8, 2 * LANES), jnp.int32)],
        [smem()] + [vmem()] * 7,
        row_flops * 5,
        16 * length * hidden,
    )(place, near_grad, far_grad, out_grad, conv2_weight, inner_grad, weight, rng_map)

    summed = rounded_sum(kept, swapped(sent, blocks, 1))
    own = rounded_sum(summed[:sector], swapped(summed[sector : 2 * sector], blocks, 2))
    inward = [(i, i ^ 2) for i in range(blocks) if i % bands in (1, 2)]
    outward = [(i ^ 2, i) for i in range(blocks) if i % bands in (1, 2)]
    edge = rounded_sum(
        summed[2 * sector :], lax.ppermute(summed[2 * sector :], "blk", inward)
    )
    first = band == 0
    firsts = [i for i in range(blocks) if i % bands == 0]
    lasts = [i for i in range(blocks) if i % bands == bands - 1]
    last = band == bands - 1
    outer = jnp.logical_or(first, last)
    more = ((0, sector), (0, 0), (0, 0))
    far = jnp.where(
        first,
        jnp.concatenate([edge, own[:2]], axis=0),
        jnp.where(
            last,
            jnp.concatenate([own[sector - 2 :], edge], axis=0),
            jnp.pad(ends(own, False), more),
        ),
    )

    def to_next(value):
        pairs = [(i, (i - 1) % blocks) for i in firsts]
        pairs = pairs + [(i, (i + 1) % blocks) for i in lasts]
        return lax.ppermute(value, "blk", pairs)

    far_halo = lax.ppermute(far, "blk", off_chip)
    passed = jnp.where(first, far_halo[sector:], far_halo[:2])
    near_halo = lax.ppermute(
        jnp.concatenate([ends(own, True), passed], axis=0), "blk", on_chip
    )
    grad_rows = TAPS * TAPS * (hidden + channels)
    unit = blocks * 16
    grad_rows = -(-grad_rows // unit) * unit
    wide = sector + 2
    keep, send, own_reply, other_reply = call(
        grid_kernel,
        [
            jax.ShapeDtypeStruct((grad_rows // 2, hidden), BF16),
            jax.ShapeDtypeStruct((grad_rows // 2, hidden), BF16),
            jax.ShapeDtypeStruct((sector, channels, LANES), BF16),
            jax.ShapeDtypeStruct((sector, channels, LANES), BF16),
        ],
        [
            pltpu.VMEM((sector + 4, channels, 2 * LANES), BF16),
            pltpu.VMEM(((sector + 4) * channels, length), BF16),
            pltpu.VMEM((TAPS * channels, wide * length), BF16),
            pltpu.VMEM((TAPS * hidden, wide * length), BF16),
            pltpu.VMEM((wide * hidden, length), BF16),
            pltpu.VMEM((hidden, wide * length), BF16),
            pltpu.VMEM((sector * channels, length), BF16),
            pltpu.VMEM((grad_rows, hidden), BF16),
            pltpu.VMEM((TAPS * hidden, length), F32),
            pltpu.VMEM((TAPS * hidden, length), F32),
        ],
        [smem()] + [vmem()] * 9,
        row_flops * (sector + 3 * sector // 2),
        20 * sector * length * hidden,
        limit=32,
    )(
        place,
        own,
        edge,
        near_halo,
        far_halo,
        weight,
        weight_t,
        range_hot,
        act_grads,
        out_grad.reshape(sector * length, hidden),
    )

    partner = swapped(own_reply, blocks, 2)
    edge_reply = to_next(other_reply)
    passed = lax.ppermute(edge_reply, "blk", outward)
    edge_reply = jnp.where(outer, edge_reply, passed)
    theirs = swapped(
        jnp.concatenate([own_reply, partner, edge_reply], axis=0), blocks, 1
    )
    value, other_value = total_over_blocks(keep, send, position, blocks)

    replies = (own_reply, partner, edge_reply, theirs)
    scratch = [pltpu.VMEM((seen, channels, LANES), BF16), pltpu.VMEM((turned, LANES), F32)]
    cell_flops = 2 * seen * 3 * rows * LANES * LANES
    context_grad = call(
        functools.partial(context_kernel, rows),
        jax.ShapeDtypeStruct((channels * rows, columns), BF16),
        scratch + [pltpu.VMEM((channels * (rows + SLACK), columns), F32)],
        [smem()] * 2 + [vmem()] * 5,
        cell_flops,
        10 * bins * rows * columns,
    )(place, begins, *replies, probs_t)
    logit_grad = call(
        functools.partial(logit_kernel, rows),
        jax.ShapeDtypeStruct((bins * rows, columns), F32),
        scratch + [pltpu.VMEM((bins * (rows + SLACK), columns), F32)],
        [smem()] * 2 + [vmem()] * 7,
        cell_flops,
        20 * bins * rows * columns,
    )(place, begins, *replies, probs, context_t, lidar_bins[0])

    second = TAPS * TAPS * hidden
    first_rows = TAPS * TAPS * channels
    second_grad, first_grad = call(
        functools.partial(
            finish_kernel, [order[0] for order in axis_orders(blocks.bit_length() - 1)]
        ),
        [
            jax.ShapeDtypeStruct((second, hidden), F32),
            jax.ShapeDtypeStruct((first_rows, hidden), F32),
        ],
        [pltpu.VMEM((grad_rows, hidden), BF16)],
        [smem(), vmem(), vmem()],
        1,
        6 * grad_rows * hidden,
    )(place, value, other_value)
    return (
        logit_grad.reshape(1, bins, rows, columns),
        context_grad.reshape(1, channels, rows, columns),
        first_grad.reshape(TAPS, TAPS, channels, hidden),
        second_grad.reshape(TAPS, TAPS, hidden, hidden),
    )


def solution(mesh):
    return jax.shard_map(
        shards,
        mesh=mesh,
        in_specs=(
            P(("group", "blk"), None, None, None),
            P(("group", "blk"), None, None, None),
            P(("group", "blk"), None, None),
            P(),
            P(),
            P(),
            P(),
            P(("group", "blk"), None, None),
        ),
        out_specs=(
            P(("group", "blk"), None, None, None),
            P(("group", "blk"), None, None, None),
            P("group", None, None, None),
            P("group", None, None, None),
        ),
        check_vma=False,
    )
```

```python
import functools

import jax
import jax.numpy as jnp
from jax import lax
from jax.experimental import pallas as pl
from jax.experimental.pallas import tpu as pltpu
from jax.sharding import PartitionSpec as P

DEPTH_WEIGHT = 3.0
TAPS = 3
LANES = 128
SLACK = 8
F32 = jnp.float32
BF16 = jnp.bfloat16


def product(left, right, left_dim, right_dim):
    return lax.dot_general(
        left, right, (((left_dim,), (right_dim,)), ((), ())), preferred_element_type=F32
    )


def padded_rows(value, rows):
    missing = rows - value.shape[0]
    if missing == 0:
        return value
    return jnp.concatenate([value, jnp.zeros((missing, value.shape[1]), value.dtype)], axis=0)


def sectors_of(band, bands):
    partner = (band + 2) % bands
    return 1 + band, 1 + partner, (bands + 1) * (band % 2)


def pool_kernel(
    rows,
    sight,
    around,
    place,
    az_map,
    logits,
    context,
    probs_out,
    probs_t_out,
    context_t_out,
    kept,
    sent,
    begins,
    probs,
    apart_p,
    apart_c,
    wide_p,
    wide_c,
    done,
):
    columns = logits.shape[1]
    bins = logits.shape[0] // rows
    channels = context.shape[0] // rows
    half = kept.shape[0]
    sector = half // 3
    bands = 4
    position = place[0]
    band, camera = position % bands, position // bands
    seen = 2 * half
    begins[seen] = columns
    scores = logits[...].reshape(bins, rows, columns)
    powers = jnp.exp(scores - jnp.max(scores, axis=0, keepdims=True))
    shares = powers / jnp.sum(powers, axis=0, keepdims=True)
    probs[...] = shares.reshape(bins * rows, columns)
    copies = [pltpu.make_async_copy(probs, probs_out, done.at[0])]
    copies[0].start()
    pitch = rows + SLACK
    for level in range(bins):
        apart_p[level * pitch : level * pitch + rows, :] = shares[level]
    for level in range(channels):
        features = context[level * rows : (level + 1) * rows, :]
        apart_c[level * pitch : level * pitch + rows, :] = features.astype(F32)
    one = lax.broadcasted_iota(jnp.int32, (columns, columns), 0)
    same = (one == lax.broadcasted_iota(jnp.int32, (columns, columns), 1)).astype(F32)
    same = same.astype(BF16)

    def turn(row, _):
        for k in range(columns // rows):
            column = columns - 1 - row * (columns // rows) - k
            cell = az_map[camera, column] - camera * sight + sight // 4
            cell = jnp.where(cell < 0, cell + around, cell)
            begins[jnp.where(cell >= around, cell - around, cell)] = column
        block = padded_rows(apart_p[pl.ds(row, bins, stride=pitch), :], LANES)
        wide_p[pl.ds(row, columns, stride=pitch), :] = jnp.transpose(block)
        block = padded_rows(apart_c[pl.ds(row, channels, stride=pitch), :].astype(BF16), LANES)
        wide_c[pl.ds(row, columns, stride=pitch), :] = product(same, block, 1, 1)
        return 0

    lax.fori_loop(0, rows, turn, 0, unroll=8)
    for wide, out in ((wide_p, probs_t_out), (wide_c, context_t_out)):
        wide[columns * pitch :, :] = jnp.zeros((pitch, LANES), F32)
        source = wide.reshape(columns + 1, pitch, LANES).at[:, 0:rows, :]
        copies.append(pltpu.make_async_copy(source, out, done.at[len(copies)]))
        copies[-1].start()
    line = lax.broadcasted_iota(jnp.int32, (TAPS * rows, LANES), 0)

    def cell_sum(cell):
        start = begins[cell]
        spans = [pl.ds(pl.multiple_of((start + k) * pitch, 8), rows) for k in range(TAPS)]
        features = jnp.concatenate([wide_c[span, :] for span in spans], axis=0)
        shares = jnp.concatenate([wide_p[span, :] for span in spans], axis=0)
        width = (begins[cell + 1] - start) * rows
        features = jnp.where(line < width, features, 0.0).astype(BF16)
        return product(features, shares.astype(BF16), 0, 0)[:channels].astype(BF16)

    near = band + 1 - 2 * (band % 2)
    for group, (mine, theirs) in enumerate(
        zip(sectors_of(band, bands), sectors_of(near, bands))
    ):

        def one_cell(step, _, group=group, mine=mine, theirs=theirs):
            sent[group * sector + step] = cell_sum(theirs * sector + step)
            kept[group * sector + step] = cell_sum(mine * sector + step)
            return 0

        lax.fori_loop(0, sector, one_cell, 0, unroll=4)
    for copy in copies:
        copy.wait()


def act_row(taps, source, start, out, row):
    hidden, length = out.shape[1:]
    stacked = jnp.concatenate([source[start + i] for i in range(TAPS)], axis=1)
    sums = product(taps, stacked, 1, 1)
    place = lax.broadcasted_iota(jnp.int32, (hidden, length), 1)
    ahead = pltpu.roll(sums[:hidden], length - 1, 1)
    behind = pltpu.roll(sums[2 * hidden :], 1, 1)
    total = sums[hidden : 2 * hidden]
    total = total + jnp.where(place < length - 1, ahead, 0.0)
    total = total + jnp.where(place > 0, behind, 0.0)
    out[row] = total.astype(BF16)


def act_taps_of(weight):
    hidden = weight.shape[3]
    return jnp.concatenate(
        [weight[TAPS - 1 - i].reshape(TAPS * hidden, hidden) for i in range(TAPS)], axis=1
    )


def inner_acts_kernel(upstream, weight, out):
    def step(row, _):
        act_row(act_taps_of(weight), upstream, row, out, row)
        return 0

    lax.fori_loop(0, out.shape[0], step, 0)


def outer_acts_kernel(
    place,
    near,
    far,
    upstream,
    weight,
    inner,
    first_weight,
    ranges,
    out,
    weight_t,
    range_hot,
    low,
    high,
    picks,
):
    sector, length, hidden = upstream.shape
    bands = 4
    cameras, bins = ranges.shape
    channels = first_weight.shape[1] // TAPS
    lanes = range_hot.shape[1] // 2
    mine, camera = place[0] % bands, place[0] // bands
    other = jnp.where(mine < bands // 2, camera + cameras - 1, camera + 1) % cameras
    picks[...] = jnp.full(picks.shape, -1, jnp.int32)
    picks[0:1, 0:bins] = ranges[pl.ds(camera, 1), :]
    picks[0:1, lanes : lanes + bins] = ranges[pl.ds(other, 1), :]
    spots = lax.broadcasted_iota(jnp.int32, (length, 2 * lanes), 0)
    range_hot[...] = (spots == picks[0:1, :]).astype(F32).astype(BF16)
    for column in range(TAPS):
        for row in range(TAPS):
            weight_t[column * hidden : (column + 1) * hidden, row * channels : (row + 1) * channels] = (
                jnp.transpose(
                    first_weight[row, column * channels : (column + 1) * channels, :].astype(F32)
                ).astype(BF16)
            )
    ready = inner.shape[0]
    out[2 : 2 + ready] = inner[...]
    low[2:4] = upstream[0:2]
    high[0:2] = upstream[sector - 2 :]

    @pl.when(place[0] % 2 == 0)
    def _():
        low[0:2] = far[...]
        high[2:4] = near[...]

    @pl.when(place[0] % 2 == 1)
    def _():
        low[0:2] = near[...]
        high[2:4] = far[...]

    def step(row, _):
        act_row(act_taps_of(weight), low, row, out, row)
        act_row(act_taps_of(weight), high, row, out, row + sector)
        return 0

    def more(row, _):
        act_row(act_taps_of(weight), upstream, row, out, row + 2)
        return 0

    lax.fori_loop(0, 2, step, 0)
    lax.fori_loop(ready, sector - 2, more, 0)


def grid_kernel(
    place,
    own,
    edge,
    near_halo,
    far_halo,
    weight,
    weight_t,
    range_hot,
    act_grads,
    upstream,
    keep,
    send,
    own_reply,
    other_reply,
    cells,
    grid_low,
    grid_taps,
    act_taps,
    slope_rows,
    slope_lanes,
    grid_grad,
    grads,
    sums_a,
    sums_b,
):
    sector, channels, lanes = own.shape
    hidden, length = act_grads.shape[1:]
    bands = 4
    position = place[0]
    mine, core = position % bands, position % 2
    wide = sector + 4
    cells[2 : 2 + sector, :, :lanes] = own[...]
    cells[:, :, lanes:] = jnp.zeros((wide, channels, lanes), BF16)

    @pl.when(mine == 0)
    def _():
        cells[0:2, :, :lanes] = edge[sector - 2 : sector]
        cells[2 + sector :, :, :lanes] = near_halo[0:2]
        cells[0 : sector + 2, :, lanes:] = far_halo[...]

    @pl.when(mine == 1)
    def _():
        cells[0:2, :, :lanes] = near_halo[0:2]
        cells[2 + sector :, :, :lanes] = far_halo[0:2]
        cells[0:2, :, lanes:] = near_halo[2:4]

    @pl.when(mine == bands - 2)
    def _():
        cells[0:2, :, :lanes] = far_halo[0:2]
        cells[2 + sector :, :, :lanes] = near_halo[0:2]
        cells[2 + sector :, :, lanes:] = near_halo[2:4]

    @pl.when(mine == bands - 1)
    def _():
        cells[0:2, :, :lanes] = near_halo[0:2]
        cells[2 + sector :, :, :lanes] = edge[0:2]
        cells[2:, :, lanes:] = far_halo[...]

    def behind(value):
        turned = pltpu.roll(value, 1, 1)
        lane = lax.broadcasted_iota(jnp.int32, (value.shape[0], LANES), 1)
        first = jnp.where(lane > 0, turned[:, :LANES], 0.0)
        return jnp.concatenate([first, turned[:, LANES:]], axis=1)

    def ahead(value):
        turned = pltpu.roll(value, length - 1, 1)
        lane = lax.broadcasted_iota(jnp.int32, (value.shape[0], LANES), 1)
        last = jnp.where(lane < LANES - 1, turned[:, length - LANES :], 0.0)
        return jnp.concatenate([turned[:, : length - LANES], last], axis=1)

    for chunk in range(0, wide, 4):
        block = cells[chunk : chunk + 4].reshape(4 * channels, 2 * lanes)
        summed = product(block, range_hot[...], 1, 1)
        for row in range(chunk, chunk + 4):
            value = summed[(row - chunk) * channels : (row - chunk + 1) * channels]
            grid_low[row * channels : (row + 1) * channels, :] = value.astype(BF16)
            if 0 < row < wide - 1:
                spread = pl.ds((row - 1) * length, length)
                grid_taps[0:channels, spread] = behind(value).astype(BF16)
                grid_taps[channels : 2 * channels, spread] = value.astype(BF16)
                grid_taps[2 * channels :, spread] = ahead(value).astype(BF16)

    flipped = jnp.concatenate([weight[TAPS - 1 - i] for i in range(TAPS)], axis=1)

    def convolved(row, into):
        source = pl.ds(pl.multiple_of(row * channels, channels), TAPS * channels)
        into[...] = product(weight_t[...], grid_low[source, :], 1, 0)

    def back(row):
        source = pl.ds(pl.multiple_of(row * hidden, hidden), TAPS * hidden)
        sums = product(flipped, slope_rows[source, :], 1, 0)
        value = ahead(sums[:channels]) + sums[channels : 2 * channels]
        value = value + behind(sums[2 * channels :])
        grid_grad[pl.ds(pl.multiple_of(row * channels, channels), channels), :] = value.astype(BF16)

    def activated(row, sums):
        value = behind(sums[:hidden, :]) + sums[hidden : 2 * hidden, :]
        value = value + ahead(sums[2 * hidden :, :])
        logistic = 0.5 + 0.5 * jnp.tanh(0.5 * value)
        active = value * logistic
        start = pl.multiple_of(row * length, length)
        spread = pl.ds(start, length)
        low = active.astype(BF16)
        act_taps[0:hidden, spread] = pltpu.roll(low, 1, 1)
        act_taps[hidden : 2 * hidden, spread] = low
        act_taps[2 * hidden :, spread] = pltpu.roll(low, length - 1, 1)
        nothing = jnp.zeros((hidden, LANES), BF16)
        lane = lax.broadcasted_iota(jnp.int32, (hidden, LANES), 1)
        first = pl.ds(start, LANES)
        act_taps[0:hidden, first] = jnp.where(lane > 0, act_taps[0:hidden, first], nothing)
        last = pl.ds(pl.multiple_of(start + length - LANES, LANES), LANES)
        act_taps[2 * hidden :, last] = jnp.where(
            lane < LANES - 1, act_taps[2 * hidden :, last], nothing
        )
        slope = logistic * (1.0 + value * (1.0 - logistic))
        result = (act_grads[row].astype(F32) * slope).astype(BF16)
        slope_rows[pl.ds(pl.multiple_of(row * hidden, hidden), hidden), :] = result
        slope_lanes[:, spread] = result

    rows = sector + 2
    slope_rows[0 : 3 * hidden, :] = jnp.zeros((3 * hidden, length), BF16)

    def two_rows(pair, _):
        row = 2 * pair
        back(jnp.maximum(row - 3, 0))
        convolved(row + 1, sums_b)
        activated(row, sums_a)
        back(jnp.maximum(row - 2, 0))
        convolved(jnp.minimum(row + 2, rows - 1), sums_a)
        activated(row + 1, sums_b)
        return 0

    convolved(0, sums_a)
    lax.fori_loop(0, rows // 2, two_rows, 0)
    back(sector - 1)
    count = sector * length
    tall = TAPS * hidden
    short = TAPS * channels

    def second(tap, _):
        window = pl.ds(pl.multiple_of(tap * length, length), count)
        result = product(act_taps[:, window], upstream[...], 1, 0)
        grads[pl.ds(pl.multiple_of(tap * tall, tall), tall), :] = result.astype(BF16)
        return 0

    lax.fori_loop(0, TAPS, second, 0)
    windows = [grid_taps[:, tap * length : tap * length + count] for tap in range(TAPS)]
    result = product(
        jnp.concatenate(windows, axis=0), slope_lanes[:, length : length + count], 1, 1
    )
    grads[TAPS * tall : TAPS * (tall + short), :] = result.astype(BF16)
    base = TAPS * (tall + short)
    grads[base:, :] = jnp.zeros((grads.shape[0] - base, hidden), BF16)
    half = keep.shape[0]
    keep[...] = grads[pl.ds(pl.multiple_of(core * half, half), half), :]
    send[...] = grads[pl.ds(pl.multiple_of((1 - core) * half, half), half), :]
    picked = product(grid_grad[...], range_hot[...], 1, 0).astype(BF16)
    own_reply[...] = picked[:, :lanes].reshape(sector, channels, lanes)
    other_reply[...] = picked[:, lanes:].reshape(sector, channels, lanes)


def finish_kernel(shifts, place, value, other, second, first, total):
    half = value.shape[0]
    size = half // 4
    position = place[0]
    core = position % 2
    for source, side in ((value, core), (other, 1 - core)):
        digit = jnp.where(side == 0, position >> shifts[0], position >> shifts[1]) & 3
        for mask in range(4):
            spot = side * half + (digit ^ mask) * size
            total[pl.ds(pl.multiple_of(spot, size), size), :] = source[
                mask * size : (mask + 1) * size, :
            ]
    count = second.shape[0]
    second[...] = total[0:count, :].astype(F32)
    first[...] = total[count : count + first.shape[0], :].astype(F32)


def lay_out(place, sector, mine, theirs, wedges):
    bands = 4
    band = place[0] % bands
    near = band + 1 - 2 * (band % 2)
    for group, spot in enumerate(sectors_of(band, bands)):
        wedges[pl.ds(spot * sector, sector)] = mine[group][...]
    for group, spot in enumerate(sectors_of(near, bands)):
        wedges[pl.ds(spot * sector, sector)] = theirs[group * sector : (group + 1) * sector]


def logit_kernel(
    rows,
    place,
    begins,
    own,
    partner,
    edge,
    theirs,
    probs,
    context_t,
    lidar,
    logit_grad,
    wedges,
    wide,
    apart,
):
    columns = probs.shape[1]
    bins = probs.shape[0] // rows
    sector, channels, _ = own.shape
    lay_out(place, sector, (own, partner, edge), theirs, wedges)

    pitch = rows + SLACK

    def one_cell(cell, _):
        start = begins[cell]
        features = context_t[pl.ds(start, TAPS)].reshape(TAPS * rows, LANES)
        result = product(features[:, :channels].astype(BF16), wedges[cell], 1, 0)
        for k in range(TAPS):
            span = pl.ds(pl.multiple_of((start + k) * pitch, 8), rows)
            wide[span, :] = result[k * rows : (k + 1) * rows]
        return 0

    lax.fori_loop(0, wedges.shape[0], one_cell, 0, unroll=8)

    def turn(row, _):
        block = jnp.transpose(wide[pl.ds(row, columns, stride=pitch), :])
        apart[pl.ds(row, bins, stride=pitch), :] = block[:bins]
        return 0

    lax.fori_loop(0, rows, turn, 0, unroll=8)
    sums = [jnp.zeros((rows, columns), F32) for _ in range(4)]
    for level in range(bins):
        share = probs[level * rows : (level + 1) * rows, :]
        sums[level % 4] += share * apart[level * pitch : level * pitch + rows, :]
    expected = (sums[0] + sums[1]) + (sums[2] + sums[3])
    target = lidar[...]
    seen = jnp.where(target >= 0, DEPTH_WEIGHT, 0.0)
    for level in range(bins):
        share = probs[level * rows : (level + 1) * rows, :]
        slope = apart[level * pitch : level * pitch + rows, :]
        hit = jnp.where(target == level, DEPTH_WEIGHT, 0.0)
        result = share * (slope - expected) + (seen * share - hit)
        logit_grad[level * rows : (level + 1) * rows, :] = result


def context_kernel(
    rows,
    place,
    begins,
    own,
    partner,
    edge,
    theirs,
    probs_t,
    context_grad,
    wedges,
    wide,
    apart,
):
    columns = context_grad.shape[1]
    sector, channels, _ = own.shape
    lay_out(place, sector, (own, partner, edge), theirs, wedges)

    pitch = rows + SLACK

    def one_cell(cell, _):
        start = begins[cell]
        shares = probs_t[pl.ds(start, TAPS)].reshape(TAPS * rows, LANES)
        result = product(shares.astype(BF16), wedges[cell], 1, 1)
        for k in range(TAPS):
            span = pl.ds(pl.multiple_of((start + k) * pitch, 8), rows)
            wide[span, 0:channels] = result[k * rows : (k + 1) * rows]
        return 0

    lax.fori_loop(0, wedges.shape[0], one_cell, 0, unroll=8)
    one = lax.broadcasted_iota(jnp.int32, (channels, channels), 0)
    same = (one == lax.broadcasted_iota(jnp.int32, (channels, channels), 1)).astype(F32)
    same = same.astype(BF16)

    def turn(row, _):
        block = wide[pl.ds(row, columns, stride=pitch), :][:, :channels].astype(BF16)
        apart[pl.ds(row, channels, stride=pitch), :] = product(same, block, 1, 1)
        return 0

    lax.fori_loop(0, rows, turn, 0, unroll=8)
    for level in range(channels):
        block = apart[level * pitch : level * pitch + rows, :]
        context_grad[level * rows : (level + 1) * rows, :] = block.astype(BF16)


def vmem():
    return pl.BlockSpec(memory_space=pltpu.VMEM)


def smem():
    return pl.BlockSpec(memory_space=pltpu.SMEM)


def anywhere():
    return pl.BlockSpec(memory_space=pltpu.HBM)


def call(kernel, out_shape, scratch, spaces, flops, moved, outs=None, limit=16):
    many = isinstance(out_shape, (list, tuple))
    return pl.pallas_call(
        kernel,
        out_shape=out_shape,
        in_specs=spaces,
        out_specs=outs or ([vmem() for _ in out_shape] if many else vmem()),
        scratch_shapes=scratch,
        compiler_params=pltpu.CompilerParams(vmem_limit_bytes=limit * 1024 * 1024),
        cost_estimate=pl.CostEstimate(flops=flops, bytes_accessed=moved, transcendentals=0),
    )


def rounded_sum(left, right):
    return (left.astype(F32) + right.astype(F32)).astype(BF16)


def swapped(value, blocks, mask):
    return lax.ppermute(value, "blk", [(i, i ^ mask) for i in range(blocks)])


def piece(value, index, count):
    size = value.shape[0] // count
    return lax.dynamic_slice_in_dim(value, index * size, size, 0)


def axis_orders(count):
    pairs = list(range(1, count, 2))
    return pairs, pairs[1:] + pairs[:1]


def total_over_blocks(keep, send, position, blocks):
    count = blocks.bit_length() - 1
    orders = axis_orders(count)
    core = position & 1
    digits = [
        jnp.where(core == 0, position >> one, position >> two) & 3 for one, two in zip(*orders)
    ]

    def sent(part, step, mask):
        to = [(i, i ^ (mask << orders[i & 1][step])) for i in range(blocks)]
        return lax.ppermute(part, "blk", to)

    value = rounded_sum(keep, swapped(send, blocks, 1))
    for step, digit in enumerate(digits):
        leaving = [piece(value, digit ^ mask, 4) for mask in (3, 1, 2)]
        arrived = [sent(part, step, mask) for part, mask in zip(leaving, (3, 1, 2))]
        total = piece(value, digit, 4).astype(F32)
        for part in arrived:
            total = total + part.astype(F32)
        value = total.astype(BF16)
    for step, digit in reversed(list(enumerate(digits))):
        held = [value] + [sent(value, step, mask) for mask in (1, 2, 3)]
        if step == 0:
            value = jnp.concatenate(held, axis=0)
            break
        high, low = digit >> 1 == 1, digit & 1 == 1

        def at(k):
            one = jnp.where(low, held[k ^ 1], held[k])
            two = jnp.where(low, held[k ^ 3], held[k ^ 2])
            return jnp.where(high, two, one)

        value = jnp.concatenate([at(k) for k in range(4)], axis=0)
    return value, swapped(value, blocks, 1)


def shards(
    depth_logits, context, lidar_bins, az_map, rng_map, conv1_weight, conv2_weight, out_grad
):
    blocks = lax.axis_size("blk")
    position = lax.axis_index("blk")
    cameras, columns = az_map.shape
    bands = blocks // cameras
    sector, length, hidden = out_grad.shape
    bins, rows = depth_logits.shape[1:3]
    channels = context.shape[1]
    if bands != 4 or blocks != 1 << (blocks.bit_length() - 1) or blocks.bit_length() % 2 or bins > LANES or channels > LANES or sector < 6 or sector % 2:
        raise ValueError("unsupported sizes")
    band = position % bands
    sight = bands * sector
    seen = sight + sight // 2

    core = position & 1
    place = position.reshape(1)
    on_chip = [(i, i ^ 1) for i in range(blocks)]
    off_chip = [(i, (i + 1 if i & 1 else i - 1) % blocks) for i in range(blocks)]

    def ends(value, near):
        return jnp.where((core == 0) == near, value[-2:], value[:2])

    far_grad = lax.ppermute(ends(out_grad, False), "blk", off_chip)
    near_grad = lax.ppermute(ends(out_grad, True), "blk", on_chip)

    turned = (columns + 1) * (rows + SLACK)
    half = 3 * sector
    probs, probs_t, context_t, kept, sent, begins = call(
        functools.partial(pool_kernel, rows, sight, blocks * sector),
        [
            jax.ShapeDtypeStruct((bins * rows, columns), F32),
            jax.ShapeDtypeStruct((columns + 1, rows, LANES), F32),
            jax.ShapeDtypeStruct((columns + 1, rows, LANES), F32),
            jax.ShapeDtypeStruct((half, channels, LANES), BF16),
            jax.ShapeDtypeStruct((half, channels, LANES), BF16),
            jax.ShapeDtypeStruct((seen + 1,), jnp.int32),
        ],
        [
            pltpu.VMEM((bins * rows, columns), F32),
            pltpu.VMEM(((bins + 1) * (rows + SLACK), columns), F32),
            pltpu.VMEM(((channels + 1) * (rows + SLACK), columns), F32),
            pltpu.VMEM((turned, LANES), F32),
            pltpu.VMEM((turned, LANES), F32),
            pltpu.SemaphoreType.DMA((3,)),
        ],
        [smem(), smem(), vmem(), vmem()],
        2 * seen * 3 * rows * LANES * LANES,
        20 * bins * rows * columns,
        [anywhere()] * 3 + [vmem()] * 2 + [smem()],
        limit=56,
    )(
        place,
        az_map,
        depth_logits[0].reshape(bins * rows, columns),
        context[0].reshape(channels * rows, columns),
    )

    row_flops = 2 * TAPS * TAPS * hidden * hidden * length

    inner_grad = call(
        inner_acts_kernel,
        jax.ShapeDtypeStruct((sector - 3, hidden, length), BF16),
        [],
        [vmem()] * 2,
        row_flops * (sector - 3),
        4 * sector * length * hidden,
    )(out_grad, conv2_weight)
    weight = conv1_weight.reshape(TAPS, TAPS * channels, hidden)
    act_grads, weight_t, range_hot = call(
        outer_acts_kernel,
        [
            jax.ShapeDtypeStruct((sector + 2, hidden, length), BF16),
            jax.ShapeDtypeStruct((TAPS * hidden, TAPS * channels), BF16),
            jax.ShapeDtypeStruct((length, 2 * LANES), BF16),
        ],
        [pltpu.VMEM((4, length, hidden), BF16)] * 2 + [pltpu.VMEM((8, 2 * LANES), jnp.int32)],
        [smem()] + [vmem()] * 7,
        row_flops * 5,
        16 * length * hidden,
    )(place, near_grad, far_grad, out_grad, conv2_weight, inner_grad, weight, rng_map)

    summed = rounded_sum(kept, swapped(sent, blocks, 1))
    own = rounded_sum(summed[:sector], swapped(summed[sector : 2 * sector], blocks, 2))
    inward = [(i, i ^ 2) for i in range(blocks) if i % bands in (1, 2)]
    outward = [(i ^ 2, i) for i in range(blocks) if i % bands in (1, 2)]
    edge = rounded_sum(
        summed[2 * sector :], lax.ppermute(summed[2 * sector :], "blk", inward)
    )
    first = band == 0
    firsts = [i for i in range(blocks) if i % bands == 0]
    lasts = [i for i in range(blocks) if i % bands == bands - 1]
    last = band == bands - 1
    outer = jnp.logical_or(first, last)
    more = ((0, sector), (0, 0), (0, 0))
    far = jnp.where(
        first,
        jnp.concatenate([edge, own[:2]], axis=0),
        jnp.where(
            last,
            jnp.concatenate([own[sector - 2 :], edge], axis=0),
            jnp.pad(ends(own, False), more),
        ),
    )

    def to_next(value):
        pairs = [(i, (i - 1) % blocks) for i in firsts]
        pairs = pairs + [(i, (i + 1) % blocks) for i in lasts]
        return lax.ppermute(value, "blk", pairs)

    far_halo = lax.ppermute(far, "blk", off_chip)
    passed = jnp.where(first, far_halo[sector:], far_halo[:2])
    near_halo = lax.ppermute(
        jnp.concatenate([ends(own, True), passed], axis=0), "blk", on_chip
    )
    grad_rows = TAPS * TAPS * (hidden + channels)
    unit = blocks * 16
    grad_rows = -(-grad_rows // unit) * unit
    wide = sector + 2
    keep, send, own_reply, other_reply = call(
        grid_kernel,
        [
            jax.ShapeDtypeStruct((grad_rows // 2, hidden), BF16),
            jax.ShapeDtypeStruct((grad_rows // 2, hidden), BF16),
            jax.ShapeDtypeStruct((sector, channels, LANES), BF16),
            jax.ShapeDtypeStruct((sector, channels, LANES), BF16),
        ],
        [
            pltpu.VMEM((sector + 4, channels, 2 * LANES), BF16),
            pltpu.VMEM(((sector + 4) * channels, length), BF16),
            pltpu.VMEM((TAPS * channels, wide * length), BF16),
            pltpu.VMEM((TAPS * hidden, wide * length), BF16),
            pltpu.VMEM((wide * hidden, length), BF16),
            pltpu.VMEM((hidden, wide * length), BF16),
            pltpu.VMEM((sector * channels, length), BF16),
            pltpu.VMEM((grad_rows, hidden), BF16),
            pltpu.VMEM((TAPS * hidden, length), F32),
            pltpu.VMEM((TAPS * hidden, length), F32),
        ],
        [smem()] + [vmem()] * 9,
        row_flops * (sector + 3 * sector // 2),
        20 * sector * length * hidden,
        limit=32,
    )(
        place,
        own,
        edge,
        near_halo,
        far_halo,
        weight,
        weight_t,
        range_hot,
        act_grads,
        out_grad.reshape(sector * length, hidden),
    )

    partner = swapped(own_reply, blocks, 2)
    edge_reply = to_next(other_reply)
    passed = lax.ppermute(edge_reply, "blk", outward)
    edge_reply = jnp.where(outer, edge_reply, passed)
    theirs = swapped(
        jnp.concatenate([own_reply, partner, edge_reply], axis=0), blocks, 1
    )
    value, other_value = total_over_blocks(keep, send, position, blocks)

    replies = (own_reply, partner, edge_reply, theirs)
    scratch = [pltpu.VMEM((seen, channels, LANES), BF16), pltpu.VMEM((turned, LANES), F32)]
    cell_flops = 2 * seen * 3 * rows * LANES * LANES
    context_grad = call(
        functools.partial(context_kernel, rows),
        jax.ShapeDtypeStruct((channels * rows, columns), BF16),
        scratch + [pltpu.VMEM(((channels + 1) * (rows + SLACK), columns), F32)],
        [smem()] * 2 + [vmem()] * 5,
        cell_flops,
        10 * bins * rows * columns,
    )(place, begins, *replies, probs_t)
    logit_grad = call(
        functools.partial(logit_kernel, rows),
        jax.ShapeDtypeStruct((bins * rows, columns), F32),
        scratch + [pltpu.VMEM(((bins + 1) * (rows + SLACK), columns), F32)],
        [smem()] * 2 + [vmem()] * 7,
        cell_flops,
        20 * bins * rows * columns,
    )(place, begins, *replies, probs, context_t, lidar_bins[0])

    second = TAPS * TAPS * hidden
    first_rows = TAPS * TAPS * channels
    second_grad, first_grad = call(
        functools.partial(
            finish_kernel, [order[0] for order in axis_orders(blocks.bit_length() - 1)]
        ),
        [
            jax.ShapeDtypeStruct((second, hidden), F32),
            jax.ShapeDtypeStruct((first_rows, hidden), F32),
        ],
        [pltpu.VMEM((grad_rows, hidden), BF16)],
        [smem(), vmem(), vmem()],
        1,
        6 * grad_rows * hidden,
    )(place, value, other_value)
    return (
        logit_grad.reshape(1, bins, rows, columns),
        context_grad.reshape(1, channels, rows, columns),
        first_grad.reshape(TAPS, TAPS, channels, hidden),
        second_grad.reshape(TAPS, TAPS, hidden, hidden),
    )


def solution(mesh):
    return jax.shard_map(
        shards,
        mesh=mesh,
        in_specs=(
            P(("group", "blk"), None, None, None),
            P(("group", "blk"), None, None, None),
            P(("group", "blk"), None, None),
            P(),
            P(),
            P(),
            P(),
            P(("group", "blk"), None, None),
        ),
        out_specs=(
            P(("group", "blk"), None, None, None),
            P(("group", "blk"), None, None, None),
            P("group", None, None, None),
            P("group", None, None, None),
        ),
        check_vma=False,
    )
```

```python
import functools

import jax
import jax.numpy as jnp
from jax import lax
from jax.experimental import pallas as pl
from jax.experimental.pallas import tpu as pltpu
from jax.sharding import PartitionSpec as P

DEPTH_WEIGHT = 3.0
TAPS = 3
LANES = 128
SLACK = 8
F32 = jnp.float32
BF16 = jnp.bfloat16


def product(left, right, left_dim, right_dim):
    return lax.dot_general(
        left, right, (((left_dim,), (right_dim,)), ((), ())), preferred_element_type=F32
    )


def padded_rows(value, rows):
    missing = rows - value.shape[0]
    if missing == 0:
        return value
    return jnp.concatenate([value, jnp.zeros((missing, value.shape[1]), value.dtype)], axis=0)


def sectors_of(band, bands):
    partner = (band + 2) % bands
    return 1 + band, 1 + partner, (bands + 1) * (band % 2)


def pool_kernel(
    rows,
    sight,
    around,
    place,
    az_map,
    logits,
    context,
    probs_out,
    probs_t_out,
    context_t_out,
    kept,
    sent,
    begins,
    probs,
    apart_p,
    apart_c,
    wide_p,
    wide_c,
    done,
):
    columns = logits.shape[1]
    bins = logits.shape[0] // rows
    channels = context.shape[0] // rows
    half = kept.shape[0]
    sector = half // 3
    bands = 4
    position = place[0]
    band, camera = position % bands, position // bands
    seen = 2 * half
    begins[seen] = columns
    scores = logits[...].reshape(bins, rows, columns)
    powers = jnp.exp(scores - jnp.max(scores, axis=0, keepdims=True))
    shares = powers / jnp.sum(powers, axis=0, keepdims=True)
    probs[...] = shares.reshape(bins * rows, columns)
    copies = [pltpu.make_async_copy(probs, probs_out, done.at[0])]
    copies[0].start()
    pitch = rows + SLACK
    for level in range(bins):
        apart_p[level * pitch : level * pitch + rows, :] = shares[level]
    for level in range(channels):
        features = context[level * rows : (level + 1) * rows, :]
        apart_c[level * pitch : level * pitch + rows, :] = features.astype(F32)
    one = lax.broadcasted_iota(jnp.int32, (columns, columns), 0)
    same = (one == lax.broadcasted_iota(jnp.int32, (columns, columns), 1)).astype(F32)
    same = same.astype(BF16)

    def turn(row, _):
        for k in range(columns // rows):
            column = columns - 1 - row * (columns // rows) - k
            cell = az_map[camera, column] - camera * sight + sight // 4
            cell = jnp.where(cell < 0, cell + around, cell)
            begins[jnp.where(cell >= around, cell - around, cell)] = column
        block = padded_rows(apart_p[pl.ds(row, bins, stride=pitch), :], LANES)
        wide_p[pl.ds(row, columns, stride=pitch), :] = jnp.transpose(block)
        block = padded_rows(apart_c[pl.ds(row, channels, stride=pitch), :].astype(BF16), LANES)
        wide_c[pl.ds(row, columns, stride=pitch), :] = product(same, block, 1, 1)
        return 0

    lax.fori_loop(0, rows, turn, 0, unroll=8)
    for wide, out in ((wide_p, probs_t_out), (wide_c, context_t_out)):
        wide[columns * pitch :, :] = jnp.zeros((pitch, LANES), F32)
        source = wide.reshape(columns + 1, pitch, LANES).at[:, 0:rows, :]
        copies.append(pltpu.make_async_copy(source, out, done.at[len(copies)]))
        copies[-1].start()
    line = lax.broadcasted_iota(jnp.int32, (TAPS * rows, LANES), 0)

    def cell_sum(cell):
        start = begins[cell]
        spans = [pl.ds(pl.multiple_of((start + k) * pitch, 8), rows) for k in range(TAPS)]
        features = jnp.concatenate([wide_c[span, :] for span in spans], axis=0)
        shares = jnp.concatenate([wide_p[span, :] for span in spans], axis=0)
        width = (begins[cell + 1] - start) * rows
        features = jnp.where(line < width, features, 0.0).astype(BF16)
        return product(features, shares.astype(BF16), 0, 0)[:channels].astype(BF16)

    near = band + 1 - 2 * (band % 2)
    for group, (mine, theirs) in enumerate(
        zip(sectors_of(band, bands), sectors_of(near, bands))
    ):

        def one_cell(step, _, group=group, mine=mine, theirs=theirs):
            sent[group * sector + step] = cell_sum(theirs * sector + step)
            kept[group * sector + step] = cell_sum(mine * sector + step)
            return 0

        lax.fori_loop(0, sector, one_cell, 0, unroll=4)
    for copy in copies:
        copy.wait()


def act_row(taps, source, start, out, row):
    hidden, length = out.shape[1:]
    stacked = jnp.concatenate([source[start + i] for i in range(TAPS)], axis=1)
    sums = product(taps, stacked, 1, 1)
    place = lax.broadcasted_iota(jnp.int32, (hidden, length), 1)
    ahead = pltpu.roll(sums[:hidden], length - 1, 1)
    behind = pltpu.roll(sums[2 * hidden :], 1, 1)
    total = sums[hidden : 2 * hidden]
    total = total + jnp.where(place < length - 1, ahead, 0.0)
    total = total + jnp.where(place > 0, behind, 0.0)
    out[row] = total.astype(BF16)


def act_taps_of(weight):
    hidden = weight.shape[3]
    return jnp.concatenate(
        [weight[TAPS - 1 - i].reshape(TAPS * hidden, hidden) for i in range(TAPS)], axis=1
    )


def inner_acts_kernel(upstream, weight, out):
    def step(row, _):
        act_row(act_taps_of(weight), upstream, row, out, row)
        return 0

    lax.fori_loop(0, out.shape[0], step, 0)


def outer_acts_kernel(
    place,
    near,
    far,
    upstream,
    weight,
    inner,
    first_weight,
    ranges,
    out,
    weight_t,
    range_hot,
    low,
    high,
    picks,
):
    sector, length, hidden = upstream.shape
    bands = 4
    cameras, bins = ranges.shape
    channels = first_weight.shape[1] // TAPS
    lanes = range_hot.shape[1] // 2
    mine, camera = place[0] % bands, place[0] // bands
    other = jnp.where(mine < bands // 2, camera + cameras - 1, camera + 1) % cameras
    picks[...] = jnp.full(picks.shape, -1, jnp.int32)
    picks[0:1, 0:bins] = ranges[pl.ds(camera, 1), :]
    picks[0:1, lanes : lanes + bins] = ranges[pl.ds(other, 1), :]
    spots = lax.broadcasted_iota(jnp.int32, (length, 2 * lanes), 0)
    range_hot[...] = (spots == picks[0:1, :]).astype(F32).astype(BF16)
    for column in range(TAPS):
        for row in range(TAPS):
            weight_t[column * hidden : (column + 1) * hidden, row * channels : (row + 1) * channels] = (
                jnp.transpose(
                    first_weight[row, column * channels : (column + 1) * channels, :].astype(F32)
                ).astype(BF16)
            )
    ready = inner.shape[0]
    out[2 : 2 + ready] = inner[...]
    low[2:4] = upstream[0:2]
    high[0:2] = upstream[sector - 2 :]

    @pl.when(place[0] % 2 == 0)
    def _():
        low[0:2] = far[...]
        high[2:4] = near[...]

    @pl.when(place[0] % 2 == 1)
    def _():
        low[0:2] = near[...]
        high[2:4] = far[...]

    def step(row, _):
        act_row(act_taps_of(weight), low, row, out, row)
        act_row(act_taps_of(weight), high, row, out, row + sector)
        return 0

    def more(row, _):
        act_row(act_taps_of(weight), upstream, row, out, row + 2)
        return 0

    lax.fori_loop(0, 2, step, 0)
    lax.fori_loop(ready, sector - 2, more, 0)


def grid_kernel(
    place,
    own,
    edge,
    near_halo,
    far_halo,
    weight,
    weight_t,
    range_hot,
    act_grads,
    upstream,
    keep,
    send,
    own_reply,
    other_reply,
    cells,
    grid_low,
    grid_taps,
    act_taps,
    slope_rows,
    slope_lanes,
    grid_grad,
    grads,
    sums_a,
    sums_b,
):
    sector, channels, lanes = own.shape
    hidden, length = act_grads.shape[1:]
    bands = 4
    position = place[0]
    mine, core = position % bands, position % 2
    wide = sector + 4
    cells[2 : 2 + sector, :, :lanes] = own[...]
    cells[:, :, lanes:] = jnp.zeros((wide, channels, lanes), BF16)

    @pl.when(mine == 0)
    def _():
        cells[0:2, :, :lanes] = edge[sector - 2 : sector]
        cells[2 + sector :, :, :lanes] = near_halo[0:2]
        cells[0 : sector + 2, :, lanes:] = far_halo[...]

    @pl.when(mine == 1)
    def _():
        cells[0:2, :, :lanes] = near_halo[0:2]
        cells[2 + sector :, :, :lanes] = far_halo[0:2]
        cells[0:2, :, lanes:] = near_halo[2:4]

    @pl.when(mine == bands - 2)
    def _():
        cells[0:2, :, :lanes] = far_halo[0:2]
        cells[2 + sector :, :, :lanes] = near_halo[0:2]
        cells[2 + sector :, :, lanes:] = near_halo[2:4]

    @pl.when(mine == bands - 1)
    def _():
        cells[0:2, :, :lanes] = near_halo[0:2]
        cells[2 + sector :, :, :lanes] = edge[0:2]
        cells[2:, :, lanes:] = far_halo[...]

    def behind(value):
        turned = pltpu.roll(value, 1, 1)
        lane = lax.broadcasted_iota(jnp.int32, (value.shape[0], LANES), 1)
        first = jnp.where(lane > 0, turned[:, :LANES], 0.0)
        return jnp.concatenate([first, turned[:, LANES:]], axis=1)

    def ahead(value):
        turned = pltpu.roll(value, length - 1, 1)
        lane = lax.broadcasted_iota(jnp.int32, (value.shape[0], LANES), 1)
        last = jnp.where(lane < LANES - 1, turned[:, length - LANES :], 0.0)
        return jnp.concatenate([turned[:, : length - LANES], last], axis=1)

    for chunk in range(0, wide, 4):
        block = cells[chunk : chunk + 4].reshape(4 * channels, 2 * lanes)
        summed = product(block, range_hot[...], 1, 1)
        for row in range(chunk, chunk + 4):
            value = summed[(row - chunk) * channels : (row - chunk + 1) * channels]
            grid_low[row * channels : (row + 1) * channels, :] = value.astype(BF16)
            if 0 < row < wide - 1:
                spread = pl.ds((row - 1) * length, length)
                grid_taps[0:channels, spread] = behind(value).astype(BF16)
                grid_taps[channels : 2 * channels, spread] = value.astype(BF16)
                grid_taps[2 * channels :, spread] = ahead(value).astype(BF16)

    flipped = jnp.concatenate([weight[TAPS - 1 - i] for i in range(TAPS)], axis=1)

    def convolved(row, into):
        source = pl.ds(pl.multiple_of(row * channels, channels), TAPS * channels)
        into[...] = product(weight_t[...], grid_low[source, :], 1, 0)

    def back(row):
        source = pl.ds(pl.multiple_of(row * hidden, hidden), TAPS * hidden)
        sums = product(flipped, slope_rows[source, :], 1, 0)
        value = ahead(sums[:channels]) + sums[channels : 2 * channels]
        value = value + behind(sums[2 * channels :])
        grid_grad[pl.ds(pl.multiple_of(row * channels, channels), channels), :] = value.astype(BF16)

    def activated(row, sums):
        value = behind(sums[:hidden, :]) + sums[hidden : 2 * hidden, :]
        value = value + ahead(sums[2 * hidden :, :])
        logistic = 0.5 + 0.5 * jnp.tanh(0.5 * value)
        active = value * logistic
        start = pl.multiple_of(row * length, length)
        spread = pl.ds(start, length)
        low = active.astype(BF16)
        act_taps[0:hidden, spread] = pltpu.roll(low, 1, 1)
        act_taps[hidden : 2 * hidden, spread] = low
        act_taps[2 * hidden :, spread] = pltpu.roll(low, length - 1, 1)
        nothing = jnp.zeros((hidden, LANES), BF16)
        lane = lax.broadcasted_iota(jnp.int32, (hidden, LANES), 1)
        first = pl.ds(start, LANES)
        act_taps[0:hidden, first] = jnp.where(lane > 0, act_taps[0:hidden, first], nothing)
        last = pl.ds(pl.multiple_of(start + length - LANES, LANES), LANES)
        act_taps[2 * hidden :, last] = jnp.where(
            lane < LANES - 1, act_taps[2 * hidden :, last], nothing
        )
        slope = logistic * (1.0 + value * (1.0 - logistic))
        result = (act_grads[row].astype(F32) * slope).astype(BF16)
        slope_rows[pl.ds(pl.multiple_of(row * hidden, hidden), hidden), :] = result
        slope_lanes[:, spread] = result

    rows = sector + 2
    slope_rows[0 : 3 * hidden, :] = jnp.zeros((3 * hidden, length), BF16)

    def two_rows(pair, _):
        row = 2 * pair
        back(jnp.maximum(row - 3, 0))
        convolved(row + 1, sums_b)
        activated(row, sums_a)
        back(jnp.maximum(row - 2, 0))
        convolved(jnp.minimum(row + 2, rows - 1), sums_a)
        activated(row + 1, sums_b)
        return 0

    convolved(0, sums_a)
    lax.fori_loop(0, rows // 2, two_rows, 0)
    back(sector - 1)
    count = sector * length
    tall = TAPS * hidden
    short = TAPS * channels

    def second(tap, _):
        window = pl.ds(pl.multiple_of(tap * length, length), count)
        result = product(act_taps[:, window], upstream[...], 1, 0)
        grads[pl.ds(pl.multiple_of(tap * tall, tall), tall), :] = result.astype(BF16)
        return 0

    lax.fori_loop(0, TAPS, second, 0)
    windows = [grid_taps[:, tap * length : tap * length + count] for tap in range(TAPS)]
    result = product(
        jnp.concatenate(windows, axis=0), slope_lanes[:, length : length + count], 1, 1
    )
    grads[TAPS * tall : TAPS * (tall + short), :] = result.astype(BF16)
    base = TAPS * (tall + short)
    grads[base:, :] = jnp.zeros((grads.shape[0] - base, hidden), BF16)
    half = keep.shape[0]
    keep[...] = grads[pl.ds(pl.multiple_of(core * half, half), half), :]
    send[...] = grads[pl.ds(pl.multiple_of((1 - core) * half, half), half), :]
    picked = product(grid_grad[...], range_hot[...], 1, 0).astype(BF16)
    own_reply[...] = picked[:, :lanes].reshape(sector, channels, lanes)
    other_reply[...] = picked[:, lanes:].reshape(sector, channels, lanes)


def finish_kernel(shifts, place, value, other, second, first, total):
    half = value.shape[0]
    size = half // 4
    position = place[0]
    core = position % 2
    for source, side in ((value, core), (other, 1 - core)):
        digit = jnp.where(side == 0, position >> shifts[0], position >> shifts[1]) & 3
        for mask in range(4):
            spot = side * half + (digit ^ mask) * size
            total[pl.ds(pl.multiple_of(spot, size), size), :] = source[
                mask * size : (mask + 1) * size, :
            ]
    count = second.shape[0]
    second[...] = total[0:count, :].astype(F32)
    first[...] = total[count : count + first.shape[0], :].astype(F32)


def lay_out(place, sector, mine, theirs, wedges):
    bands = 4
    band = place[0] % bands
    near = band + 1 - 2 * (band % 2)
    for group, spot in enumerate(sectors_of(band, bands)):
        wedges[pl.ds(spot * sector, sector)] = mine[group][...]
    for group, spot in enumerate(sectors_of(near, bands)):
        wedges[pl.ds(spot * sector, sector)] = theirs[group * sector : (group + 1) * sector]


def logit_kernel(
    rows,
    place,
    begins,
    own,
    partner,
    edge,
    theirs,
    probs,
    context_t,
    lidar,
    logit_grad,
    wedges,
    wide,
    apart,
):
    columns = probs.shape[1]
    bins = probs.shape[0] // rows
    sector, channels, _ = own.shape
    lay_out(place, sector, (own, partner, edge), theirs, wedges)

    pitch = rows + SLACK

    def one_cell(cell, _):
        start = begins[cell]
        features = context_t[pl.ds(start, TAPS)].reshape(TAPS * rows, LANES)
        result = product(features[:, :channels].astype(BF16), wedges[cell], 1, 0)
        for k in range(TAPS):
            span = pl.ds(pl.multiple_of((start + k) * pitch, 8), rows)
            wide[span, :] = result[k * rows : (k + 1) * rows]
        return 0

    lax.fori_loop(0, wedges.shape[0], one_cell, 0, unroll=8)

    def turn(row, _):
        block = jnp.transpose(wide[pl.ds(row, columns, stride=pitch), :])
        apart[pl.ds(row, bins, stride=pitch), :] = block[:bins]
        return 0

    lax.fori_loop(0, rows, turn, 0, unroll=8)
    sums = [jnp.zeros((rows, columns), F32) for _ in range(4)]
    for level in range(bins):
        share = probs[level * rows : (level + 1) * rows, :]
        sums[level % 4] += share * apart[level * pitch : level * pitch + rows, :]
    expected = (sums[0] + sums[1]) + (sums[2] + sums[3])
    target = lidar[...]
    seen = jnp.where(target >= 0, DEPTH_WEIGHT, 0.0)
    for level in range(bins):
        share = probs[level * rows : (level + 1) * rows, :]
        slope = apart[level * pitch : level * pitch + rows, :]
        hit = jnp.where(target == level, DEPTH_WEIGHT, 0.0)
        result = share * (slope - expected) + (seen * share - hit)
        logit_grad[level * rows : (level + 1) * rows, :] = result


def context_kernel(
    rows,
    place,
    begins,
    own,
    partner,
    edge,
    theirs,
    probs_t,
    context_grad,
    wedges,
    wide,
    apart,
):
    columns = context_grad.shape[1]
    sector, channels, _ = own.shape
    lay_out(place, sector, (own, partner, edge), theirs, wedges)

    pitch = rows + SLACK

    def one_cell(cell, _):
        start = begins[cell]
        shares = probs_t[pl.ds(start, TAPS)].reshape(TAPS * rows, LANES)
        result = product(shares.astype(BF16), wedges[cell], 1, 1)
        for k in range(TAPS):
            span = pl.ds(pl.multiple_of((start + k) * pitch, 8), rows)
            wide[span, 0:channels] = result[k * rows : (k + 1) * rows]
        return 0

    lax.fori_loop(0, wedges.shape[0], one_cell, 0, unroll=8)
    one = lax.broadcasted_iota(jnp.int32, (channels, channels), 0)
    same = (one == lax.broadcasted_iota(jnp.int32, (channels, channels), 1)).astype(F32)
    same = same.astype(BF16)

    def turn(row, _):
        block = wide[pl.ds(row, columns, stride=pitch), :][:, :channels].astype(BF16)
        apart[pl.ds(row, channels, stride=pitch), :] = product(same, block, 1, 1)
        return 0

    lax.fori_loop(0, rows, turn, 0, unroll=8)
    for level in range(channels):
        block = apart[level * pitch : level * pitch + rows, :]
        context_grad[level * rows : (level + 1) * rows, :] = block.astype(BF16)


def vmem():
    return pl.BlockSpec(memory_space=pltpu.VMEM)


def smem():
    return pl.BlockSpec(memory_space=pltpu.SMEM)


def anywhere():
    return pl.BlockSpec(memory_space=pltpu.HBM)


def call(kernel, out_shape, scratch, spaces, flops, moved, outs=None, limit=16):
    many = isinstance(out_shape, (list, tuple))
    return pl.pallas_call(
        kernel,
        out_shape=out_shape,
        in_specs=spaces,
        out_specs=outs or ([vmem() for _ in out_shape] if many else vmem()),
        scratch_shapes=scratch,
        compiler_params=pltpu.CompilerParams(vmem_limit_bytes=limit * 1024 * 1024),
        cost_estimate=pl.CostEstimate(flops=flops, bytes_accessed=moved, transcendentals=0),
    )


def rounded_sum(left, right):
    return (left.astype(F32) + right.astype(F32)).astype(BF16)


def swapped(value, blocks, mask):
    return lax.ppermute(value, "blk", [(i, i ^ mask) for i in range(blocks)])


def piece(value, index, count):
    size = value.shape[0] // count
    return lax.dynamic_slice_in_dim(value, index * size, size, 0)


def axis_orders(count):
    pairs = list(range(1, count, 2))
    return pairs, pairs[1:] + pairs[:1]


def total_over_blocks(keep, send, position, blocks):
    count = blocks.bit_length() - 1
    orders = axis_orders(count)
    core = position & 1
    digits = [
        jnp.where(core == 0, position >> one, position >> two) & 3 for one, two in zip(*orders)
    ]

    def sent(part, step, mask):
        to = [(i, i ^ (mask << orders[i & 1][step])) for i in range(blocks)]
        return lax.ppermute(part, "blk", to)

    value = rounded_sum(keep, swapped(send, blocks, 1))
    for step, digit in enumerate(digits):
        leaving = [piece(value, digit ^ mask, 4) for mask in (3, 1, 2)]
        arrived = [sent(part, step, mask) for part, mask in zip(leaving, (3, 1, 2))]
        total = piece(value, digit, 4).astype(F32)
        for part in arrived:
            total = total + part.astype(F32)
        value = total.astype(BF16)
    for step, digit in reversed(list(enumerate(digits))):
        held = [value] + [sent(value, step, mask) for mask in (1, 2, 3)]
        if step == 0:
            value = jnp.concatenate(held, axis=0)
            break
        high, low = digit >> 1 == 1, digit & 1 == 1

        def at(k):
            one = jnp.where(low, held[k ^ 1], held[k])
            two = jnp.where(low, held[k ^ 3], held[k ^ 2])
            return jnp.where(high, two, one)

        value = jnp.concatenate([at(k) for k in range(4)], axis=0)
    return value, swapped(value, blocks, 1)


def shards(
    depth_logits, context, lidar_bins, az_map, rng_map, conv1_weight, conv2_weight, out_grad
):
    blocks = lax.axis_size("blk")
    position = lax.axis_index("blk")
    cameras, columns = az_map.shape
    bands = blocks // cameras
    sector, length, hidden = out_grad.shape
    bins, rows = depth_logits.shape[1:3]
    channels = context.shape[1]
    if bands != 4 or blocks != 1 << (blocks.bit_length() - 1) or blocks.bit_length() % 2 or bins > LANES or channels > LANES or sector < 6 or sector % 2:
        raise ValueError("unsupported sizes")
    band = position % bands
    sight = bands * sector
    seen = sight + sight // 2

    core = position & 1
    place = position.reshape(1)
    on_chip = [(i, i ^ 1) for i in range(blocks)]
    off_chip = [(i, (i + 1 if i & 1 else i - 1) % blocks) for i in range(blocks)]

    def ends(value, near):
        return jnp.where((core == 0) == near, value[-2:], value[:2])

    far_grad = lax.ppermute(ends(out_grad, False), "blk", off_chip)
    near_grad = lax.ppermute(ends(out_grad, True), "blk", on_chip)

    turned = (columns + 1) * (rows + SLACK)
    half = 3 * sector
    probs, probs_t, context_t, kept, sent, begins = call(
        functools.partial(pool_kernel, rows, sight, blocks * sector),
        [
            jax.ShapeDtypeStruct((bins * rows, columns), F32),
            jax.ShapeDtypeStruct((columns + 1, rows, LANES), F32),
            jax.ShapeDtypeStruct((columns + 1, rows, LANES), F32),
            jax.ShapeDtypeStruct((half, channels, LANES), BF16),
            jax.ShapeDtypeStruct((half, channels, LANES), BF16),
            jax.ShapeDtypeStruct((seen + 1,), jnp.int32),
        ],
        [
            pltpu.VMEM((bins * rows, columns), F32),
            pltpu.VMEM(((bins + 1) * (rows + SLACK), columns), F32),
            pltpu.VMEM(((channels + 1) * (rows + SLACK), columns), F32),
            pltpu.VMEM((turned, LANES), F32),
            pltpu.VMEM((turned, LANES), F32),
            pltpu.SemaphoreType.DMA((3,)),
        ],
        [smem(), smem(), vmem(), vmem()],
        2 * seen * 3 * rows * LANES * LANES,
        20 * bins * rows * columns,
        [anywhere()] * 3 + [vmem()] * 2 + [smem()],
        limit=56,
    )(
        place,
        az_map,
        depth_logits[0].reshape(bins * rows, columns),
        context[0].reshape(channels * rows, columns),
    )

    row_flops = 2 * TAPS * TAPS * hidden * hidden * length

    inner_grad = call(
        inner_acts_kernel,
        jax.ShapeDtypeStruct((sector - 3, hidden, length), BF16),
        [],
        [vmem()] * 2,
        row_flops * (sector - 3),
        4 * sector * length * hidden,
    )(out_grad, conv2_weight)
    weight = conv1_weight.reshape(TAPS, TAPS * channels, hidden)
    act_grads, weight_t, range_hot = call(
        outer_acts_kernel,
        [
            jax.ShapeDtypeStruct((sector + 2, hidden, length), BF16),
            jax.ShapeDtypeStruct((TAPS * hidden, TAPS * channels), BF16),
            jax.ShapeDtypeStruct((length, 2 * LANES), BF16),
        ],
        [pltpu.VMEM((4, length, hidden), BF16)] * 2 + [pltpu.VMEM((8, 2 * LANES), jnp.int32)],
        [smem()] + [vmem()] * 7,
        row_flops * 5,
        16 * length * hidden,
    )(place, near_grad, far_grad, out_grad, conv2_weight, inner_grad, weight, rng_map)

    arrived = swapped(sent, blocks, 1)
    summed = rounded_sum(kept[sector:], arrived[sector:])
    other_pair = swapped(summed[:sector], blocks, 2)
    own = kept[:sector].astype(F32) + arrived[:sector].astype(F32) + other_pair.astype(F32)
    own = own.astype(BF16)
    inward = [(i, i ^ 2) for i in range(blocks) if i % bands in (1, 2)]
    outward = [(i ^ 2, i) for i in range(blocks) if i % bands in (1, 2)]
    edge = rounded_sum(
        summed[sector:], lax.ppermute(summed[sector:], "blk", inward)
    )
    first = band == 0
    firsts = [i for i in range(blocks) if i % bands == 0]
    lasts = [i for i in range(blocks) if i % bands == bands - 1]
    last = band == bands - 1
    outer = jnp.logical_or(first, last)
    more = ((0, sector), (0, 0), (0, 0))
    far = jnp.where(
        first,
        jnp.concatenate([edge, own[:2]], axis=0),
        jnp.where(
            last,
            jnp.concatenate([own[sector - 2 :], edge], axis=0),
            jnp.pad(ends(own, False), more),
        ),
    )

    def to_next(value):
        pairs = [(i, (i - 1) % blocks) for i in firsts]
        pairs = pairs + [(i, (i + 1) % blocks) for i in lasts]
        return lax.ppermute(value, "blk", pairs)

    far_halo = lax.ppermute(far, "blk", off_chip)
    passed = jnp.where(first, far_halo[sector:], far_halo[:2])
    near_halo = lax.ppermute(
        jnp.concatenate([ends(own, True), passed], axis=0), "blk", on_chip
    )
    grad_rows = TAPS * TAPS * (hidden + channels)
    unit = blocks * 16
    grad_rows = -(-grad_rows // unit) * unit
    wide = sector + 2
    keep, send, own_reply, other_reply = call(
        grid_kernel,
        [
            jax.ShapeDtypeStruct((grad_rows // 2, hidden), BF16),
            jax.ShapeDtypeStruct((grad_rows // 2, hidden), BF16),
            jax.ShapeDtypeStruct((sector, channels, LANES), BF16),
            jax.ShapeDtypeStruct((sector, channels, LANES), BF16),
        ],
        [
            pltpu.VMEM((sector + 4, channels, 2 * LANES), BF16),
            pltpu.VMEM(((sector + 4) * channels, length), BF16),
            pltpu.VMEM((TAPS * channels, wide * length), BF16),
            pltpu.VMEM((TAPS * hidden, wide * length), BF16),
            pltpu.VMEM((wide * hidden, length), BF16),
            pltpu.VMEM((hidden, wide * length), BF16),
            pltpu.VMEM((sector * channels, length), BF16),
            pltpu.VMEM((grad_rows, hidden), BF16),
            pltpu.VMEM((TAPS * hidden, length), F32),
            pltpu.VMEM((TAPS * hidden, length), F32),
        ],
        [smem()] + [vmem()] * 9,
        row_flops * (sector + 3 * sector // 2),
        20 * sector * length * hidden,
        limit=32,
    )(
        place,
        own,
        edge,
        near_halo,
        far_halo,
        weight,
        weight_t,
        range_hot,
        act_grads,
        out_grad.reshape(sector * length, hidden),
    )

    partner = swapped(own_reply, blocks, 2)
    edge_reply = to_next(other_reply)
    passed = lax.ppermute(edge_reply, "blk", outward)
    edge_reply = jnp.where(outer, edge_reply, passed)
    theirs = swapped(
        jnp.concatenate([own_reply, partner, edge_reply], axis=0), blocks, 1
    )
    value, other_value = total_over_blocks(keep, send, position, blocks)

    replies = (own_reply, partner, edge_reply, theirs)
    scratch = [pltpu.VMEM((seen, channels, LANES), BF16), pltpu.VMEM((turned, LANES), F32)]
    cell_flops = 2 * seen * 3 * rows * LANES * LANES
    context_grad = call(
        functools.partial(context_kernel, rows),
        jax.ShapeDtypeStruct((channels * rows, columns), BF16),
        scratch + [pltpu.VMEM(((channels + 1) * (rows + SLACK), columns), F32)],
        [smem()] * 2 + [vmem()] * 5,
        cell_flops,
        10 * bins * rows * columns,
    )(place, begins, *replies, probs_t)
    logit_grad = call(
        functools.partial(logit_kernel, rows),
        jax.ShapeDtypeStruct((bins * rows, columns), F32),
        scratch + [pltpu.VMEM(((bins + 1) * (rows + SLACK), columns), F32)],
        [smem()] * 2 + [vmem()] * 7,
        cell_flops,
        20 * bins * rows * columns,
    )(place, begins, *replies, probs, context_t, lidar_bins[0])

    second = TAPS * TAPS * hidden
    first_rows = TAPS * TAPS * channels
    second_grad, first_grad = call(
        functools.partial(
            finish_kernel, [order[0] for order in axis_orders(blocks.bit_length() - 1)]
        ),
        [
            jax.ShapeDtypeStruct((second, hidden), F32),
            jax.ShapeDtypeStruct((first_rows, hidden), F32),
        ],
        [pltpu.VMEM((grad_rows, hidden), BF16)],
        [smem(), vmem(), vmem()],
        1,
        6 * grad_rows * hidden,
    )(place, value, other_value)
    return (
        logit_grad.reshape(1, bins, rows, columns),
        context_grad.reshape(1, channels, rows, columns),
        first_grad.reshape(TAPS, TAPS, channels, hidden),
        second_grad.reshape(TAPS, TAPS, hidden, hidden),
    )


def solution(mesh):
    return jax.shard_map(
        shards,
        mesh=mesh,
        in_specs=(
            P(("group", "blk"), None, None, None),
            P(("group", "blk"), None, None, None),
            P(("group", "blk"), None, None),
            P(),
            P(),
            P(),
            P(),
            P(("group", "blk"), None, None),
        ),
        out_specs=(
            P(("group", "blk"), None, None, None),
            P(("group", "blk"), None, None, None),
            P("group", None, None, None),
            P("group", None, None, None),
        ),
        check_vma=False,
    )
```
